32 devices in a mesh: sec: 2 (over x), gx: 4 (over y, core), gy: 4 (over z).
Axes of the slice: x: 2, y: 2, z: 4, core: 2. Of those that a mesh axis runs over, the one named last changes fastest.
Arguments:
- pressure: float32 [50, 128, 512], P(None, ('sec', 'gx'), 'gy'), may hold values from -4 to 4
- pressure_old: float32 [50, 128, 512], P(None, ('sec', 'gx'), 'gy'), may hold values from -4 to 4
- conductivity: float32 [50, 128, 512], P(None, ('sec', 'gx'), 'gy'), may hold values from 0.3 to 3
- vg_alpha: float32 [50, 128, 512], P(None, ('sec', 'gx'), 'gy'), may hold values from 0.5 to 4
- porosity: float32 [50, 128, 512], P(None, ('sec', 'gx'), 'gy'), may hold values from 0.3 to 0.5
- land_mask: int32 [128, 512], P(('sec', 'gx'), 'gy'), may hold values 0 or 1
- nitrate: float32 [10, 8192], P(None, ('sec', 'gx', 'gy')), may hold values from 0.5 to 2
- patch_column: int32 [8192], P(('sec', 'gx', 'gy')), may hold values from 0 to 2047
- crop_type: int32 [8192], P(('sec', 'gx', 'gy')), may hold values from 0 to 7
- patch_weight: float32 [8192], P(('sec', 'gx', 'gy')), may hold values from 0.2 to 2
- rain: float32 [8192], P(('sec', 'gx', 'gy')), may hold values from 0.1 to 1
- root_decay: float32 [8], replicated, may hold values from 0.05 to 0.8
Outputs:
- residual: float32 [50, 128, 512], P(None, ('sec', 'gx'), 'gy')
- nitrate_out: float32 [10, 8192], P(None, ('sec', 'gx', 'gy'))
The draws below stay inside these ranges and needn't reach their ends.
All inputs are finite; a program needn't handle non-finite values. No bound on the sum of `land_mask` on one device may be relied on, other than what follows from the above.
Results may differ from the reference program's by a relative error of at most 0.0003.
The reference program's roundings to bfloat16 on the way (of `sat_top` and `patch_sat`) count: a program that leaves them out, or rounds other values in their place, can miss the bound.
Values may be sent and summed in bfloat16 or wider, within the bound.
No kernel may reach another device: no remote copies, remote signals or barrier semaphores. Data moves between devices by JAX's collectives and lax.ppermute only.
A program may use at most 192 MiB of HBM per device.

```python
import math
import jax
import jax.numpy as jnp
from jax import lax

NZ = 50
NTOP = 10
CX = 16
CY = 128
PB = 16
NCROP = 8
NSUB = 4
NX = 128
NY = 512
NG = 16
PDEV = 256
PATCHES = 8192
N_GX = 4
N_GY = 4


def with_ends(array, stream_key, low, high):
    longest = array.shape.index(max(array.shape))
    spots = []
    for shift in (0, 1):
        where = [jax.random.randint(jax.random.fold_in(stream_key, axis), (), 0, length) for axis, length in enumerate(array.shape)]
        where[longest] = (where[longest] + shift) % array.shape[longest]
        spots.append(tuple(where))
    return array.at[spots[0]].set(low).at[spots[1]].set(high)


def shard_levels(stream_key, extent, pieces, least, high):
    def one(axis_at, parts):
        heights = jax.random.uniform(jax.random.fold_in(jax.random.fold_in(stream_key, 6), axis_at), (parts,), jnp.float32, least / len(pieces), high / len(pieces))
        return jnp.repeat(jnp.exp(heights), extent[axis_at] // parts).reshape((-1,) + (1,) * (len(extent) - axis_at - 1))

    loudness = one(*pieces[0])
    for cut in pieces[1:]:
        loudness = loudness * one(*cut)
    return loudness


def noise(own_key, shape, spread, reach, split=(), kind=jnp.bfloat16):
    entries = spread * jax.random.normal(own_key, shape, jnp.float32)
    if split:
        entries = entries * shard_levels(own_key, shape, split, -0.22, 0.18)
    return jnp.clip(entries, -reach, reach).astype(kind)


def setup_inputs(seed: int = 0) -> dict:
    key_list = jax.random.split(jax.random.key(seed), 13)
    return {
        "pressure": noise(key_list[0], (NZ, NX, NY), 1.0, 4.0, ((1, 8), (2, 4)), jnp.float32),
        "pressure_old": noise(key_list[1], (NZ, NX, NY), 1.0, 4.0, ((1, 8), (2, 4)), jnp.float32),
        "conductivity": jnp.clip(jnp.exp(math.log(3.0) - 2.3025851 * jax.random.uniform(key_list[2], (NZ, NX, NY), jnp.float32) ** shard_levels(key_list[2], (NZ, NX, NY), ((1, 8), (2, 4)), -0.2, 0.2)), 0.3, 3.0),
        "vg_alpha": jnp.clip(jnp.exp(math.log(4.0) - 2.0794415 * jax.random.uniform(key_list[3], (NZ, NX, NY), jnp.float32) ** shard_levels(key_list[3], (NZ, NX, NY), ((1, 8), (2, 4)), -0.2, 0.2)), 0.5, 4.0),
        "porosity": jnp.clip(0.3 + 0.19999999 * jax.random.uniform(key_list[4], (NZ, NX, NY), jnp.float32) ** shard_levels(key_list[4], (NZ, NX, NY), ((1, 8), (2, 4)), -0.2, 0.2), 0.3, 0.5),
        "land_mask": with_ends((jax.random.randint(key_list[5], (NX, NY), 0, 4) < 3).astype(jnp.int32), jax.random.fold_in(key_list[5], 1), 0, 1),
        "nitrate": jnp.clip(0.5 + 1.5 * jax.random.uniform(key_list[6], (NTOP, PATCHES), jnp.float32) ** shard_levels(key_list[6], (NTOP, PATCHES), ((1, 32),), -0.2, 0.2), 0.5, 2.0),
        "patch_column": with_ends(jax.random.randint(key_list[7], (PATCHES,), 0, CX * CY), jax.random.fold_in(key_list[7], 1), 0, (CX * CY) - 1).astype(jnp.int32),
        "crop_type": with_ends(jax.random.randint(key_list[8], (PATCHES,), 0, NCROP), jax.random.fold_in(key_list[8], 1), 0, NCROP - 1).astype(jnp.int32),
        "patch_weight": jnp.clip(jnp.exp(math.log(2.0) - 2.3025851 * jax.random.uniform(key_list[9], (PATCHES,), jnp.float32) ** shard_levels(key_list[9], (PATCHES,), ((0, 32),), -0.2, 0.2)), 0.2, 2.0),
        "rain": jnp.clip(jnp.exp(math.log(1.0) - 2.3025851 * jax.random.uniform(key_list[10], (PATCHES,), jnp.float32) ** shard_levels(key_list[10], (PATCHES,), ((0, 32),), -0.2, 0.2)), 0.1, 1.0),
        "root_decay": jnp.clip(jnp.exp(jax.random.uniform(key_list[11], (NCROP,), jnp.float32, math.log(0.05), math.log(0.8))), 0.05, 0.8),
    }


def saturation(head, alpha_field):
    suction = jax.nn.softplus(-head)
    scaled = alpha_field * suction
    return 1.0 / jnp.sqrt(1.0 + scaled * scaled)

def outflow(pressure, conduct, head_pad, cond_pad):
    head_x = head_pad[:, :, 1:-1]
    cond_x = cond_pad[:, :, 1:-1]
    flux_x = 0.5 * (cond_x[:, :-1] + cond_x[:, 1:]) * (head_x[:, :-1] - head_x[:, 1:])
    head_y = head_pad[:, 1:-1, :]
    cond_y = cond_pad[:, 1:-1, :]
    flux_y = 0.5 * (cond_y[:, :, :-1] + cond_y[:, :, 1:]) * (head_y[:, :, :-1] - head_y[:, :, 1:])
    flux_z = 0.5 * (conduct[:-1] + conduct[1:]) * (pressure[:-1] - pressure[1:] + 1.0)
    zero_top = jnp.zeros_like(conduct[:1])
    flux_z = jnp.concatenate([zero_top, flux_z, conduct[-1:]], 0)
    return flux_x[:, 1:] - flux_x[:, :-1] + (flux_y[:, :, 1:] - flux_y[:, :, :-1]) + (flux_z[1:] - flux_z[:-1])

def reference(pressure, pressure_old, conductivity, vg_alpha, porosity, land_mask, nitrate, patch_column, crop_type, patch_weight, rain, root_decay):
    wet = saturation(pressure, vg_alpha)
    wet_old = saturation(pressure_old, vg_alpha)
    conduct = conductivity * wet * wet * wet
    sat_top = wet[:NTOP].astype(jnp.bfloat16)
    index = jnp.arange(PATCHES, dtype=jnp.int32)
    device = index // PDEV
    section = device // NG
    block = index % PDEV // PB
    col_x = (section * N_GX + block // N_GY) * CX + patch_column // CY
    col_y = block % N_GY * CY + patch_column % CY
    patch_sat = sat_top[:, col_x, col_y]
    sat_p = patch_sat.astype(jnp.float32)
    decay = root_decay[crop_type]
    levels = jnp.arange(NTOP, dtype=jnp.float32) + 0.5
    profile = jnp.exp(-levels[:, None] * decay[None, :])
    profile = profile / lax.optimization_barrier(jnp.sum(profile, axis=0, keepdims=True))
    extraction = patch_weight[None, :] * profile * sat_p
    inflow = rain * (1.0 - sat_p[0])
    sources = jnp.concatenate([(inflow - extraction[0])[None], -extraction[1:]], 0)
    nitrogen = nitrate
    for step in range(NSUB):
        upper = jnp.concatenate([nitrogen[:1], nitrogen[:-1]], 0)
        lower = jnp.concatenate([nitrogen[1:], nitrogen[-1:]], 0)
        nitrogen = nitrogen + 0.2 * (upper + lower - 2.0 * nitrogen) - 0.3 * sat_p * sat_p * nitrogen
    segment = col_x * NY + col_y
    summed = jax.ops.segment_sum(sources.T, segment, num_segments=NX * NY)
    column_source = summed.T.reshape(NTOP, NX, NY) * land_mask.astype(jnp.float32)[None]
    head_pad = jnp.pad(pressure, ((0, 0), (1, 1), (1, 1)))
    cond_pad = jnp.pad(conduct, ((0, 0), (1, 1), (1, 1)))
    residual = porosity * (wet - wet_old) + outflow(pressure, conduct, head_pad, cond_pad)
    residual = jnp.concatenate([residual[:NTOP] - column_source, residual[NTOP:]], 0)
    return (residual, nitrogen)
```

```python
import jax
import jax.numpy as jnp
from jax import lax
from jax.sharding import PartitionSpec as P

NSUB = 4


def swap_pairs(size, first):
    pairs = []
    for i in range(first, size - 1, 2):
        pairs += [(i, i + 1), (i + 1, i)]
    return pairs


def neighbours(value, axis, dim):
    size, length = (lax.axis_size(axis), value.shape[dim])
    even = lax.axis_index(axis) % 2 == 0
    leading = lax.slice_in_dim(value, 0, 1, axis=dim)
    last = lax.slice_in_dim(value, length - 1, length, axis=dim)
    first_swap = lax.ppermute(jnp.where(even, last, leading), axis, swap_pairs(size, 0))
    second_swap = lax.ppermute(jnp.where(even, leading, last), axis, swap_pairs(size, 1))
    before = jnp.where(even, second_swap, first_swap)
    after = jnp.where(even, first_swap, second_swap)
    return before, after


def saturation(head, alpha_field):
    suction = jax.nn.softplus(-head)
    scaled = alpha_field * suction
    return 1.0 / jnp.sqrt(1.0 + scaled * scaled)


def outflow(pressure, conduct, sides_x, sides_y):
    def flux(head, cond, before, after, dim):
        head = jnp.concatenate([before[0], head, after[0]], dim)
        cond = jnp.concatenate([before[1], cond, after[1]], dim)
        size = head.shape[dim]
        low = lambda v: lax.slice_in_dim(v, 0, size - 1, axis=dim)
        high = lambda v: lax.slice_in_dim(v, 1, size, axis=dim)
        face = 0.5 * (low(cond) + high(cond)) * (low(head) - high(head))
        return lax.slice_in_dim(face, 1, size - 1, axis=dim) - lax.slice_in_dim(face, 0, size - 2, axis=dim)

    flux_z = 0.5 * (conduct[:-1] + conduct[1:]) * (pressure[:-1] - pressure[1:] + 1.0)
    flux_z = jnp.concatenate([jnp.zeros_like(conduct[:1]), flux_z, conduct[-1:]], 0)
    return (
        flux(pressure, conduct, *sides_x, 1)
        + flux(pressure, conduct, *sides_y, 2)
        + (flux_z[1:] - flux_z[:-1])
    )


def deposit(values, row_hot, lane_hot):
    spread = values[:, None, :] * row_hot[None]
    top, width_x, slots = spread.shape
    total = lax.dot_general(
        spread.reshape(top * width_x, slots),
        lane_hot,
        (((1,), (1,)), ((), ())),
        precision=lax.Precision.HIGHEST,
        preferred_element_type=jnp.float32,
    )
    return total.reshape(top, width_x, lane_hot.shape[0])


def patch_sources(sat_p, kinds_of, root_decay, weights, rainfall, top):
    kinds = jnp.arange(root_decay.shape[0], dtype=jnp.int32)
    decay = jnp.sum(
        jnp.where(kinds_of[None, :] == kinds[:, None], root_decay[:, None], 0.0), axis=0
    )
    levels = jnp.arange(top, dtype=jnp.float32) + 0.5
    profile = jnp.exp(-levels[:, None] * decay[None, :])
    profile = profile / jnp.sum(profile, axis=0, keepdims=True)
    extraction = weights[None, :] * profile * sat_p
    inflow = rainfall * (1.0 - sat_p[0])
    return jnp.concatenate([(inflow - extraction[0])[None], -extraction[1:]], 0)


def per_device(
    pressure,
    pressure_old,
    conductivity,
    vg_alpha,
    porosity,
    land_mask,
    nitrate,
    patch_column,
    crop_type,
    patch_weight,
    rain,
    root_decay,
):
    layers, width_x, width_y = pressure.shape
    top = nitrate.shape[0]
    slots = patch_column.shape[0]
    owners = lax.axis_size(("gx", "gy"))
    per_block = slots // owners
    wet = saturation(pressure, vg_alpha)
    wet_old = saturation(pressure_old, vg_alpha)
    conduct = conductivity * wet * wet * wet
    sat_top = wet[:top].astype(jnp.bfloat16)
    group = ("gx", "gy")
    sent = jnp.stack([patch_column.astype(jnp.float32), crop_type.astype(jnp.float32), patch_weight, rain])
    sent = sent.reshape(4, owners, per_block).transpose(1, 0, 2).reshape(owners, 4 * per_block)
    got = lax.all_to_all(sent, group, split_axis=0, concat_axis=0, tiled=True)
    got = got.reshape(owners, 4, per_block).transpose(1, 0, 2).reshape(4, slots)
    ids = got[0].astype(jnp.int32)
    row_hot = (ids // width_y)[None, :] == jnp.arange(width_x, dtype=jnp.int32)[:, None]
    lane_hot = (ids % width_y)[None, :] == jnp.arange(width_y, dtype=jnp.int32)[:, None]
    picked = jnp.dot(
        sat_top.reshape(top * width_x, width_y),
        lane_hot.astype(jnp.bfloat16),
        preferred_element_type=jnp.float32,
    ).reshape(top, width_x, slots)
    patch_sat = jnp.sum(jnp.where(row_hot[None], picked, 0.0), 1)
    back = patch_sat.astype(jnp.bfloat16).reshape(top, owners, per_block).transpose(1, 0, 2).reshape(owners, top * per_block)
    back = lax.all_to_all(back, group, split_axis=0, concat_axis=0, tiled=True)
    sat_p = back.reshape(owners, top, per_block).transpose(1, 0, 2).reshape(top, slots).astype(jnp.float32)
    sources = patch_sources(patch_sat, got[1].astype(jnp.int32), root_decay, got[2], got[3], top)
    nitrogen = nitrate
    for step in range(NSUB):
        upper = jnp.concatenate([nitrogen[:1], nitrogen[:-1]], 0)
        lower = jnp.concatenate([nitrogen[1:], nitrogen[-1:]], 0)
        nitrogen = (
            nitrogen + 0.2 * (upper + lower - 2.0 * nitrogen) - 0.3 * sat_p * sat_p * nitrogen
        )
    stacked = jnp.stack([pressure, conduct])
    sides_x = neighbours(stacked, ("sec", "gx"), 2)
    sides_y = neighbours(stacked, "gy", 3)
    residual = porosity * (wet - wet_old) + outflow(pressure, conduct, sides_x, sides_y)
    column_source = deposit(sources, row_hot.astype(jnp.float32), lane_hot.astype(jnp.float32))
    column_source = column_source * land_mask.astype(jnp.float32)[None]
    residual = jnp.concatenate([residual[:top] - column_source, residual[top:]], 0)
    return (residual, nitrogen)


def solution(mesh):
    placed = (
        P(None, ("sec", "gx"), "gy"),
        P(None, ("sec", "gx"), "gy"),
        P(None, ("sec", "gx"), "gy"),
        P(None, ("sec", "gx"), "gy"),
        P(None, ("sec", "gx"), "gy"),
        P(("sec", "gx"), "gy"),
        P(None, ("sec", "gx", "gy")),
        P(("sec", "gx", "gy")),
        P(("sec", "gx", "gy")),
        P(("sec", "gx", "gy")),
        P(("sec", "gx", "gy")),
        P(),
    )
    return jax.shard_map(
        per_device,
        mesh=mesh,
        in_specs=placed,
        out_specs=(P(None, ("sec", "gx"), "gy"), P(None, ("sec", "gx", "gy"))),
        check_vma=False,
    )
```

```python
import functools

import jax
import jax.numpy as jnp
from jax import lax
from jax.experimental import pallas as pl
from jax.experimental.pallas import tpu as pltpu
from jax.sharding import PartitionSpec as P

NSUB = 4
LANES = 128
CHUNK = 10
VMEM_LIMIT = 48 * 1024 * 1024


def call(body, outs, name, smem=(), count=0, flops=100000, exps=0):
    specs = [
        pl.BlockSpec(memory_space=pltpu.SMEM if i in smem else pltpu.VMEM) for i in range(count)
    ]
    return pl.pallas_call(
        body,
        out_shape=outs,
        in_specs=specs,
        name=name,
        compiler_params=pltpu.CompilerParams(vmem_limit_bytes=VMEM_LIMIT),
        cost_estimate=pl.CostEstimate(flops=flops, bytes_accessed=1000000, transcendentals=exps),
    )


def iota(shape, dim):
    return lax.broadcasted_iota(jnp.int32, shape, dim)


def saturation(head, alpha_field):
    suction = jnp.maximum(-head, 0.0) + jnp.log1p(jnp.exp(-jnp.abs(head)))
    scaled = alpha_field * suction
    return lax.rsqrt(1.0 + scaled * scaled)


def join_blocks(rows, per_block, slot):
    height = LANES // per_block
    if slot:
        rows = pltpu.roll(rows, LANES - slot * per_block, 1)
    moved = pltpu.roll(rows, 0, 1, stride=per_block, stride_axis=0)
    own = iota((height, LANES), 1) // per_block == iota((height, LANES), 0)
    return jnp.sum(jnp.where(own, moved, 0.0), axis=0, keepdims=True)


def pack_kernel(per_block, column, crop, weight, rain, out):
    height = LANES // per_block
    for h in range(column.shape[0]):
        rows = [ref[h : h + 1, :].astype(jnp.float32) for ref in (column, crop, weight, rain)]
        rows.append(jnp.zeros((height - len(rows), LANES), jnp.float32))
        rows = jnp.concatenate(rows, axis=0)
        for j in range(height):
            out[h * height + j : h * height + j + 1, :] = join_blocks(rows, per_block, j)


def even_place(axes):
    index = 0
    for axis in axes:
        index = index * lax.axis_size(axis) + lax.axis_index(axis)
    return index % 2 == 0


def wet_kernel(top, axes_x, axes_y, pressure, alpha, conductivity, sat, conduct, wet_out, *sends):
    x_first, x_second, y_first, y_second = sends
    layers, width_x, width_y = pressure.shape
    for start in range(0, layers, CHUNK):
        part = slice(start, min(layers, start + CHUNK))
        wet = saturation(pressure[part], alpha[part])
        conduct[part] = conductivity[part] * wet * wet * wet
        wet_out[part] = wet
        if part.start < top:
            stop = min(part.stop, top)
            kept = wet[: stop - part.start].reshape((stop - part.start) * width_x, width_y)
            sat[part.start * width_x : stop * width_x, :] = kept.astype(jnp.bfloat16)
    even = even_place(axes_x)
    for field, ref in enumerate((pressure, conduct)):
        rows = slice(field * layers, (field + 1) * layers)
        low, high = ref[:, 0, :], ref[:, width_x - 1, :]
        x_first[rows, :] = jnp.where(even, high, low)
        x_second[rows, :] = jnp.where(even, low, high)
    even = even_place(axes_y)
    lane = iota((width_x, width_y), 1)
    low = jnp.zeros((width_x, width_y), jnp.float32)
    high = jnp.zeros((width_x, width_y), jnp.float32)
    for field, ref in enumerate((pressure, conduct)):
        for k in range(layers):
            place = field * layers + k
            value = ref[k]
            low = jnp.where(lane == place, pltpu.roll(value, place, 1), low)
            high = jnp.where(lane == place, pltpu.roll(value, (place + 1) % width_y, 1), high)
    y_first[...] = jnp.where(even, high, low)
    y_second[...] = jnp.where(even, low, high)


def hot(ids, size):
    return iota((size, LANES), 0) == ids


def pick_kernel(per_block, top, width_x, got, sat, back, patch_sat):
    height = LANES // per_block
    width_y = sat.shape[1]
    for h in range(got.shape[0] // height):
        rows = slice(h * height, (h + 1) * height)
        ids = join_blocks(got[rows, :], per_block, 0).astype(jnp.int32)
        lane_hot = hot(lax.rem(ids, width_y), width_y).astype(jnp.float32).astype(jnp.bfloat16)
        row_hot = hot(lax.div(ids, width_y), width_x)
        picked = jnp.dot(sat[...], lane_hot, preferred_element_type=jnp.float32)
        patch_sat[h] = jnp.zeros(patch_sat.shape[1:], jnp.float32)
        for k in range(top):
            one = picked[k * width_x : (k + 1) * width_x]
            patch_sat[h, k : k + 1, :] = jnp.sum(
                jnp.where(row_hot, one, 0.0), axis=0, keepdims=True
            )
        for i in range(back.shape[1] // LANES):
            block = patch_sat[h, i * height : (i + 1) * height, :]
            for j in range(height):
                row = slice(h * height + j, h * height + j + 1)
                back[row, i * LANES : (i + 1) * LANES] = join_blocks(block, per_block, j)


def column_sources(per_block, top, width_x, width_y, got, patch_sat, root_decay):
    height = LANES // per_block
    total = jnp.zeros((top * width_x, width_y), jnp.float32)
    for h in range(got.shape[0] // height):
        rows = got[h * height : (h + 1) * height, :]
        ids, crop, weight, rain = (join_blocks(rows, per_block, slot) for slot in range(4))
        ids = ids.astype(jnp.int32)
        crop = crop.astype(jnp.int32)
        decay = jnp.zeros((1, LANES), jnp.float32)
        for kind in range(root_decay.shape[0]):
            decay = jnp.where(crop == kind, root_decay[kind], decay)
        level = iota((top, LANES), 0)
        profile = jnp.exp(-(level.astype(jnp.float32) + 0.5) * decay)
        profile = profile / jnp.sum(profile, axis=0, keepdims=True)
        sat = patch_sat[h][:top]
        inflow = jnp.where(level == 0, rain * (1.0 - sat), 0.0)
        sources = inflow - weight * profile * sat
        lane_hot = hot(lax.rem(ids, width_y), width_y).astype(jnp.float32)
        row_hot = hot(lax.div(ids, width_y), width_x)
        spread = jnp.concatenate(
            [jnp.where(row_hot, sources[k : k + 1], 0.0) for k in range(top)], axis=0
        )
        total = total + lax.dot_general(
            spread,
            lane_hot,
            (((1,), (1,)), ((), ())),
            precision=lax.Precision.HIGHEST,
            preferred_element_type=jnp.float32,
        )
    return total


def balance_kernel(per_block, top, axes_x, axes_y, *refs):
    pressure, pressure_old, alpha, porosity, conduct, wet = refs[:6]
    got, patch_sat, root_decay, land = refs[6:10]
    x_sent, x_got, y_sent, y_got = refs[10:12], refs[12:14], refs[14:16], refs[16:18]
    out, x_faces = refs[18:]
    layers, width_x, width_y = pressure.shape
    sources = column_sources(per_block, top, width_x, width_y, got, patch_sat, root_decay)
    sources = sources.reshape(top, width_x, width_y) * land[...].astype(jnp.float32)[None]

    def sides(even, sent, got):
        low, high = jnp.where(even, sent[1], sent[0]), jnp.where(even, sent[0], sent[1])
        before, after = jnp.where(even, got[1], got[0]), jnp.where(even, got[0], got[1])
        return low, high, before, after

    even = even_place(axes_x)
    heads = sides(even, [r[:layers, :] for r in x_sent], [r[:layers, :] for r in x_got])
    conds = sides(even, [r[layers:, :] for r in x_sent], [r[layers:, :] for r in x_got])
    x_faces[0] = 0.5 * (conds[2] + conds[0]) * (heads[2] - heads[0])
    x_faces[1] = 0.5 * (conds[1] + conds[3]) * (heads[1] - heads[3])
    even = even_place(axes_y)
    heads = sides(even, [r[...] for r in y_sent], [r[...] for r in y_got])
    conds = [pltpu.roll(v, width_y - layers, 1) for v in heads]
    y_before = 0.5 * (conds[2] + conds[0]) * (heads[2] - heads[0])
    y_after = 0.5 * (conds[1] + conds[3]) * (heads[1] - heads[3])

    for start in range(0, layers, CHUNK):
        stop = min(layers, start + CHUNK)
        shape = (stop - start, width_x, width_y)
        head, cond = pressure[start:stop], conduct[start:stop]
        row, lane = iota(shape, 1), iota(shape, 2)
        wet_old = saturation(pressure_old[start:stop], alpha[start:stop])
        total = porosity[start:stop] * (wet[start:stop] - wet_old)
        for axis, place, size in ((1, row, width_x), (2, lane, width_y)):
            face = (
                0.5
                * (cond + pltpu.roll(cond, size - 1, axis))
                * (head - pltpu.roll(head, size - 1, axis))
            )
            face = jnp.where(place == size - 1, 0.0, face)
            total = total + (face - pltpu.roll(face, 1, axis))
        below = min(layers, stop + 1)
        head, cond = pressure[max(0, start - 1) : below], conduct[max(0, start - 1) : below]
        down = 0.5 * (cond[:-1] + cond[1:]) * (head[:-1] - head[1:] + 1.0)
        if start == 0:
            down = jnp.concatenate([jnp.zeros_like(cond[:1]), down], 0)
        if stop == layers:
            down = jnp.concatenate([down, cond[-1:]], 0)
        total = total + (down[1:] - down[:-1])
        row, lane = row[0], lane[0]
        for k in range(start, stop):
            edge = jnp.where(row == 0, -x_faces[0, k : k + 1, :], 0.0)
            edge = edge + jnp.where(row == width_x - 1, x_faces[1, k : k + 1, :], 0.0)
            low = pltpu.roll(y_before, (width_y - k) % width_y, 1)
            high = pltpu.roll(y_after, (width_y - 1 - k) % width_y, 1)
            edge = edge - jnp.where(lane == 0, low, 0.0) + jnp.where(lane == width_y - 1, high, 0.0)
            one = total[k - start] + edge
            out[k] = one - sources[k] if k < top else one


def nitrate_kernel(per_block, back, nitrate, out, sat):
    height = LANES // per_block
    top = nitrate.shape[0]
    for h in range(back.shape[0] // height):
        rows = slice(h * height, (h + 1) * height)
        lanes = slice(h * LANES, (h + 1) * LANES)
        for k in range(top):
            where, slot = divmod(k, height)
            block = back[rows, where * LANES : (where + 1) * LANES]
            sat[k : k + 1, :] = join_blocks(block, per_block, slot)
        loss = 0.3 * sat[...] * sat[...]
        value = nitrate[:, lanes]
        for _ in range(NSUB):
            upper = jnp.concatenate([value[:1], value[:-1]], 0)
            lower = jnp.concatenate([value[1:], value[-1:]], 0)
            value = value + 0.2 * (upper + lower - 2.0 * value) - loss * value
        out[:, lanes] = value


def swap_pairs(size, first):
    pairs = []
    for i in range(first, size - 1, 2):
        pairs += [(i, i + 1), (i + 1, i)]
    return pairs


def per_device(
    pressure,
    pressure_old,
    conductivity,
    vg_alpha,
    porosity,
    land_mask,
    nitrate,
    patch_column,
    crop_type,
    patch_weight,
    rain,
    root_decay,
):
    layers, width_x, width_y = pressure.shape
    top, slots = nitrate.shape
    group, axes_x, axes_y = ("gx", "gy"), ("sec", "gx"), ("gy",)
    owners = lax.axis_size(group)
    per_block = slots // owners
    if LANES % per_block or slots % LANES or 4 * per_block >= LANES:
        raise ValueError("block size")
    if width_y != LANES or width_x % 8 or 2 * layers > LANES:
        raise ValueError("grid size")
    height = LANES // per_block
    f32 = jnp.float32
    shape = jax.ShapeDtypeStruct
    field = shape((layers, width_x, width_y), f32)

    flat = [v.reshape(slots // LANES, LANES) for v in (patch_column, crop_type, patch_weight, rain)]
    sent = call(
        functools.partial(pack_kernel, per_block), shape((owners, LANES), f32), "pack", count=4
    )(*flat)
    got = lax.all_to_all(sent, group, split_axis=0, concat_axis=0, tiled=True)

    x_edge, y_edge = shape((2 * layers, width_y), f32), shape((width_x, width_y), f32)
    sat, conduct, wet, *edges = call(
        functools.partial(wet_kernel, top, axes_x, axes_y),
        (shape((top * width_x, width_y), jnp.bfloat16), field, field, x_edge, x_edge, y_edge, y_edge),
        "wet",
        count=3,
        exps=500000,
    )(pressure, vg_alpha, conductivity)

    x_size, y_size = lax.axis_size(axes_x), lax.axis_size(axes_y)
    x_got = [lax.ppermute(edges[i], axes_x, swap_pairs(x_size, i)) for i in (0, 1)]
    y_got = [lax.ppermute(edges[2 + i], axes_y, swap_pairs(y_size, i)) for i in (0, 1)]

    wide = -(-top // height) * LANES
    back, patch_sat = call(
        functools.partial(pick_kernel, per_block, top, width_x),
        (shape((owners, wide), f32), shape((slots // LANES, wide * height // LANES, LANES), f32)),
        "pick",
        count=2,
    )(got, sat)
    back = lax.all_to_all(back, group, split_axis=0, concat_axis=0, tiled=True)

    operands = [pressure, pressure_old, vg_alpha, porosity, conduct, wet, got, patch_sat]
    operands += [root_decay, land_mask, *edges[:2], *x_got, *edges[2:], *y_got]
    residual = pl.pallas_call(
        functools.partial(balance_kernel, per_block, top, axes_x, axes_y),
        out_shape=field,
        in_specs=[
            pl.BlockSpec(memory_space=pltpu.SMEM if i == 8 else pltpu.VMEM)
            for i in range(len(operands))
        ],
        scratch_shapes=[pltpu.VMEM((2, layers, width_y), f32)],
        name="balance",
        compiler_params=pltpu.CompilerParams(vmem_limit_bytes=VMEM_LIMIT),
        cost_estimate=pl.CostEstimate(flops=5000000, bytes_accessed=3000000, transcendentals=200000),
    )(*operands)
    nitrate_out = pl.pallas_call(
        functools.partial(nitrate_kernel, per_block),
        out_shape=shape((top, slots), f32),
        in_specs=[pl.BlockSpec(memory_space=pltpu.VMEM)] * 2,
        scratch_shapes=[pltpu.VMEM((top, LANES), f32)],
        name="nitrate",
        compiler_params=pltpu.CompilerParams(vmem_limit_bytes=VMEM_LIMIT),
    )(back, nitrate)
    return (residual, nitrate_out)


def solution(mesh):
    placed = (
        P(None, ("sec", "gx"), "gy"),
        P(None, ("sec", "gx"), "gy"),
        P(None, ("sec", "gx"), "gy"),
        P(None, ("sec", "gx"), "gy"),
        P(None, ("sec", "gx"), "gy"),
        P(("sec", "gx"), "gy"),
        P(None, ("sec", "gx", "gy")),
        P(("sec", "gx", "gy")),
        P(("sec", "gx", "gy")),
        P(("sec", "gx", "gy")),
        P(("sec", "gx", "gy")),
        P(),
    )
    return jax.shard_map(
        per_device,
        mesh=mesh,
        in_specs=placed,
        out_specs=(P(None, ("sec", "gx"), "gy"), P(None, ("sec", "gx", "gy"))),
        check_vma=False,
    )
```

```python
import functools

import jax
import jax.numpy as jnp
from jax import lax
from jax.experimental import pallas as pl
from jax.experimental.pallas import tpu as pltpu
from jax.sharding import PartitionSpec as P

NSUB = 4
LANES = 128
CHUNK = 10
FIELD_LANE = 104
VMEM_LIMIT = 24 * 1024 * 1024


def iota(shape, dim):
    return lax.broadcasted_iota(jnp.int32, shape, dim)


def place_of(axes):
    index = 0
    for axis in axes:
        index = index * lax.axis_size(axis) + lax.axis_index(axis)
    return index


def parts_of(layers):
    return [(i, min(layers, i + CHUNK)) for i in range(0, layers, CHUNK)]


def saturation(head, alpha_field):
    suction = jnp.maximum(-head, 0.0) + jnp.log1p(jnp.exp(-jnp.abs(head)))
    scaled = alpha_field * suction
    return lax.rsqrt(1.0 + scaled * scaled)


def join_blocks(rows, per_block, slot):
    height = LANES // per_block
    if slot:
        rows = pltpu.roll(rows, LANES - slot * per_block, 1)
    moved = pltpu.roll(rows, 0, 1, stride=per_block, stride_axis=0)
    own = iota((height, LANES), 1) // per_block == iota((height, LANES), 0)
    return jnp.sum(jnp.where(own, moved, 0.0), axis=0, keepdims=True)


def front_kernel(per_block, top, axes_x, axes_y, *refs):
    fields, grids = refs[:4], refs[4:7]
    sent, sat, head, alpha, conduct, wet_out, x_first, x_second, y_edges = refs[7:16]
    fields_in, perm, sent_in, small_sems, sems, sent_sem = refs[16:]
    layers, width_x, width_y = head.shape
    height = LANES // per_block
    small = [pltpu.make_async_copy(fields[i], fields_in[i], small_sems.at[i]) for i in range(4)]
    for copy in small:
        copy.start()
    parts = parts_of(layers)
    large = []
    for i, (start, stop) in enumerate(parts):
        rows = pl.ds(start, stop - start)
        for j, (source, target) in enumerate(zip(grids, (head, alpha, perm))):
            copy = pltpu.make_async_copy(source.at[rows], target.at[rows], sems.at[i, j])
            copy.start()
            large.append(copy)
    for copy in small:
        copy.wait()
    for h in range(sent_in.shape[0] // height):
        rows = [ref[h : h + 1, :].astype(jnp.float32) for ref in fields_in]
        rows.append(jnp.zeros((4, LANES), jnp.float32))
        rows = [jnp.zeros((FIELD_LANE, LANES), jnp.float32), jnp.concatenate(rows, axis=0)]
        rows.append(jnp.zeros((LANES - FIELD_LANE - 8, LANES), jnp.float32))
        turned = jnp.concatenate(rows, axis=0).T
        sent_in[h * height : (h + 1) * height] = turned.reshape(height, per_block, LANES)
    lane = iota((width_x, width_y), 1)
    low = jnp.zeros((width_x, width_y), jnp.float32)
    high = jnp.zeros((width_x, width_y), jnp.float32)
    for i, (start, stop) in enumerate(parts):
        for copy in large[3 * i : 3 * i + 3]:
            copy.wait()
        part = slice(start, stop)
        wet = saturation(head[part], alpha[part])
        cond = perm[part] * wet * wet * wet
        conduct[part] = cond
        wet_out[part] = wet
        if start < top:
            last = min(stop, top)
            kept = wet[: last - start].reshape((last - start) * width_x, width_y)
            sat[start * width_x : last * width_x, :] = kept.astype(jnp.bfloat16)
        for first, values in ((0, head[part]), (layers, cond)):
            for k in range(start, stop):
                place = first + k
                value = values[k - start]
                low = jnp.where(lane == place, pltpu.roll(value, place, 1), low)
                high = jnp.where(lane == place, pltpu.roll(value, (place + 1) % width_y, 1), high)
    y_edges[0] = low
    y_edges[1] = high
    y_place, y_size = place_of(axes_y), lax.axis_size(axes_y)
    base = place_of(("gx", "gy"))

    @pl.when(y_place > 0)
    def _():
        sent_in[base - 1] = sent_in[base - 1] + low

    @pl.when(y_place < y_size - 1)
    def _():
        sent_in[base + 1] = sent_in[base + 1] + high

    send = pltpu.make_async_copy(sent_in, sent, sent_sem)
    send.start()
    even = place_of(axes_x) % 2 == 0
    for field, ref in enumerate((head, conduct)):
        rows = slice(field * layers, (field + 1) * layers)
        low, high = ref[:, 0, :], ref[:, width_x - 1, :]
        x_first[rows, :] = jnp.where(even, high, low)
        x_second[rows, :] = jnp.where(even, low, high)
    send.wait()


def hot(ids, size):
    return iota((size, LANES), 0) == ids


def pick_kernel(per_block, top, width_x, got, sat, back, patch_sat, fields):
    height = LANES // per_block
    width_y = sat.shape[1]
    for h in range(got.shape[0] // height):
        turned = got[h * height : (h + 1) * height].reshape(LANES, LANES).T
        rows = turned[FIELD_LANE : FIELD_LANE + 8]
        fields[h] = rows
        ids = rows[0:1].astype(jnp.int32)
        lane_hot = hot(lax.rem(ids, width_y), width_y).astype(jnp.float32).astype(jnp.bfloat16)
        row_hot = hot(lax.div(ids, width_y), width_x)
        picked = jnp.dot(sat[...], lane_hot, preferred_element_type=jnp.float32)
        patch_sat[h] = jnp.zeros(patch_sat.shape[1:], jnp.float32)
        for k in range(top):
            one = picked[k * width_x : (k + 1) * width_x]
            patch_sat[h, k : k + 1, :] = jnp.sum(
                jnp.where(row_hot, one, 0.0), axis=0, keepdims=True
            )
        for i in range(back.shape[1]):
            block = patch_sat[h, i * height : (i + 1) * height, :]
            for j in range(height):
                row = slice(h * height + j, h * height + j + 1)
                back[row, i, :] = join_blocks(block, per_block, j)


def column_sources(top, width_x, width_y, fields, patch_sat, root_decay):
    total = jnp.zeros((top * width_x, width_y), jnp.float32)
    for h in range(fields.shape[0]):
        ids, crop, weight, rain = (fields[h, i : i + 1, :] for i in range(4))
        ids = ids.astype(jnp.int32)
        crop = crop.astype(jnp.int32)
        decay = jnp.zeros((1, LANES), jnp.float32)
        for kind in range(root_decay.shape[0]):
            decay = jnp.where(crop == kind, root_decay[kind], decay)
        level = iota((top, LANES), 0)
        profile = jnp.exp(-(level.astype(jnp.float32) + 0.5) * decay)
        profile = profile / jnp.sum(profile, axis=0, keepdims=True)
        sat = patch_sat[h][:top]
        inflow = jnp.where(level == 0, rain * (1.0 - sat), 0.0)
        sources = inflow - weight * profile * sat
        lane_hot = hot(lax.rem(ids, width_y), width_y).astype(jnp.float32)
        row_hot = hot(lax.div(ids, width_y), width_x)
        spread = jnp.concatenate(
            [jnp.where(row_hot, sources[k : k + 1], 0.0) for k in range(top)], axis=0
        )
        total = total + lax.dot_general(
            spread,
            lane_hot,
            (((1,), (1,)), ((), ())),
            precision=lax.Precision.HIGHEST,
            preferred_element_type=jnp.float32,
        )
    return total


def balance_kernel(top, axes_x, axes_y, *refs):
    grids = refs[:2]
    head, alpha, conduct, wet, got, fields, patch_sat, root_decay, land = refs[2:11]
    x_sent, x_got, y_edges = refs[11:13], refs[13:15], refs[15]
    residual, order = refs[16:18]
    head_old, porosity, out, x_faces, sems, out_sems = refs[18:]
    layers, width_x, width_y = head.shape
    parts = parts_of(layers)
    copies = []
    for i, (start, stop) in enumerate(parts):
        rows = pl.ds(start, stop - start)
        for j, (source, target) in enumerate(zip(grids, (head_old, porosity))):
            copy = pltpu.make_async_copy(source.at[rows], target.at[rows], sems.at[i, j])
            copy.start()
            copies.append(copy)
    order[...] = jnp.zeros(order.shape, order.dtype)
    sources = column_sources(top, width_x, width_y, fields, patch_sat, root_decay)
    sources = sources.reshape(top, width_x, width_y) * land[...].astype(jnp.float32)[None]

    even = place_of(axes_x) % 2 == 0
    faces = []
    for rows in (slice(0, layers), slice(layers, 2 * layers)):
        first, second = (r[rows, :] for r in x_sent)
        low, high = jnp.where(even, second, first), jnp.where(even, first, second)
        first, second = (r[rows, :] for r in x_got)
        before, after = jnp.where(even, second, first), jnp.where(even, first, second)
        faces.append((low, high, before, after))
    heads, conds = faces
    x_faces[0] = 0.5 * (conds[2] + conds[0]) * (heads[2] - heads[0])
    x_faces[1] = 0.5 * (conds[1] + conds[3]) * (heads[1] - heads[3])
    y_place, y_size = place_of(axes_y), lax.axis_size(axes_y)
    base = place_of(("gx", "gy"))
    before = jnp.where(y_place > 0, got[jnp.maximum(base - 1, 0)], 0.0)
    after = jnp.where(y_place < y_size - 1, got[jnp.minimum(base + 1, got.shape[0] - 1)], 0.0)
    heads = (y_edges[0], y_edges[1], before, after)
    conds = [pltpu.roll(v, width_y - layers, 1) for v in heads]
    y_before = 0.5 * (conds[2] + conds[0]) * (heads[2] - heads[0])
    y_after = 0.5 * (conds[1] + conds[3]) * (heads[1] - heads[3])

    writes = []
    for i, (start, stop) in enumerate(parts):
        for copy in copies[2 * i : 2 * i + 2]:
            copy.wait()
        shape = (stop - start, width_x, width_y)
        part, cond = head[start:stop], conduct[start:stop]
        row, lane = iota(shape, 1), iota(shape, 2)
        wet_old = saturation(head_old[start:stop], alpha[start:stop])
        total = porosity[start:stop] * (wet[start:stop] - wet_old)
        for axis, place, size in ((1, row, width_x), (2, lane, width_y)):
            face = (
                0.5
                * (cond + pltpu.roll(cond, size - 1, axis))
                * (part - pltpu.roll(part, size - 1, axis))
            )
            face = jnp.where(place == size - 1, 0.0, face)
            total = total + (face - pltpu.roll(face, 1, axis))
        below = min(layers, stop + 1)
        part, cond = head[max(0, start - 1) : below], conduct[max(0, start - 1) : below]
        down = 0.5 * (cond[:-1] + cond[1:]) * (part[:-1] - part[1:] + 1.0)
        if start == 0:
            down = jnp.concatenate([jnp.zeros_like(cond[:1]), down], 0)
        if stop == layers:
            down = jnp.concatenate([down, cond[-1:]], 0)
        total = total + (down[1:] - down[:-1])
        row, lane = row[0], lane[0]
        for k in range(start, stop):
            edge = jnp.where(row == 0, -x_faces[0, k : k + 1, :], 0.0)
            edge = edge + jnp.where(row == width_x - 1, x_faces[1, k : k + 1, :], 0.0)
            low = pltpu.roll(y_before, (width_y - k) % width_y, 1)
            high = pltpu.roll(y_after, (width_y - 1 - k) % width_y, 1)
            edge = edge - jnp.where(lane == 0, low, 0.0) + jnp.where(lane == width_y - 1, high, 0.0)
            one = total[k - start] + edge
            out[k] = one - sources[k] if k < top else one
        rows = pl.ds(start, stop - start)
        copy = pltpu.make_async_copy(out.at[rows], residual.at[rows], out_sems.at[i])
        copy.start()
        writes.append(copy)
    for copy in writes:
        copy.wait()


def nitrate_kernel(per_block, back, nitrate, order, out, sat):
    height = LANES // per_block
    top = nitrate.shape[0]
    for h in range(back.shape[0] // height):
        rows = slice(h * height, (h + 1) * height)
        lanes = slice(h * LANES, (h + 1) * LANES)
        for k in range(top):
            where, slot = divmod(k, height)
            sat[k : k + 1, :] = join_blocks(back[rows, where, :], per_block, slot)
        loss = 0.3 * sat[...] * sat[...]
        value = nitrate[:, lanes]
        for _ in range(NSUB):
            upper = jnp.concatenate([value[:1], value[:-1]], 0)
            lower = jnp.concatenate([value[1:], value[-1:]], 0)
            value = value + 0.2 * (upper + lower - 2.0 * value) - loss * value
        out[:, lanes] = value


def swap_pairs(size, first):
    pairs = []
    for i in range(first, size - 1, 2):
        pairs += [(i, i + 1), (i + 1, i)]
    return pairs


def call(body, name, ins, outs, scratch=()):
    space = {"V": pltpu.VMEM, "S": pltpu.SMEM, "H": pltpu.HBM}
    return pl.pallas_call(
        body,
        out_shape=tuple(shape for shape, _ in outs),
        in_specs=[pl.BlockSpec(memory_space=space[i]) for i in ins],
        out_specs=tuple(pl.BlockSpec(memory_space=space[i]) for _, i in outs),
        scratch_shapes=scratch,
        name=name,
        compiler_params=pltpu.CompilerParams(vmem_limit_bytes=VMEM_LIMIT),
        cost_estimate=pl.CostEstimate(flops=1000, bytes_accessed=1000, transcendentals=0),
    )


def per_device(
    pressure,
    pressure_old,
    conductivity,
    vg_alpha,
    porosity,
    land_mask,
    nitrate,
    patch_column,
    crop_type,
    patch_weight,
    rain,
    root_decay,
):
    layers, width_x, width_y = pressure.shape
    top, slots = nitrate.shape
    group, axes_x, axes_y = ("gx", "gy"), ("sec", "gx"), ("gy",)
    owners = lax.axis_size(group)
    per_block = slots // owners
    if LANES % per_block or slots % LANES or per_block != width_x:
        raise ValueError("block size")
    if width_y != LANES or width_x % 8 or 2 * layers > FIELD_LANE:
        raise ValueError("grid size")
    height = LANES // per_block
    banks = slots // LANES
    wide = -(-top // height)
    f32 = jnp.float32
    shape, dma = jax.ShapeDtypeStruct, pltpu.SemaphoreType.DMA
    field = shape((layers, width_x, width_y), f32)
    field_in = pltpu.VMEM((layers, width_x, width_y), f32)
    count = len(parts_of(layers))

    flat = [v.reshape(banks, LANES) for v in (patch_column, crop_type, patch_weight, rain)]
    x_edge = shape((2 * layers, width_y), f32)
    sent, sat, head, alpha, conduct, wet, *x_sent, y_edges = call(
        functools.partial(front_kernel, per_block, top, axes_x, axes_y),
        "front",
        "HHHHHHH",
        (
            (shape((owners, per_block, LANES), f32), "H"),
            (shape((top * width_x, width_y), jnp.bfloat16), "V"),
            (field, "V"),
            (field, "V"),
            (field, "V"),
            (field, "V"),
            (x_edge, "V"),
            (x_edge, "V"),
            (shape((2, width_x, width_y), f32), "V"),
        ),
        (
            [pltpu.VMEM((banks, LANES), v.dtype) for v in flat],
            field_in,
            pltpu.VMEM((owners, per_block, LANES), f32),
            dma((4,)),
            dma((count, 3)),
            dma,
        ),
    )(*flat, pressure, vg_alpha, conductivity)
    got = lax.all_to_all(sent, group, split_axis=0, concat_axis=0, tiled=True)

    x_size = lax.axis_size(axes_x)
    x_got = [lax.ppermute(x_sent[i], axes_x, swap_pairs(x_size, i)) for i in (0, 1)]

    back, patch_sat, fields = call(
        functools.partial(pick_kernel, per_block, top, width_x),
        "pick",
        "VV",
        (
            (shape((owners, wide, LANES), f32), "V"),
            (shape((banks, wide * height, LANES), f32), "V"),
            (shape((banks, 8, LANES), f32), "V"),
        ),
    )(got, sat)
    back = lax.all_to_all(back, group, split_axis=0, concat_axis=0, tiled=True)

    residual, order = call(
        functools.partial(balance_kernel, top, axes_x, axes_y),
        "balance",
        "HHVVVVVVVSVVVVVV",
        ((field, "H"), (shape((8, LANES), f32), "V")),
        (
            field_in,
            field_in,
            field_in,
            pltpu.VMEM((2, layers, width_y), f32),
            dma((count, 2)),
            dma((count,)),
        ),
    )(
        pressure_old, porosity, head, alpha, conduct, wet, got, fields, patch_sat,
        root_decay, land_mask, *x_sent, *x_got, y_edges,
    )
    (nitrate_out,) = call(
        functools.partial(nitrate_kernel, per_block),
        "nitrate",
        "VVV",
        ((shape((top, slots), f32), "V"),),
        (pltpu.VMEM((top, LANES), f32),),
    )(back, nitrate, order)
    return (residual, nitrate_out)


def solution(mesh):
    placed = (
        P(None, ("sec", "gx"), "gy"),
        P(None, ("sec", "gx"), "gy"),
        P(None, ("sec", "gx"), "gy"),
        P(None, ("sec", "gx"), "gy"),
        P(None, ("sec", "gx"), "gy"),
        P(("sec", "gx"), "gy"),
        P(None, ("sec", "gx", "gy")),
        P(("sec", "gx", "gy")),
        P(("sec", "gx", "gy")),
        P(("sec", "gx", "gy")),
        P(("sec", "gx", "gy")),
        P(),
    )
    return jax.shard_map(
        per_device,
        mesh=mesh,
        in_specs=placed,
        out_specs=(P(None, ("sec", "gx"), "gy"), P(None, ("sec", "gx", "gy"))),
        check_vma=False,
    )
```

```python
import functools

import jax
import jax.numpy as jnp
from jax import lax
from jax.experimental import pallas as pl
from jax.experimental.pallas import tpu as pltpu
from jax.sharding import PartitionSpec as P

NSUB = 4
LANES = 128
CHUNK = 10
FIELD_LANE = 104
VMEM_LIMIT = 24 * 1024 * 1024


def iota(shape, dim):
    return lax.broadcasted_iota(jnp.int32, shape, dim)


def place_of(axes):
    index = 0
    for axis in axes:
        index = index * lax.axis_size(axis) + lax.axis_index(axis)
    return index


def parts_of(layers):
    return [(i, min(layers, i + CHUNK)) for i in range(0, layers, CHUNK)]


def saturation(head, alpha_field):
    suction = jnp.maximum(-head, 0.0) + jnp.log1p(jnp.exp(-jnp.abs(head)))
    scaled = alpha_field * suction
    return lax.rsqrt(1.0 + scaled * scaled)


def join_blocks(rows, per_block, slot):
    height = LANES // per_block
    if slot:
        rows = pltpu.roll(rows, LANES - slot * per_block, 1)
    moved = pltpu.roll(rows, 0, 1, stride=per_block, stride_axis=0)
    own = iota((height, LANES), 1) // per_block == iota((height, LANES), 0)
    return jnp.sum(jnp.where(own, moved, 0.0), axis=0, keepdims=True)


def front_kernel(per_block, *refs):
    fields, grids = refs[:4], refs[4:7]
    sent, head, alpha, perm, y_edges = refs[7:12]
    fields_in, sent_in, small_sems, sems, sent_sem = refs[12:]
    layers, width_x, width_y = head.shape
    height = LANES // per_block
    small = [pltpu.make_async_copy(fields[i], fields_in[i], small_sems.at[i]) for i in range(4)]
    for copy in small:
        copy.start()
    parts = parts_of(layers)
    large = []
    for i, (start, stop) in enumerate(parts):
        rows = pl.ds(start, stop - start)
        for j, (source, target) in enumerate(zip(grids, (head, alpha, perm))):
            copy = pltpu.make_async_copy(source.at[rows], target.at[rows], sems.at[i, j])
            copy.start()
            large.append(copy)
    for copy in small:
        copy.wait()
    for h in range(sent_in.shape[0] // height):
        rows = [ref[h : h + 1, :].astype(jnp.float32) for ref in fields_in]
        rows.append(jnp.zeros((4, LANES), jnp.float32))
        rows = [jnp.zeros((FIELD_LANE, LANES), jnp.float32), jnp.concatenate(rows, axis=0)]
        rows.append(jnp.zeros((LANES - FIELD_LANE - 8, LANES), jnp.float32))
        turned = jnp.concatenate(rows, axis=0).T
        sent_in[h * height : (h + 1) * height] = turned.reshape(height, per_block, LANES)
    lane = iota((width_x, width_y), 1)
    borders = [jnp.zeros((width_x, width_y), jnp.float32)] * 3
    for i, (start, stop) in enumerate(parts):
        for copy in large[3 * i : 3 * i + 3]:
            copy.wait()
        for k in range(start, stop):
            own = lane // 2 == k
            for j, ref in enumerate((head, alpha, perm)):
                moved = pltpu.roll(ref[k], (2 * k + 1) % width_y, 1)
                borders[j] = jnp.where(own, moved, borders[j])
    wet = saturation(borders[0], borders[1])
    cond = borders[2] * wet * wet * wet
    y_edges[0] = borders[0]
    y_edges[1] = cond
    even = lane % 2 == 0
    y_place, y_size = place_of(("gy",)), lax.axis_size("gy")
    base = place_of(("gx", "gy"))

    @pl.when(y_place > 0)
    def _():
        first = jnp.where(even, pltpu.roll(borders[0], width_y - 1, 1), cond)
        sent_in[base - 1] = sent_in[base - 1] + first

    @pl.when(y_place < y_size - 1)
    def _():
        last = jnp.where(even, cond, pltpu.roll(borders[0], 1, 1))
        sent_in[base + 1] = sent_in[base + 1] + last

    send = pltpu.make_async_copy(sent_in, sent, sent_sem)
    send.start()
    send.wait()


def wet_kernel(top, axes_x, *refs):
    head, alpha, perm = refs[:3]
    extra, (sat, conduct, wet_out, x_first, x_second) = refs[3:5], refs[5:10]
    extra_out, sems = refs[10:12], refs[12]
    layers, width_x, width_y = head.shape
    late = [pltpu.make_async_copy(extra[i], extra_out[i], sems.at[i]) for i in range(2)]
    for copy in late:
        copy.start()
    for start, stop in parts_of(layers):
        part = slice(start, stop)
        wet = saturation(head[part], alpha[part])
        conduct[part] = perm[part] * wet * wet * wet
        wet_out[part] = wet
        if start < top:
            last = min(stop, top)
            kept = wet[: last - start].reshape((last - start) * width_x, width_y)
            sat[start * width_x : last * width_x, :] = kept.astype(jnp.bfloat16)
    even = place_of(axes_x) % 2 == 0
    for field, ref in enumerate((head, conduct)):
        rows = slice(field * layers, (field + 1) * layers)
        low, high = ref[:, 0, :], ref[:, width_x - 1, :]
        x_first[rows, :] = jnp.where(even, high, low)
        x_second[rows, :] = jnp.where(even, low, high)
    for copy in late:
        copy.wait()


def hot(ids, size):
    return iota((size, LANES), 0) == ids


def pick_kernel(per_block, top, width_x, got, sat, back, patch_sat, fields):
    height = LANES // per_block
    width_y = sat.shape[1]
    for h in range(got.shape[0] // height):
        turned = got[h * height : (h + 1) * height].reshape(LANES, LANES).T
        rows = turned[FIELD_LANE : FIELD_LANE + 8]
        fields[h] = rows
        ids = rows[0:1].astype(jnp.int32)
        lane_hot = hot(lax.rem(ids, width_y), width_y).astype(jnp.float32).astype(jnp.bfloat16)
        row_hot = hot(lax.div(ids, width_y), width_x)
        picked = jnp.dot(sat[...], lane_hot, preferred_element_type=jnp.float32)
        patch_sat[h] = jnp.zeros(patch_sat.shape[1:], jnp.float32)
        for k in range(top):
            one = picked[k * width_x : (k + 1) * width_x]
            patch_sat[h, k : k + 1, :] = jnp.sum(
                jnp.where(row_hot, one, 0.0), axis=0, keepdims=True
            )
        for i in range(back.shape[1]):
            block = patch_sat[h, i * height : (i + 1) * height, :]
            for j in range(height):
                row = slice(h * height + j, h * height + j + 1)
                back[row, i, :] = join_blocks(block, per_block, j)


def column_sources(top, width_x, width_y, fields, patch_sat, root_decay):
    total = jnp.zeros((top * width_x, width_y), jnp.float32)
    table = root_decay[...]
    for h in range(fields.shape[0]):
        ids, crop, weight, rain = (fields[h, i : i + 1, :] for i in range(4))
        ids = ids.astype(jnp.int32)
        crop = crop.astype(jnp.int32)
        decay = jnp.zeros((1, LANES), jnp.float32)
        for kind in range(table.shape[1]):
            decay = jnp.where(crop == kind, table[:, kind : kind + 1], decay)
        level = iota((top, LANES), 0)
        profile = jnp.exp(-(level.astype(jnp.float32) + 0.5) * decay)
        profile = profile / jnp.sum(profile, axis=0, keepdims=True)
        sat = patch_sat[h][:top]
        inflow = jnp.where(level == 0, rain * (1.0 - sat), 0.0)
        sources = inflow - weight * profile * sat
        lane_hot = hot(lax.rem(ids, width_y), width_y).astype(jnp.float32)
        row_hot = hot(lax.div(ids, width_y), width_x)
        spread = jnp.concatenate(
            [jnp.where(row_hot, sources[k : k + 1], 0.0) for k in range(top)], axis=0
        )
        total = total + lax.dot_general(
            spread,
            lane_hot,
            (((1,), (1,)), ((), ())),
            precision=lax.Precision.HIGHEST,
            preferred_element_type=jnp.float32,
        )
    return total


def balance_kernel(top, axes_x, *refs):
    grids = refs[:2]
    head, alpha, conduct, wet, got, fields, patch_sat, root_decay, land = refs[2:11]
    x_sent, x_got, y_edges = refs[11:13], refs[13:15], refs[15]
    residual, order = refs[16:18]
    head_old, porosity, out, x_faces, sems, out_sems = refs[18:]
    layers, width_x, width_y = head.shape
    parts = parts_of(layers)
    copies = []
    for i, (start, stop) in enumerate(parts):
        rows = pl.ds(start, stop - start)
        for j, (source, target) in enumerate(zip(grids, (head_old, porosity))):
            copy = pltpu.make_async_copy(source.at[rows], target.at[rows], sems.at[i, j])
            copy.start()
            copies.append(copy)
    order[...] = jnp.zeros(order.shape, order.dtype)
    sources = column_sources(top, width_x, width_y, fields, patch_sat, root_decay)
    sources = sources.reshape(top, width_x, width_y) * land[...].astype(jnp.float32)[None]

    even = place_of(axes_x) % 2 == 0
    faces = []
    for rows in (slice(0, layers), slice(layers, 2 * layers)):
        first, second = (r[rows, :] for r in x_sent)
        low, high = jnp.where(even, second, first), jnp.where(even, first, second)
        first, second = (r[rows, :] for r in x_got)
        before, after = jnp.where(even, second, first), jnp.where(even, first, second)
        faces.append((low, high, before, after))
    heads, conds = faces
    x_faces[0] = 0.5 * (conds[2] + conds[0]) * (heads[2] - heads[0])
    x_faces[1] = 0.5 * (conds[1] + conds[3]) * (heads[1] - heads[3])
    y_place, y_size = place_of(("gy",)), lax.axis_size("gy")
    base = place_of(("gx", "gy"))
    before = jnp.where(y_place > 0, got[jnp.maximum(base - 1, 0)], 0.0)
    after = jnp.where(y_place < y_size - 1, got[jnp.minimum(base + 1, got.shape[0] - 1)], 0.0)
    part, cond = y_edges[0], y_edges[1]
    last = 0.5 * (cond + pltpu.roll(after, width_y - 1, 1)) * (part - after)
    first = 0.5 * (cond + pltpu.roll(before, 1, 1)) * (part - before)
    lane = iota((width_x, width_y), 1)
    y_flux = jnp.where(lane % 2 == 0, last, first)
    y_border = (lane == 0) | (lane == width_y - 1)

    writes = []
    for i, (start, stop) in enumerate(parts):
        for copy in copies[2 * i : 2 * i + 2]:
            copy.wait()
        shape = (stop - start, width_x, width_y)
        part, cond = head[start:stop], conduct[start:stop]
        row, lane = iota(shape, 1), iota(shape, 2)
        wet_old = saturation(head_old[start:stop], alpha[start:stop])
        total = porosity[start:stop] * (wet[start:stop] - wet_old)
        for axis, place, size in ((1, row, width_x), (2, lane, width_y)):
            face = (
                0.5
                * (cond + pltpu.roll(cond, size - 1, axis))
                * (part - pltpu.roll(part, size - 1, axis))
            )
            face = jnp.where(place == size - 1, 0.0, face)
            total = total + (face - pltpu.roll(face, 1, axis))
        below = min(layers, stop + 1)
        part, cond = head[max(0, start - 1) : below], conduct[max(0, start - 1) : below]
        down = 0.5 * (cond[:-1] + cond[1:]) * (part[:-1] - part[1:] + 1.0)
        if start == 0:
            down = jnp.concatenate([jnp.zeros_like(cond[:1]), down], 0)
        if stop == layers:
            down = jnp.concatenate([down, cond[-1:]], 0)
        total = total + (down[1:] - down[:-1])
        row = row[0]
        for k in range(start, stop):
            edge = jnp.where(row == 0, -x_faces[0, k : k + 1, :], 0.0)
            edge = edge + jnp.where(row == width_x - 1, x_faces[1, k : k + 1, :], 0.0)
            edge = edge + jnp.where(y_border, pltpu.roll(y_flux, width_y - 1 - 2 * k, 1), 0.0)
            one = total[k - start] + edge
            out[k] = one - sources[k] if k < top else one
        rows = pl.ds(start, stop - start)
        copy = pltpu.make_async_copy(out.at[rows], residual.at[rows], out_sems.at[i])
        copy.start()
        writes.append(copy)
    for copy in writes:
        copy.wait()


def nitrate_kernel(per_block, back, nitrate, order, out, sat):
    height = LANES // per_block
    top = nitrate.shape[0]
    for h in range(back.shape[0] // height):
        rows = slice(h * height, (h + 1) * height)
        lanes = slice(h * LANES, (h + 1) * LANES)
        for k in range(top):
            where, slot = divmod(k, height)
            sat[k : k + 1, :] = join_blocks(back[rows, where, :], per_block, slot)
        loss = 0.3 * sat[...] * sat[...]
        value = nitrate[:, lanes]
        for _ in range(NSUB):
            upper = jnp.concatenate([value[:1], value[:-1]], 0)
            lower = jnp.concatenate([value[1:], value[-1:]], 0)
            value = value + 0.2 * (upper + lower - 2.0 * value) - loss * value
        out[:, lanes] = value


def swap_pairs(size, first):
    pairs = []
    for i in range(first, size - 1, 2):
        pairs += [(i, i + 1), (i + 1, i)]
    return pairs


def call(body, name, ins, outs, scratch=()):
    space = {"V": pltpu.VMEM, "S": pltpu.SMEM, "H": pltpu.HBM}
    kernel = pl.pallas_call(
        body,
        out_shape=tuple(shape for shape, _ in outs),
        in_specs=[pl.BlockSpec(memory_space=space[i]) for i in ins],
        out_specs=tuple(pl.BlockSpec(memory_space=space[i]) for _, i in outs),
        scratch_shapes=scratch,
        name=name,
        compiler_params=pltpu.CompilerParams(vmem_limit_bytes=VMEM_LIMIT),
        cost_estimate=pl.CostEstimate(flops=1000, bytes_accessed=1000, transcendentals=0),
    )

    def run(*args):
        return kernel(
            *(
                pltpu.with_memory_space_constraint(arg, pltpu.HBM) if i == "H" else arg
                for i, arg in zip(ins, args)
            )
        )

    return run


def per_device(
    pressure,
    pressure_old,
    conductivity,
    vg_alpha,
    porosity,
    land_mask,
    nitrate,
    patch_column,
    crop_type,
    patch_weight,
    rain,
    root_decay,
):
    layers, width_x, width_y = pressure.shape
    top, slots = nitrate.shape
    group, axes_x = ("gx", "gy"), ("sec", "gx")
    owners = lax.axis_size(group)
    per_block = slots // owners
    if LANES % per_block or slots % LANES or per_block != width_x:
        raise ValueError("block size")
    if width_y != LANES or width_x % 8 or 2 * layers > FIELD_LANE:
        raise ValueError("grid size")
    height = LANES // per_block
    banks = slots // LANES
    wide = -(-top // height)
    f32 = jnp.float32
    shape, dma = jax.ShapeDtypeStruct, pltpu.SemaphoreType.DMA
    field = shape((layers, width_x, width_y), f32)
    field_in = pltpu.VMEM((layers, width_x, width_y), f32)
    count = len(parts_of(layers))

    flat = [v.reshape(banks, LANES) for v in (patch_column, crop_type, patch_weight, rain)]
    x_edge = shape((2 * layers, width_y), f32)
    sent, head, alpha, perm, y_edges = call(
        functools.partial(front_kernel, per_block),
        "front",
        "HHHHHHH",
        (
            (shape((owners, per_block, LANES), f32), "H"),
            (field, "V"),
            (field, "V"),
            (field, "V"),
            (shape((2, width_x, width_y), f32), "V"),
        ),
        (
            [pltpu.VMEM((banks, LANES), v.dtype) for v in flat],
            pltpu.VMEM((owners, per_block, LANES), f32),
            dma((4,)),
            dma((count, 3)),
            dma,
        ),
    )(*flat, pressure, vg_alpha, conductivity)
    sat, conduct, wet, *x_sent, land, table = call(
        functools.partial(wet_kernel, top, axes_x),
        "wet",
        "VVVHH",
        (
            (shape((top * width_x, width_y), jnp.bfloat16), "V"),
            (field, "V"),
            (field, "V"),
            (x_edge, "V"),
            (x_edge, "V"),
            (shape((width_x, width_y), land_mask.dtype), "V"),
            (shape((1, root_decay.shape[0]), f32), "V"),
        ),
        (dma((2,)),),
    )(head, alpha, perm, land_mask, root_decay.reshape(1, -1))
    got = lax.all_to_all(sent, group, split_axis=0, concat_axis=0, tiled=True)

    x_size = lax.axis_size(axes_x)
    x_got = [lax.ppermute(x_sent[i], axes_x, swap_pairs(x_size, i)) for i in (0, 1)]

    back, patch_sat, fields = call(
        functools.partial(pick_kernel, per_block, top, width_x),
        "pick",
        "VV",
        (
            (shape((owners, wide, LANES), f32), "V"),
            (shape((banks, wide * height, LANES), f32), "V"),
            (shape((banks, 8, LANES), f32), "V"),
        ),
    )(got, sat)
    back = lax.all_to_all(back, group, split_axis=0, concat_axis=0, tiled=True)

    residual, order = call(
        functools.partial(balance_kernel, top, axes_x),
        "balance",
        "HHVVVVVVVVVVVVVV",
        ((field, "H"), (shape((8, LANES), f32), "V")),
        (
            field_in,
            field_in,
            field_in,
            pltpu.VMEM((2, layers, width_y), f32),
            dma((count, 2)),
            dma((count,)),
        ),
    )(
        pressure_old, porosity, head, alpha, conduct, wet, got, fields, patch_sat,
        table, land, *x_sent, *x_got, y_edges,
    )
    (nitrate_out,) = call(
        functools.partial(nitrate_kernel, per_block),
        "nitrate",
        "VVV",
        ((shape((top, slots), f32), "V"),),
        (pltpu.VMEM((top, LANES), f32),),
    )(back, nitrate, order)
    return (residual, nitrate_out)


def solution(mesh):
    placed = (
        P(None, ("sec", "gx"), "gy"),
        P(None, ("sec", "gx"), "gy"),
        P(None, ("sec", "gx"), "gy"),
        P(None, ("sec", "gx"), "gy"),
        P(None, ("sec", "gx"), "gy"),
        P(("sec", "gx"), "gy"),
        P(None, ("sec", "gx", "gy")),
        P(("sec", "gx", "gy")),
        P(("sec", "gx", "gy")),
        P(("sec", "gx", "gy")),
        P(("sec", "gx", "gy")),
        P(),
    )
    return jax.shard_map(
        per_device,
        mesh=mesh,
        in_specs=placed,
        out_specs=(P(None, ("sec", "gx"), "gy"), P(None, ("sec", "gx", "gy"))),
        check_vma=False,
    )
```

```python
import functools

import jax
import jax.numpy as jnp
from jax import lax
from jax.experimental import pallas as pl
from jax.experimental.pallas import tpu as pltpu
from jax.sharding import PartitionSpec as P

NSUB = 4
LANES = 128
CHUNK = 10
FRONT_CHUNK = 25
FIELD_LANE = 104
VMEM_LIMIT = 24 * 1024 * 1024


def iota(shape, dim):
    return lax.broadcasted_iota(jnp.int32, shape, dim)


def place_of(axes):
    index = 0
    for axis in axes:
        index = index * lax.axis_size(axis) + lax.axis_index(axis)
    return index


def parts_of(layers, size=CHUNK):
    return [(i, min(layers, i + size)) for i in range(0, layers, size)]


def saturation(head, alpha_field):
    suction = jnp.maximum(-head, 0.0) + jnp.log1p(jnp.exp(-jnp.abs(head)))
    scaled = alpha_field * suction
    return lax.rsqrt(1.0 + scaled * scaled)


def fold_border(border, own_first):
    rows, width = border.shape
    upper, lower = border[: rows // 2], border[rows // 2 :]
    if own_first:
        upper = pltpu.roll(upper, width - 1, 1)
    else:
        lower = pltpu.roll(lower, 1, 1)
    return jnp.where(iota(upper.shape, 1) % 2 == 0, upper, lower)


def unfold_border(block, place):
    width = block.shape[1]
    moved = pltpu.roll(block, 1 if place else width - 1, 1)
    return jnp.concatenate([moved, block] if place else [block, moved], axis=0)


def add_border(blocks, border):
    y_place, y_size = place_of(("gy",)), lax.axis_size("gy")
    base = place_of(("gx", "gy"))

    @pl.when(y_place > 0)
    def _():
        blocks[base - 1] = blocks[base - 1] + fold_border(border, True)

    @pl.when(y_place < y_size - 1)
    def _():
        blocks[base + 1] = blocks[base + 1] + fold_border(border, False)


def neighbour_borders(blocks):
    y_place, y_size = place_of(("gy",)), lax.axis_size("gy")
    base = place_of(("gx", "gy"))
    before = blocks[jnp.maximum(base - 1, 0)]
    before = unfold_border(jnp.where(y_place > 0, before, 0.0), 1)
    after = blocks[jnp.minimum(base + 1, blocks.shape[0] - 1)]
    after = unfold_border(jnp.where(y_place < y_size - 1, after, 0.0), 0)
    return jnp.where(iota(after.shape, 1) % 2 == 0, after, before)


def border_of(ref, start, stop, border):
    lane = iota(border.shape, 1)
    for k in range(start, stop):
        moved = pltpu.roll(ref[k], (2 * k + 1) % LANES, 1)
        border = jnp.where(lane // 2 == k, moved, border)
    return border


def pack_blocks(rows, count, blocks, bank):
    height, size = blocks.shape[1], LANES // (2 * blocks.shape[1])
    above = jnp.zeros((FIELD_LANE, LANES), jnp.float32)
    below = jnp.zeros((LANES - FIELD_LANE - rows.shape[0], LANES), jnp.float32)
    turned = jnp.concatenate([above, rows, below], axis=0).T
    for b in range(size):
        upper = turned[2 * b * height : (2 * b + 1) * height]
        lower = turned[(2 * b + 1) * height : (2 * b + 2) * height]
        blocks[bank * size + b] = upper + pltpu.roll(lower, count, 1)


def unpack_blocks(blocks, count, bank, height):
    rows, size = blocks.shape[1], LANES // (2 * blocks.shape[1])
    pieces = []
    for b in range(size):
        block = blocks[bank * size + b]
        pieces += [block, pltpu.roll(block, LANES - count, 1)]
    turned = jnp.concatenate(pieces, axis=0).T
    return turned[FIELD_LANE : FIELD_LANE + height]


def front_kernel(top, *refs):
    fields, grids, extra = refs[:4], refs[4:7], refs[7:9]
    sent, head, alpha, conduct, wet_out, sat, border_out = refs[9:16]
    extra_out, (fields_in, perm, sent_in, small_sems, sems, sent_sem) = refs[16:18], refs[18:]
    layers, width_x, width_y = head.shape
    small = [pltpu.make_async_copy(fields[i], fields_in[i], small_sems.at[i]) for i in range(4)]
    extras = [pltpu.make_async_copy(extra[i], extra_out[i], small_sems.at[4 + i]) for i in range(2)]
    parts = parts_of(layers, FRONT_CHUNK)
    large = []
    for i, (start, stop) in enumerate(parts):
        rows = pl.ds(start, stop - start)
        large.append(
            [
                pltpu.make_async_copy(source.at[rows], target.at[rows], sems.at[i, j])
                for j, (source, target) in enumerate(zip(grids, (head, alpha, perm)))
            ]
        )
    for copy in (*small, *(copies[j] for j in range(3) for copies in large), *extras):
        copy.start()
    for copy in small:
        copy.wait()
    for bank in range(fields_in[0].shape[0]):
        rows = [ref[bank : bank + 1, :].astype(jnp.float32) for ref in fields_in]
        rows.append(jnp.zeros((4, LANES), jnp.float32))
        pack_blocks(jnp.concatenate(rows, axis=0), 4, sent_in, bank)
    border = jnp.zeros((width_x, width_y), jnp.float32)
    for i, (start, stop) in enumerate(parts):
        large[i][0].wait()
        border = border_of(head, start, stop, border)
    border_out[...] = border
    add_border(sent_in, border)
    send = pltpu.make_async_copy(sent_in, sent, sent_sem)
    send.start()
    for i, (start, stop) in enumerate(parts):
        large[i][1].wait()
        large[i][2].wait()
        part = slice(start, stop)
        wet = saturation(head[part], alpha[part])
        conduct[part] = perm[part] * wet * wet * wet
        wet_out[part] = wet
        if start < top:
            last = min(stop, top)
            kept = wet[: last - start].reshape((last - start) * width_x, width_y)
            sat[start * width_x : last * width_x, :] = kept.astype(jnp.bfloat16)
    for copy in (*extras, send):
        copy.wait()


def edge_kernel(axes_x, head, conduct, x_first, x_second, border_out):
    layers, width_x, width_y = head.shape
    border = jnp.zeros((width_x, width_y), jnp.float32)
    border_out[...] = border_of(conduct, 0, layers, border)
    even = place_of(axes_x) % 2 == 0
    for field, ref in enumerate((head, conduct)):
        rows = slice(field * layers, (field + 1) * layers)
        low, high = ref[:, 0, :], ref[:, width_x - 1, :]
        x_first[rows, :] = jnp.where(even, high, low)
        x_second[rows, :] = jnp.where(even, low, high)


def hot(ids, size):
    return iota((size, LANES), 0) == ids


def pick_kernel(top, width_x, got, sat, border, back, patch_sat, fields):
    width_y = sat.shape[1]
    for bank in range(fields.shape[0]):
        rows = unpack_blocks(got, 4, bank, 8)
        fields[bank] = rows
        ids = rows[0:1].astype(jnp.int32)
        lane_hot = hot(lax.rem(ids, width_y), width_y).astype(jnp.float32).astype(jnp.bfloat16)
        row_hot = hot(lax.div(ids, width_y), width_x)
        picked = jnp.dot(sat[...], lane_hot, preferred_element_type=jnp.float32)
        patch_sat[bank] = jnp.zeros(patch_sat.shape[1:], jnp.float32)
        for k in range(top):
            one = picked[k * width_x : (k + 1) * width_x]
            patch_sat[bank, k : k + 1, :] = jnp.sum(
                jnp.where(row_hot, one, 0.0), axis=0, keepdims=True
            )
        pack_blocks(patch_sat[bank], top, back, bank)
    add_border(back, border[...])


def column_sources(top, width_x, width_y, fields, patch_sat, root_decay):
    total = jnp.zeros((top * width_x, width_y), jnp.float32)
    table = root_decay[...]
    for h in range(fields.shape[0]):
        ids, crop, weight, rain = (fields[h, i : i + 1, :] for i in range(4))
        ids = ids.astype(jnp.int32)
        crop = crop.astype(jnp.int32)
        decay = jnp.zeros((1, LANES), jnp.float32)
        for kind in range(table.shape[1]):
            decay = jnp.where(crop == kind, table[:, kind : kind + 1], decay)
        level = iota((top, LANES), 0)
        profile = jnp.exp(-(level.astype(jnp.float32) + 0.5) * decay)
        profile = profile / jnp.sum(profile, axis=0, keepdims=True)
        sat = patch_sat[h][:top]
        inflow = jnp.where(level == 0, rain * (1.0 - sat), 0.0)
        sources = inflow - weight * profile * sat
        lane_hot = hot(lax.rem(ids, width_y), width_y).astype(jnp.float32)
        row_hot = hot(lax.div(ids, width_y), width_x)
        spread = jnp.concatenate(
            [jnp.where(row_hot, sources[k : k + 1], 0.0) for k in range(top)], axis=0
        )
        total = total + lax.dot_general(
            spread,
            lane_hot,
            (((1,), (1,)), ((), ())),
            precision=lax.Precision.HIGHEST,
            preferred_element_type=jnp.float32,
        )
    return total


def balance_kernel(top, axes_x, *refs):
    head_old, porosity = refs[:2]
    head, alpha, conduct, wet, fields, patch_sat, root_decay, land = refs[2:10]
    x_sent, x_got, out = refs[10:12], refs[12:14], refs[14]
    x_faces = refs[15]
    layers, width_x, width_y = head.shape
    parts = parts_of(layers)
    sources = column_sources(top, width_x, width_y, fields, patch_sat, root_decay)
    sources = sources.reshape(top, width_x, width_y) * land[...].astype(jnp.float32)[None]

    even = place_of(axes_x) % 2 == 0
    faces = []
    for rows in (slice(0, layers), slice(layers, 2 * layers)):
        first, second = (r[rows, :] for r in x_sent)
        low, high = jnp.where(even, second, first), jnp.where(even, first, second)
        first, second = (r[rows, :] for r in x_got)
        before, after = jnp.where(even, second, first), jnp.where(even, first, second)
        faces.append((low, high, before, after))
    heads, conds = faces
    x_faces[0] = 0.5 * (conds[2] + conds[0]) * (heads[2] - heads[0])
    x_faces[1] = 0.5 * (conds[1] + conds[3]) * (heads[1] - heads[3])
    for i, (start, stop) in enumerate(parts):
        shape = (stop - start, width_x, width_y)
        part, cond = head[start:stop], conduct[start:stop]
        row, lane = iota(shape, 1), iota(shape, 2)
        wet_old = saturation(head_old[start:stop], alpha[start:stop])
        total = porosity[start:stop] * (wet[start:stop] - wet_old)
        for axis, place, size in ((1, row, width_x), (2, lane, width_y)):
            face = (
                0.5
                * (cond + pltpu.roll(cond, size - 1, axis))
                * (part - pltpu.roll(part, size - 1, axis))
            )
            face = jnp.where(place == size - 1, 0.0, face)
            total = total + (face - pltpu.roll(face, 1, axis))
        below = min(layers, stop + 1)
        part, cond = head[max(0, start - 1) : below], conduct[max(0, start - 1) : below]
        down = 0.5 * (cond[:-1] + cond[1:]) * (part[:-1] - part[1:] + 1.0)
        if start == 0:
            down = jnp.concatenate([jnp.zeros_like(cond[:1]), down], 0)
        if stop == layers:
            down = jnp.concatenate([down, cond[-1:]], 0)
        total = total + (down[1:] - down[:-1])
        row = row[0]
        for k in range(start, stop):
            edge = jnp.where(row == 0, -x_faces[0, k : k + 1, :], 0.0)
            edge = edge + jnp.where(row == width_x - 1, x_faces[1, k : k + 1, :], 0.0)
            one = total[k - start] + edge
            out[k] = one - sources[k] if k < top else one


def last_kernel(back, got, heads, conds, partial, nitrate, residual, nitrate_out, out, value_out, sems):
    layers, width_x, width_y = partial.shape
    top = nitrate.shape[0]
    head, cond = heads[...], conds[...]
    flux = 0.5 * (cond + neighbour_borders(back)) * (head - neighbour_borders(got))
    lane = iota(flux.shape, 1)
    on_border = (lane == 0) | (lane == width_y - 1)
    parts = parts_of(layers, 2 * CHUNK)
    writes = []
    for i, (start, stop) in enumerate(parts):
        for k in range(start, stop):
            edge = pltpu.roll(flux, width_y - 1 - 2 * k, 1)
            out[k] = partial[k] + jnp.where(on_border, edge, 0.0)
        rows = pl.ds(start, stop - start)
        copy = pltpu.make_async_copy(out.at[rows], residual.at[rows], sems.at[i])
        copy.start()
        writes.append(copy)
    for bank in range(nitrate.shape[1] // LANES):
        sat = unpack_blocks(back, top, bank, 16)[:top]
        lanes = slice(bank * LANES, (bank + 1) * LANES)
        loss = 0.3 * sat * sat
        value = nitrate[:, lanes]
        for _ in range(NSUB):
            upper = jnp.concatenate([value[:1], value[:-1]], 0)
            lower = jnp.concatenate([value[1:], value[-1:]], 0)
            value = value + 0.2 * (upper + lower - 2.0 * value) - loss * value
        value_out[:, lanes] = value
    copy = pltpu.make_async_copy(value_out, nitrate_out, sems.at[len(parts)])
    copy.start()
    writes.append(copy)
    for copy in writes:
        copy.wait()


def swap_pairs(size, first):
    pairs = []
    for i in range(first, size - 1, 2):
        pairs += [(i, i + 1), (i + 1, i)]
    return pairs


def call(body, name, ins, outs, scratch=(), cost=1000):
    space = {"V": pltpu.VMEM, "S": pltpu.SMEM, "H": pltpu.HBM}
    kernel = pl.pallas_call(
        body,
        out_shape=tuple(shape for shape, _ in outs),
        in_specs=[pl.BlockSpec(memory_space=space[i]) for i in ins],
        out_specs=tuple(pl.BlockSpec(memory_space=space[i]) for _, i in outs),
        scratch_shapes=scratch,
        name=name,
        compiler_params=pltpu.CompilerParams(vmem_limit_bytes=VMEM_LIMIT),
        cost_estimate=pl.CostEstimate(flops=1000000000 if cost>1000 else 1000, bytes_accessed=cost, transcendentals=0),
    )

    def run(*args):
        return kernel(
            *(
                pltpu.with_memory_space_constraint(arg, pltpu.HBM) if i == "H" else arg
                for i, arg in zip(ins, args)
            )
        )

    return run


def per_device(
    pressure,
    pressure_old,
    conductivity,
    vg_alpha,
    porosity,
    land_mask,
    nitrate,
    patch_column,
    crop_type,
    patch_weight,
    rain,
    root_decay,
):
    layers, width_x, width_y = pressure.shape
    top, slots = nitrate.shape
    group, axes_x = ("gx", "gy"), ("sec", "gx")
    owners = lax.axis_size(group)
    per_block = slots // owners
    if LANES % per_block or slots % LANES or per_block != width_x:
        raise ValueError("block size")
    if width_y != LANES or width_x != 16 or 2 * layers > FIELD_LANE or FIELD_LANE + 2 * top > LANES:
        raise ValueError("grid size")
    half = width_x // 2
    banks = slots // LANES
    f32 = jnp.float32
    shape, dma = jax.ShapeDtypeStruct, pltpu.SemaphoreType.DMA
    field = shape((layers, width_x, width_y), f32)
    field_in = pltpu.VMEM((layers, width_x, width_y), f32)
    count, halves = len(parts_of(layers)), len(parts_of(layers, 2 * CHUNK))
    blocks = shape((owners, half, LANES), f32)
    border = shape((width_x, width_y), f32)

    flat = [v.reshape(banks, LANES) for v in (patch_column, crop_type, patch_weight, rain)]
    x_edge = shape((2 * layers, width_y), f32)
    sent, head, alpha, conduct, wet, sat, head_border, land, table = call(
        functools.partial(front_kernel, top),
        "front",
        "HHHHHHHHH",
        (
            (blocks, "H"),
            (field, "V"),
            (field, "V"),
            (field, "V"),
            (field, "V"),
            (shape((top * width_x, width_y), jnp.bfloat16), "V"),
            (border, "V"),
            (shape((width_x, width_y), land_mask.dtype), "V"),
            (shape((1, root_decay.shape[0]), f32), "V"),
        ),
        (
            [pltpu.VMEM((banks, LANES), v.dtype) for v in flat],
            field_in,
            pltpu.VMEM((owners, half, LANES), f32),
            dma((6,)),
            dma((len(parts_of(layers, FRONT_CHUNK)), 3)),
            dma,
        ),
    )(*flat, pressure, vg_alpha, conductivity, land_mask, root_decay.reshape(1, -1))
    got = lax.all_to_all(sent, group, split_axis=0, concat_axis=0, tiled=True)
    *x_sent, cond_border = call(
        functools.partial(edge_kernel, axes_x),
        "edge",
        "VV",
        ((x_edge, "V"), (x_edge, "V"), (border, "V")),
    )(head, conduct)

    x_size = lax.axis_size(axes_x)
    x_got = [lax.ppermute(x_sent[i], axes_x, swap_pairs(x_size, i)) for i in (0, 1)]

    back, patch_sat, fields = call(
        functools.partial(pick_kernel, top, width_x),
        "pick",
        "VVV",
        (
            (blocks, "V"),
            (shape((banks, 16, LANES), f32), "V"),
            (shape((banks, 8, LANES), f32), "V"),
        ),
    )(got, sat, cond_border)
    back = lax.all_to_all(back, group, split_axis=0, concat_axis=0, tiled=True)

    (partial,) = call(
        functools.partial(balance_kernel, top, axes_x),
        "balance",
        "VVVVVVVVVVVVVV",
        ((field, "V"),),
        (pltpu.VMEM((2, layers, width_y), f32),),
        cost=3000000,
    )(
        pressure_old, porosity, head, alpha, conduct, wet, fields, patch_sat,
        table, land, *x_sent, *x_got,
    )
    residual, nitrate_out = call(
        last_kernel,
        "last",
        "VVVVVV",
        ((field, "H"), (shape((top, slots), f32), "H")),
        (field_in, pltpu.VMEM((top, slots), f32), dma((halves + 1,))),
    )(back, got, head_border, cond_border, partial, nitrate)
    return (residual, nitrate_out)


def solution(mesh):
    placed = (
        P(None, ("sec", "gx"), "gy"),
        P(None, ("sec", "gx"), "gy"),
        P(None, ("sec", "gx"), "gy"),
        P(None, ("sec", "gx"), "gy"),
        P(None, ("sec", "gx"), "gy"),
        P(("sec", "gx"), "gy"),
        P(None, ("sec", "gx", "gy")),
        P(("sec", "gx", "gy")),
        P(("sec", "gx", "gy")),
        P(("sec", "gx", "gy")),
        P(("sec", "gx", "gy")),
        P(),
    )
    return jax.shard_map(
        per_device,
        mesh=mesh,
        in_specs=placed,
        out_specs=(P(None, ("sec", "gx"), "gy"), P(None, ("sec", "gx", "gy"))),
        check_vma=False,
    )
```

```python
import functools

import jax
import jax.numpy as jnp
from jax import lax
from jax.experimental import pallas as pl
from jax.experimental.pallas import tpu as pltpu
from jax.sharding import PartitionSpec as P

NSUB = 4
LANES = 128
CHUNK = 10
FRONT_CHUNK = 25
FIELD_LANE = 104
VMEM_LIMIT = 24 * 1024 * 1024


def iota(shape, dim):
    return lax.broadcasted_iota(jnp.int32, shape, dim)


def place_of(axes):
    index = 0
    for axis in axes:
        index = index * lax.axis_size(axis) + lax.axis_index(axis)
    return index


def parts_of(layers, size=CHUNK):
    return [(i, min(layers, i + size)) for i in range(0, layers, size)]


def saturation(head, alpha_field):
    suction = jnp.maximum(-head, 0.0) + jnp.log1p(jnp.exp(-jnp.abs(head)))
    scaled = alpha_field * suction
    return lax.rsqrt(1.0 + scaled * scaled)


def fold_border(border, own_first):
    rows, width = border.shape
    upper, lower = border[: rows // 2], border[rows // 2 :]
    if own_first:
        upper = pltpu.roll(upper, width - 1, 1)
    else:
        lower = pltpu.roll(lower, 1, 1)
    return jnp.where(iota(upper.shape, 1) % 2 == 0, upper, lower)


def unfold_border(block, place):
    width = block.shape[1]
    moved = pltpu.roll(block, 1 if place else width - 1, 1)
    return jnp.concatenate([moved, block] if place else [block, moved], axis=0)


def add_border(blocks, border):
    y_place, y_size = place_of(("gy",)), lax.axis_size("gy")
    base = place_of(("gx", "gy"))

    @pl.when(y_place > 0)
    def _():
        blocks[base - 1] = blocks[base - 1] + fold_border(border, True)

    @pl.when(y_place < y_size - 1)
    def _():
        blocks[base + 1] = blocks[base + 1] + fold_border(border, False)


def neighbour_borders(blocks):
    y_place, y_size = place_of(("gy",)), lax.axis_size("gy")
    base = place_of(("gx", "gy"))
    before = blocks[jnp.maximum(base - 1, 0)]
    before = unfold_border(jnp.where(y_place > 0, before, 0.0), 1)
    after = blocks[jnp.minimum(base + 1, blocks.shape[0] - 1)]
    after = unfold_border(jnp.where(y_place < y_size - 1, after, 0.0), 0)
    return jnp.where(iota(after.shape, 1) % 2 == 0, after, before)


def border_of(ref, start, stop, border):
    lane = iota(border.shape, 1)
    for k in range(start, stop):
        moved = pltpu.roll(ref[k], (2 * k + 1) % LANES, 1)
        border = jnp.where(lane // 2 == k, moved, border)
    return border


def pack_blocks(rows, count, blocks, bank):
    height, size = blocks.shape[1], LANES // (2 * blocks.shape[1])
    above = jnp.zeros((FIELD_LANE, LANES), jnp.float32)
    below = jnp.zeros((LANES - FIELD_LANE - rows.shape[0], LANES), jnp.float32)
    turned = jnp.concatenate([above, rows, below], axis=0).T
    for b in range(size):
        upper = turned[2 * b * height : (2 * b + 1) * height]
        lower = turned[(2 * b + 1) * height : (2 * b + 2) * height]
        blocks[bank * size + b] = upper + pltpu.roll(lower, count, 1)


def unpack_blocks(blocks, count, bank, height):
    rows, size = blocks.shape[1], LANES // (2 * blocks.shape[1])
    pieces = []
    for b in range(size):
        block = blocks[bank * size + b]
        pieces += [block, pltpu.roll(block, LANES - count, 1)]
    turned = jnp.concatenate(pieces, axis=0).T
    return turned[FIELD_LANE : FIELD_LANE + height]


def front_kernel(top, *refs):
    fields, grids, extra = refs[:4], refs[4:7], refs[7:9]
    sent, head, alpha, conduct, wet_out, sat, head_border, cond_border = refs[9:17]
    extra_out, (fields_in, perm, small_sems, sems) = refs[17:19], refs[19:]
    layers, width_x, width_y = head.shape
    small = [pltpu.make_async_copy(fields[i], fields_in[i], small_sems.at[i]) for i in range(4)]
    extras = [pltpu.make_async_copy(extra[i], extra_out[i], small_sems.at[4 + i]) for i in range(2)]
    parts = parts_of(layers, FRONT_CHUNK)
    large = []
    for i, (start, stop) in enumerate(parts):
        rows = pl.ds(start, stop - start)
        large.append(
            [
                pltpu.make_async_copy(source.at[rows], target.at[rows], sems.at[i, j])
                for j, (source, target) in enumerate(zip(grids, (head, alpha, perm)))
            ]
        )
    for copy in (*small, *(copy for copies in large for copy in copies), *extras):
        copy.start()
    for copy in small:
        copy.wait()
    for bank in range(fields_in[0].shape[0]):
        rows = [ref[bank : bank + 1, :].astype(jnp.float32) for ref in fields_in]
        rows.append(jnp.zeros((4, LANES), jnp.float32))
        pack_blocks(jnp.concatenate(rows, axis=0), 4, sent, bank)
    heads = jnp.zeros((width_x, width_y), jnp.float32)
    conds = jnp.zeros((width_x, width_y), jnp.float32)
    for copies, (start, stop) in zip(large, parts):
        for copy in copies:
            copy.wait()
        part = slice(start, stop)
        wet = saturation(head[part], alpha[part])
        conduct[part] = perm[part] * wet * wet * wet
        wet_out[part] = wet
        if start < top:
            last = min(stop, top)
            kept = wet[: last - start].reshape((last - start) * width_x, width_y)
            sat[start * width_x : last * width_x, :] = kept.astype(jnp.bfloat16)
        heads = border_of(head, start, stop, heads)
        conds = border_of(conduct, start, stop, conds)
    head_border[...] = heads
    cond_border[...] = conds
    add_border(sent, heads)
    for copy in extras:
        copy.wait()


def edge_kernel(axes_x, head, conduct, order, x_first, x_second):
    layers, width_x, width_y = head.shape
    even = place_of(axes_x) % 2 == 0
    for field, ref in enumerate((head, conduct)):
        rows = slice(field * layers, (field + 1) * layers)
        low, high = ref[:, 0, :], ref[:, width_x - 1, :]
        x_first[rows, :] = jnp.where(even, high, low)
        x_second[rows, :] = jnp.where(even, low, high)


def hot(ids, size):
    return iota((size, LANES), 0) == ids


def pick_kernel(top, width_x, got, sat, border, back, patch_sat, fields):
    width_y = sat.shape[1]
    for bank in range(fields.shape[0]):
        rows = unpack_blocks(got, 4, bank, 8)
        fields[bank] = rows
        ids = rows[0:1].astype(jnp.int32)
        lane_hot = hot(lax.rem(ids, width_y), width_y).astype(jnp.float32).astype(jnp.bfloat16)
        row_hot = hot(lax.div(ids, width_y), width_x)
        picked = jnp.dot(sat[...], lane_hot, preferred_element_type=jnp.float32)
        patch_sat[bank] = jnp.zeros(patch_sat.shape[1:], jnp.float32)
        for k in range(top):
            one = picked[k * width_x : (k + 1) * width_x]
            patch_sat[bank, k : k + 1, :] = jnp.sum(
                jnp.where(row_hot, one, 0.0), axis=0, keepdims=True
            )
        pack_blocks(patch_sat[bank], top, back, bank)
    add_border(back, border[...])


def column_sources(top, width_x, width_y, fields, patch_sat, root_decay):
    total = jnp.zeros((top * width_x, width_y), jnp.float32)
    table = root_decay[...]
    for h in range(fields.shape[0]):
        ids, crop, weight, rain = (fields[h, i : i + 1, :] for i in range(4))
        ids = ids.astype(jnp.int32)
        crop = crop.astype(jnp.int32)
        decay = jnp.zeros((1, LANES), jnp.float32)
        for kind in range(table.shape[1]):
            decay = jnp.where(crop == kind, table[:, kind : kind + 1], decay)
        level = iota((top, LANES), 0)
        profile = jnp.exp(-(level.astype(jnp.float32) + 0.5) * decay)
        profile = profile / jnp.sum(profile, axis=0, keepdims=True)
        sat = patch_sat[h][:top]
        inflow = jnp.where(level == 0, rain * (1.0 - sat), 0.0)
        sources = inflow - weight * profile * sat
        lane_hot = hot(lax.rem(ids, width_y), width_y).astype(jnp.float32)
        row_hot = hot(lax.div(ids, width_y), width_x)
        spread = jnp.concatenate(
            [jnp.where(row_hot, sources[k : k + 1], 0.0) for k in range(top)], axis=0
        )
        total = total + lax.dot_general(
            spread,
            lane_hot,
            (((1,), (1,)), ((), ())),
            precision=lax.Precision.HIGHEST,
            preferred_element_type=jnp.float32,
        )
    return total


def interior_kernel(top, *refs):
    head_old, porosity, head, alpha, conduct, wet = refs[:6]
    fields, patch_sat, root_decay, land, order, out = refs[6:]
    layers, width_x, width_y = head.shape
    sources = column_sources(top, width_x, width_y, fields, patch_sat, root_decay)
    sources = sources.reshape(top, width_x, width_y) * land[...].astype(jnp.float32)[None]
    for start, stop in parts_of(layers):
        shape = (stop - start, width_x, width_y)
        part, cond = head[start:stop], conduct[start:stop]
        row, lane = iota(shape, 1), iota(shape, 2)
        wet_old = saturation(head_old[start:stop], alpha[start:stop])
        total = porosity[start:stop] * (wet[start:stop] - wet_old)
        for axis, place, size in ((1, row, width_x), (2, lane, width_y)):
            face = (
                0.5
                * (cond + pltpu.roll(cond, size - 1, axis))
                * (part - pltpu.roll(part, size - 1, axis))
            )
            face = jnp.where(place == size - 1, 0.0, face)
            total = total + (face - pltpu.roll(face, 1, axis))
        below = min(layers, stop + 1)
        part, cond = head[max(0, start - 1) : below], conduct[max(0, start - 1) : below]
        down = 0.5 * (cond[:-1] + cond[1:]) * (part[:-1] - part[1:] + 1.0)
        if start == 0:
            down = jnp.concatenate([jnp.zeros_like(cond[:1]), down], 0)
        if stop == layers:
            down = jnp.concatenate([down, cond[-1:]], 0)
        total = total + (down[1:] - down[:-1])
        if start < top:
            last = min(stop, top)
            own = total[: last - start] - sources[start:last]
            total = jnp.concatenate([own, total[last - start :]], 0) if last < stop else own
        out[start:stop] = total


def last_kernel(axes_x, *refs):
    back, got, y_heads, y_conds, partial, nitrate = refs[:6]
    x_sent, x_got = refs[6:8], refs[8:10]
    residual, nitrate_out, out, value_out, x_faces, sems = refs[10:]
    layers, width_x, width_y = partial.shape
    top = nitrate.shape[0]
    even = place_of(axes_x) % 2 == 0
    faces = []
    for rows in (slice(0, layers), slice(layers, 2 * layers)):
        first, second = (r[rows, :] for r in x_sent)
        low, high = jnp.where(even, second, first), jnp.where(even, first, second)
        first, second = (r[rows, :] for r in x_got)
        before, after = jnp.where(even, second, first), jnp.where(even, first, second)
        faces.append((low, high, before, after))
    heads, conds = faces
    x_faces[0] = 0.5 * (conds[0] + conds[2]) * (heads[0] - heads[2])
    x_faces[1] = 0.5 * (conds[1] + conds[3]) * (heads[1] - heads[3])
    flux = 0.5 * (y_conds[...] + neighbour_borders(back)) * (y_heads[...] - neighbour_borders(got))
    row, lane = iota(flux.shape, 0), iota(flux.shape, 1)
    on_border = (lane == 0) | (lane == width_y - 1)
    parts = parts_of(layers, 2 * CHUNK)
    writes = []
    for i, (start, stop) in enumerate(parts):
        for k in range(start, stop):
            edge = pltpu.roll(flux, width_y - 1 - 2 * k, 1)
            one = partial[k] + jnp.where(on_border, edge, 0.0)
            one = one + jnp.where(row == 0, x_faces[0, k : k + 1, :], 0.0)
            one = one + jnp.where(row == width_x - 1, x_faces[1, k : k + 1, :], 0.0)
            out[k] = one
        rows = pl.ds(start, stop - start)
        copy = pltpu.make_async_copy(out.at[rows], residual.at[rows], sems.at[i])
        copy.start()
        writes.append(copy)
    for bank in range(nitrate.shape[1] // LANES):
        sat = unpack_blocks(back, top, bank, 16)[:top]
        lanes = slice(bank * LANES, (bank + 1) * LANES)
        loss = 0.3 * sat * sat
        value = nitrate[:, lanes]
        for _ in range(NSUB):
            upper = jnp.concatenate([value[:1], value[:-1]], 0)
            lower = jnp.concatenate([value[1:], value[-1:]], 0)
            value = value + 0.2 * (upper + lower - 2.0 * value) - loss * value
        value_out[:, lanes] = value
    copy = pltpu.make_async_copy(value_out, nitrate_out, sems.at[len(parts)])
    copy.start()
    writes.append(copy)
    for copy in writes:
        copy.wait()


def swap_pairs(size, first):
    pairs = []
    for i in range(first, size - 1, 2):
        pairs += [(i, i + 1), (i + 1, i)]
    return pairs


def call(body, name, ins, outs, scratch=(), cost=1000):
    space = {"V": pltpu.VMEM, "S": pltpu.SMEM, "H": pltpu.HBM}
    kernel = pl.pallas_call(
        body,
        out_shape=tuple(shape for shape, _ in outs),
        in_specs=[pl.BlockSpec(memory_space=space[i]) for i in ins],
        out_specs=tuple(pl.BlockSpec(memory_space=space[i]) for _, i in outs),
        scratch_shapes=scratch,
        name=name,
        compiler_params=pltpu.CompilerParams(vmem_limit_bytes=VMEM_LIMIT),
        cost_estimate=pl.CostEstimate(flops=cost, bytes_accessed=cost, transcendentals=0),
    )

    def run(*args):
        return kernel(
            *(
                pltpu.with_memory_space_constraint(arg, pltpu.HBM) if i == "H" else arg
                for i, arg in zip(ins, args)
            )
        )

    return run


def per_device(
    pressure,
    pressure_old,
    conductivity,
    vg_alpha,
    porosity,
    land_mask,
    nitrate,
    patch_column,
    crop_type,
    patch_weight,
    rain,
    root_decay,
):
    layers, width_x, width_y = pressure.shape
    top, slots = nitrate.shape
    group, axes_x = ("gx", "gy"), ("sec", "gx")
    owners = lax.axis_size(group)
    per_block = slots // owners
    if LANES % per_block or slots % LANES or per_block != width_x:
        raise ValueError("block size")
    if width_y != LANES or width_x != 16 or 2 * layers > FIELD_LANE or FIELD_LANE + 2 * top > LANES:
        raise ValueError("grid size")
    half = width_x // 2
    banks = slots // LANES
    f32 = jnp.float32
    shape, dma = jax.ShapeDtypeStruct, pltpu.SemaphoreType.DMA
    field = shape((layers, width_x, width_y), f32)
    field_in = pltpu.VMEM((layers, width_x, width_y), f32)
    count, halves = len(parts_of(layers)), len(parts_of(layers, 2 * CHUNK))
    blocks = shape((owners, half, LANES), f32)
    border = shape((width_x, width_y), f32)

    flat = [v.reshape(banks, LANES) for v in (patch_column, crop_type, patch_weight, rain)]
    x_edge = shape((2 * layers, width_y), f32)
    sent, head, alpha, conduct, wet, sat, head_border, cond_border, land, table = call(
        functools.partial(front_kernel, top),
        "front",
        "HHHHHHHHH",
        (
            (blocks, "V"),
            (field, "V"),
            (field, "V"),
            (field, "V"),
            (field, "V"),
            (shape((top * width_x, width_y), jnp.bfloat16), "V"),
            (border, "V"),
            (border, "V"),
            (shape((width_x, width_y), land_mask.dtype), "V"),
            (shape((1, root_decay.shape[0]), f32), "V"),
        ),
        (
            [pltpu.VMEM((banks, LANES), v.dtype) for v in flat],
            field_in,
            dma((6,)),
            dma((len(parts_of(layers, FRONT_CHUNK)), 3)),
        ),
    )(*flat, pressure, vg_alpha, conductivity, land_mask, root_decay.reshape(1, -1))
    got = lax.all_to_all(sent, group, split_axis=0, concat_axis=0, tiled=True)
    back, patch_sat, fields = call(
        functools.partial(pick_kernel, top, width_x),
        "pick",
        "VVV",
        (
            (blocks, "V"),
            (shape((banks, 16, LANES), f32), "V"),
            (shape((banks, 8, LANES), f32), "V"),
        ),
    )(got, sat, cond_border)
    back = lax.all_to_all(back, group, split_axis=0, concat_axis=0, tiled=True)

    x_sent = call(
        functools.partial(edge_kernel, axes_x), "edge", "VVV", ((x_edge, "V"), (x_edge, "V"))
    )(head, conduct, patch_sat)
    x_size = lax.axis_size(axes_x)
    x_got = [lax.ppermute(x_sent[i], axes_x, swap_pairs(x_size, i)) for i in (0, 1)]
    (partial,) = call(
        functools.partial(interior_kernel, top), "interior", "VVVVVVVVVVV", ((field, "V"),)
    )(
        pressure_old, porosity, head, alpha, conduct, wet, fields, patch_sat, table, land,
        x_sent[0],
    )

    residual, nitrate_out = call(
        functools.partial(last_kernel, axes_x),
        "last",
        "VVVVVVVVVV",
        ((field, "H"), (shape((top, slots), f32), "H")),
        (
            field_in,
            pltpu.VMEM((top, slots), f32),
            pltpu.VMEM((2, layers, width_y), f32),
            dma((halves + 1,)),
        ),
    )(
        back, got, head_border, cond_border, partial, nitrate, *x_sent, *x_got,
    )
    return (residual, nitrate_out)


def solution(mesh):
    placed = (
        P(None, ("sec", "gx"), "gy"),
        P(None, ("sec", "gx"), "gy"),
        P(None, ("sec", "gx"), "gy"),
        P(None, ("sec", "gx"), "gy"),
        P(None, ("sec", "gx"), "gy"),
        P(("sec", "gx"), "gy"),
        P(None, ("sec", "gx", "gy")),
        P(("sec", "gx", "gy")),
        P(("sec", "gx", "gy")),
        P(("sec", "gx", "gy")),
        P(("sec", "gx", "gy")),
        P(),
    )
    return jax.shard_map(
        per_device,
        mesh=mesh,
        in_specs=placed,
        out_specs=(P(None, ("sec", "gx"), "gy"), P(None, ("sec", "gx", "gy"))),
        check_vma=False,
    )
```

```python
import functools

import jax
import jax.numpy as jnp
from jax import lax
from jax.experimental import pallas as pl
from jax.experimental.pallas import tpu as pltpu
from jax.sharding import PartitionSpec as P

NSUB = 4
LANES = 128
CHUNK = 10
FRONT_CHUNK = 25
FIELD_LANE = 104
VMEM_LIMIT = 24 * 1024 * 1024


def iota(shape, dim):
    return lax.broadcasted_iota(jnp.int32, shape, dim)


def place_of(axes):
    index = 0
    for axis in axes:
        index = index * lax.axis_size(axis) + lax.axis_index(axis)
    return index


def parts_of(layers, size=CHUNK):
    return [(i, min(layers, i + size)) for i in range(0, layers, size)]


def saturation(head, alpha_field):
    suction = jnp.maximum(-head, 0.0) + jnp.log1p(jnp.exp(-jnp.abs(head)))
    scaled = alpha_field * suction
    return lax.rsqrt(1.0 + scaled * scaled)


def fold_border(border, own_first):
    rows, width = border.shape
    upper, lower = border[: rows // 2], border[rows // 2 :]
    if own_first:
        upper = pltpu.roll(upper, width - 1, 1)
    else:
        lower = pltpu.roll(lower, 1, 1)
    return jnp.where(iota(upper.shape, 1) % 2 == 0, upper, lower)


def unfold_border(block, place):
    width = block.shape[1]
    moved = pltpu.roll(block, 1 if place else width - 1, 1)
    return jnp.concatenate([moved, block] if place else [block, moved], axis=0)


def add_border(blocks, border):
    y_place, y_size = place_of(("gy",)), lax.axis_size("gy")
    base = place_of(("gx", "gy"))

    @pl.when(y_place > 0)
    def _():
        blocks[base - 1] = blocks[base - 1] + fold_border(border, True)

    @pl.when(y_place < y_size - 1)
    def _():
        blocks[base + 1] = blocks[base + 1] + fold_border(border, False)


def neighbour_borders(blocks):
    y_place, y_size = place_of(("gy",)), lax.axis_size("gy")
    base = place_of(("gx", "gy"))
    before = blocks[jnp.maximum(base - 1, 0)]
    before = unfold_border(jnp.where(y_place > 0, before, 0.0), 1)
    after = blocks[jnp.minimum(base + 1, blocks.shape[0] - 1)]
    after = unfold_border(jnp.where(y_place < y_size - 1, after, 0.0), 0)
    return jnp.where(iota(after.shape, 1) % 2 == 0, after, before)


def border_of(ref, start, stop, border):
    lane = iota(border.shape, 1)
    for k in range(start, stop):
        moved = pltpu.roll(ref[k], (2 * k + 1) % LANES, 1)
        border = jnp.where(lane // 2 == k, moved, border)
    return border


def pack_blocks(rows, count, blocks, bank):
    height, size = blocks.shape[1], LANES // (2 * blocks.shape[1])
    above = jnp.zeros((FIELD_LANE, LANES), jnp.float32)
    below = jnp.zeros((LANES - FIELD_LANE - rows.shape[0], LANES), jnp.float32)
    turned = jnp.concatenate([above, rows, below], axis=0).T
    for b in range(size):
        upper = turned[2 * b * height : (2 * b + 1) * height]
        lower = turned[(2 * b + 1) * height : (2 * b + 2) * height]
        blocks[bank * size + b] = upper + pltpu.roll(lower, count, 1)


def unpack_blocks(blocks, count, bank, height):
    rows, size = blocks.shape[1], LANES // (2 * blocks.shape[1])
    pieces = []
    for b in range(size):
        block = blocks[bank * size + b]
        pieces += [block, pltpu.roll(block, LANES - count, 1)]
    turned = jnp.concatenate(pieces, axis=0).T
    return turned[FIELD_LANE : FIELD_LANE + height]


def front_kernel(*refs):
    fields, grid, extra = refs[:4], refs[4], refs[5:7]
    sent, head, head_border, *extra_out = refs[7:12]
    fields_in, small_sems, sems = refs[12:]
    layers, width_x, width_y = head.shape
    small = [pltpu.make_async_copy(fields[i], fields_in[i], small_sems.at[i]) for i in range(4)]
    extras = [pltpu.make_async_copy(extra[i], extra_out[i], small_sems.at[4 + i]) for i in range(2)]
    parts = parts_of(layers, FRONT_CHUNK)
    large = []
    for i, (start, stop) in enumerate(parts):
        rows = pl.ds(start, stop - start)
        large.append(pltpu.make_async_copy(grid.at[rows], head.at[rows], sems.at[i]))
    for copy in (*small, *large, *extras):
        copy.start()
    for copy in small:
        copy.wait()
    for bank in range(fields_in[0].shape[0]):
        rows = [ref[bank : bank + 1, :].astype(jnp.float32) for ref in fields_in]
        rows.append(jnp.zeros((4, LANES), jnp.float32))
        pack_blocks(jnp.concatenate(rows, axis=0), 4, sent, bank)
    heads = jnp.zeros((width_x, width_y), jnp.float32)
    for copy, (start, stop) in zip(large, parts):
        copy.wait()
        heads = border_of(head, start, stop, heads)
    head_border[...] = heads
    add_border(sent, heads)
    for copy in extras:
        copy.wait()


def edge_kernel(axes_x, head, alpha, perm, order, x_first, x_second, conduct, wet_out):
    layers, width_x, width_y = head.shape
    for start, stop in parts_of(layers):
        part = slice(start, stop)
        wet = saturation(head[part], alpha[part])
        conduct[part] = perm[part] * wet * wet * wet
        wet_out[part] = wet
    even = place_of(axes_x) % 2 == 0
    for field, ref in enumerate((head, conduct)):
        rows = slice(field * layers, (field + 1) * layers)
        low, high = ref[:, 0, :], ref[:, width_x - 1, :]
        x_first[rows, :] = jnp.where(even, high, low)
        x_second[rows, :] = jnp.where(even, low, high)


def hot(ids, size):
    return iota((size, LANES), 0) == ids


def pick_kernel(top, got, head, alpha, perm, head_border, back, patch_sat, fields, cond_border):
    layers, width_x, width_y = head.shape
    sat = saturation(head[:top], alpha[:top]).reshape(top * width_x, width_y).astype(jnp.bfloat16)
    zero = jnp.zeros((width_x, width_y), jnp.float32)
    wet = saturation(head_border[...], border_of(alpha, 0, layers, zero))
    border = border_of(perm, 0, layers, zero) * wet * wet * wet
    cond_border[...] = border
    for bank in range(fields.shape[0]):
        rows = unpack_blocks(got, 4, bank, 8)
        fields[bank] = rows
        ids = rows[0:1].astype(jnp.int32)
        lane_hot = hot(lax.rem(ids, width_y), width_y).astype(jnp.float32).astype(jnp.bfloat16)
        row_hot = hot(lax.div(ids, width_y), width_x)
        picked = jnp.dot(sat, lane_hot, preferred_element_type=jnp.float32)
        patch_sat[bank] = jnp.zeros(patch_sat.shape[1:], jnp.float32)
        for k in range(top):
            one = picked[k * width_x : (k + 1) * width_x]
            patch_sat[bank, k : k + 1, :] = jnp.sum(
                jnp.where(row_hot, one, 0.0), axis=0, keepdims=True
            )
        pack_blocks(patch_sat[bank], top, back, bank)
    add_border(back, border)


def column_sources(top, width_x, width_y, fields, patch_sat, root_decay):
    total = jnp.zeros((top * width_x, width_y), jnp.float32)
    table = root_decay[...]
    for h in range(fields.shape[0]):
        ids, crop, weight, rain = (fields[h, i : i + 1, :] for i in range(4))
        ids = ids.astype(jnp.int32)
        crop = crop.astype(jnp.int32)
        decay = jnp.zeros((1, LANES), jnp.float32)
        for kind in range(table.shape[1]):
            decay = jnp.where(crop == kind, table[:, kind : kind + 1], decay)
        level = iota((top, LANES), 0)
        profile = jnp.exp(-(level.astype(jnp.float32) + 0.5) * decay)
        profile = profile / jnp.sum(profile, axis=0, keepdims=True)
        sat = patch_sat[h][:top]
        inflow = jnp.where(level == 0, rain * (1.0 - sat), 0.0)
        sources = inflow - weight * profile * sat
        lane_hot = hot(lax.rem(ids, width_y), width_y).astype(jnp.float32)
        row_hot = hot(lax.div(ids, width_y), width_x)
        spread = jnp.concatenate(
            [jnp.where(row_hot, sources[k : k + 1], 0.0) for k in range(top)], axis=0
        )
        total = total + lax.dot_general(
            spread,
            lane_hot,
            (((1,), (1,)), ((), ())),
            precision=lax.Precision.HIGHEST,
            preferred_element_type=jnp.float32,
        )
    return total


def interior_kernel(top, *refs):
    head_old, porosity, head, alpha, conduct, wet = refs[:6]
    fields, patch_sat, root_decay, land, order, out = refs[6:]
    layers, width_x, width_y = head.shape
    sources = column_sources(top, width_x, width_y, fields, patch_sat, root_decay)
    sources = sources.reshape(top, width_x, width_y) * land[...].astype(jnp.float32)[None]
    for start, stop in parts_of(layers):
        shape = (stop - start, width_x, width_y)
        part, cond = head[start:stop], conduct[start:stop]
        row, lane = iota(shape, 1), iota(shape, 2)
        wet_old = saturation(head_old[start:stop], alpha[start:stop])
        total = porosity[start:stop] * (wet[start:stop] - wet_old)
        for axis, place, size in ((1, row, width_x), (2, lane, width_y)):
            face = (
                0.5
                * (cond + pltpu.roll(cond, size - 1, axis))
                * (part - pltpu.roll(part, size - 1, axis))
            )
            face = jnp.where(place == size - 1, 0.0, face)
            total = total + (face - pltpu.roll(face, 1, axis))
        below = min(layers, stop + 1)
        part, cond = head[max(0, start - 1) : below], conduct[max(0, start - 1) : below]
        down = 0.5 * (cond[:-1] + cond[1:]) * (part[:-1] - part[1:] + 1.0)
        if start == 0:
            down = jnp.concatenate([jnp.zeros_like(cond[:1]), down], 0)
        if stop == layers:
            down = jnp.concatenate([down, cond[-1:]], 0)
        total = total + (down[1:] - down[:-1])
        if start < top:
            last = min(stop, top)
            own = total[: last - start] - sources[start:last]
            total = jnp.concatenate([own, total[last - start :]], 0) if last < stop else own
        out[start:stop] = total


def last_kernel(axes_x, *refs):
    back, got, y_heads, y_conds, partial, nitrate = refs[:6]
    x_sent, x_got = refs[6:8], refs[8:10]
    residual, nitrate_out, out, value_out, x_faces, sems = refs[10:]
    layers, width_x, width_y = partial.shape
    top = nitrate.shape[0]
    even = place_of(axes_x) % 2 == 0
    faces = []
    for rows in (slice(0, layers), slice(layers, 2 * layers)):
        first, second = (r[rows, :] for r in x_sent)
        low, high = jnp.where(even, second, first), jnp.where(even, first, second)
        first, second = (r[rows, :] for r in x_got)
        before, after = jnp.where(even, second, first), jnp.where(even, first, second)
        faces.append((low, high, before, after))
    heads, conds = faces
    x_faces[0] = 0.5 * (conds[0] + conds[2]) * (heads[0] - heads[2])
    x_faces[1] = 0.5 * (conds[1] + conds[3]) * (heads[1] - heads[3])
    flux = 0.5 * (y_conds[...] + neighbour_borders(back)) * (y_heads[...] - neighbour_borders(got))
    row, lane = iota(flux.shape, 0), iota(flux.shape, 1)
    on_border = (lane == 0) | (lane == width_y - 1)
    parts = parts_of(layers, 2 * CHUNK)
    writes = []
    for i, (start, stop) in enumerate(parts):
        for k in range(start, stop):
            edge = pltpu.roll(flux, width_y - 1 - 2 * k, 1)
            one = partial[k] + jnp.where(on_border, edge, 0.0)
            one = one + jnp.where(row == 0, x_faces[0, k : k + 1, :], 0.0)
            one = one + jnp.where(row == width_x - 1, x_faces[1, k : k + 1, :], 0.0)
            out[k] = one
        rows = pl.ds(start, stop - start)
        copy = pltpu.make_async_copy(out.at[rows], residual.at[rows], sems.at[i])
        copy.start()
        writes.append(copy)
    for bank in range(nitrate.shape[1] // LANES):
        sat = unpack_blocks(back, top, bank, 16)[:top]
        lanes = slice(bank * LANES, (bank + 1) * LANES)
        loss = 0.3 * sat * sat
        value = nitrate[:, lanes]
        for _ in range(NSUB):
            upper = jnp.concatenate([value[:1], value[:-1]], 0)
            lower = jnp.concatenate([value[1:], value[-1:]], 0)
            value = value + 0.2 * (upper + lower - 2.0 * value) - loss * value
        value_out[:, lanes] = value
    copy = pltpu.make_async_copy(value_out, nitrate_out, sems.at[len(parts)])
    copy.start()
    writes.append(copy)
    for copy in writes:
        copy.wait()


def swap_pairs(size, first):
    pairs = []
    for i in range(first, size - 1, 2):
        pairs += [(i, i + 1), (i + 1, i)]
    return pairs


def call(body, name, ins, outs, scratch=(), cost=1000):
    space = {"V": pltpu.VMEM, "S": pltpu.SMEM, "H": pltpu.HBM}
    kernel = pl.pallas_call(
        body,
        out_shape=tuple(shape for shape, _ in outs),
        in_specs=[pl.BlockSpec(memory_space=space[i]) for i in ins],
        out_specs=tuple(pl.BlockSpec(memory_space=space[i]) for _, i in outs),
        scratch_shapes=scratch,
        name=name,
        compiler_params=pltpu.CompilerParams(vmem_limit_bytes=VMEM_LIMIT),
        cost_estimate=pl.CostEstimate(flops=cost, bytes_accessed=cost, transcendentals=0),
    )

    def run(*args):
        return kernel(
            *(
                pltpu.with_memory_space_constraint(arg, pltpu.HBM) if i == "H" else arg
                for i, arg in zip(ins, args)
            )
        )

    return run


def per_device(
    pressure,
    pressure_old,
    conductivity,
    vg_alpha,
    porosity,
    land_mask,
    nitrate,
    patch_column,
    crop_type,
    patch_weight,
    rain,
    root_decay,
):
    layers, width_x, width_y = pressure.shape
    top, slots = nitrate.shape
    group, axes_x = ("gx", "gy"), ("sec", "gx")
    owners = lax.axis_size(group)
    per_block = slots // owners
    if LANES % per_block or slots % LANES or per_block != width_x:
        raise ValueError("block size")
    if width_y != LANES or width_x != 16 or 2 * layers > FIELD_LANE or FIELD_LANE + 2 * top > LANES:
        raise ValueError("grid size")
    half = width_x // 2
    banks = slots // LANES
    f32 = jnp.float32
    shape, dma = jax.ShapeDtypeStruct, pltpu.SemaphoreType.DMA
    field = shape((layers, width_x, width_y), f32)
    field_in = pltpu.VMEM((layers, width_x, width_y), f32)
    count, halves = len(parts_of(layers)), len(parts_of(layers, 2 * CHUNK))
    blocks = shape((owners, half, LANES), f32)
    border = shape((width_x, width_y), f32)

    flat = [v.reshape(banks, LANES) for v in (patch_column, crop_type, patch_weight, rain)]
    x_edge = shape((2 * layers, width_y), f32)
    sent, head, head_border, table, land = call(
        front_kernel,
        "front",
        "HHHHHHH",
        (
            (blocks, "V"),
            (field, "V"),
            (border, "V"),
            (shape((1, root_decay.shape[0]), f32), "V"),
            (shape((width_x, width_y), land_mask.dtype), "V"),
        ),
        (
            [pltpu.VMEM((banks, LANES), v.dtype) for v in flat],
            dma((6,)),
            dma((len(parts_of(layers, FRONT_CHUNK)),)),
        ),
        cost=1000000000,
    )(*flat, pressure, root_decay.reshape(1, -1), land_mask)
    got = lax.all_to_all(sent, group, split_axis=0, concat_axis=0, tiled=True)
    back, patch_sat, fields, cond_border = call(
        functools.partial(pick_kernel, top),
        "pick",
        "VVVVV",
        (
            (blocks, "V"),
            (shape((banks, 16, LANES), f32), "V"),
            (shape((banks, 8, LANES), f32), "V"),
            (border, "V"),
        ),
    )(got, head, vg_alpha, conductivity, head_border)
    back = lax.all_to_all(back, group, split_axis=0, concat_axis=0, tiled=True)

    *x_sent, conduct, wet = call(
        functools.partial(edge_kernel, axes_x),
        "edge",
        "VVVV",
        ((x_edge, "V"), (x_edge, "V"), (field, "V"), (field, "V")),
    )(head, vg_alpha, conductivity, patch_sat)
    x_size = lax.axis_size(axes_x)
    x_got = [lax.ppermute(x_sent[i], axes_x, swap_pairs(x_size, i)) for i in (0, 1)]
    (partial,) = call(
        functools.partial(interior_kernel, top), "interior", "VVVVVVVVVVV", ((field, "V"),)
    )(
        pressure_old, porosity, head, vg_alpha, conduct, wet, fields, patch_sat, table, land,
        x_sent[0],
    )

    residual, nitrate_out = call(
        functools.partial(last_kernel, axes_x),
        "last",
        "VVVVVVVVVV",
        ((field, "H"), (shape((top, slots), f32), "H")),
        (
            field_in,
            pltpu.VMEM((top, slots), f32),
            pltpu.VMEM((2, layers, width_y), f32),
            dma((halves + 1,)),
        ),
    )(
        back, got, head_border, cond_border, partial, nitrate, *x_sent, *x_got,
    )
    return (residual, nitrate_out)


def solution(mesh):
    placed = (
        P(None, ("sec", "gx"), "gy"),
        P(None, ("sec", "gx"), "gy"),
        P(None, ("sec", "gx"), "gy"),
        P(None, ("sec", "gx"), "gy"),
        P(None, ("sec", "gx"), "gy"),
        P(("sec", "gx"), "gy"),
        P(None, ("sec", "gx", "gy")),
        P(("sec", "gx", "gy")),
        P(("sec", "gx", "gy")),
        P(("sec", "gx", "gy")),
        P(("sec", "gx", "gy")),
        P(),
    )
    return jax.shard_map(
        per_device,
        mesh=mesh,
        in_specs=placed,
        out_specs=(P(None, ("sec", "gx"), "gy"), P(None, ("sec", "gx", "gy"))),
        check_vma=False,
    )
```

```python
import functools

import jax
import jax.numpy as jnp
from jax import lax
from jax.experimental import pallas as pl
from jax.experimental.pallas import tpu as pltpu
from jax.sharding import PartitionSpec as P

NSUB = 4
LANES = 128
CHUNK = 10
FRONT_CHUNK = 25
EXTRA_LANE, MAIN_LANE = 104, 112
VMEM_LIMIT = 24 * 1024 * 1024


def iota(shape, dim):
    return lax.broadcasted_iota(jnp.int32, shape, dim)


def place_of(axes):
    index = 0
    for axis in axes:
        index = index * lax.axis_size(axis) + lax.axis_index(axis)
    return index


def parts_of(layers, size=CHUNK):
    return [(i, min(layers, i + size)) for i in range(0, layers, size)]


def saturation(head, alpha_field):
    suction = jnp.maximum(-head, 0.0) + jnp.log1p(jnp.exp(-jnp.abs(head)))
    scaled = alpha_field * suction
    return lax.rsqrt(1.0 + scaled * scaled)


def fold_border(border, own_first):
    rows, width = border.shape
    upper, lower = border[: rows // 2], border[rows // 2 :]
    if own_first:
        upper = pltpu.roll(upper, width - 1, 1)
    else:
        lower = pltpu.roll(lower, 1, 1)
    return jnp.where(iota(upper.shape, 1) % 2 == 0, upper, lower)


def unfold_border(block, place):
    width = block.shape[1]
    moved = pltpu.roll(block, 1 if place else width - 1, 1)
    return jnp.concatenate([moved, block] if place else [block, moved], axis=0)


def add_border(blocks, border):
    y_place, y_size = place_of(("gy",)), lax.axis_size("gy")
    base = place_of(("gx", "gy"))

    @pl.when(y_place > 0)
    def _():
        blocks[base - 1] = blocks[base - 1] + fold_border(border, True)

    @pl.when(y_place < y_size - 1)
    def _():
        blocks[base + 1] = blocks[base + 1] + fold_border(border, False)


def neighbour_borders(blocks):
    y_place, y_size = place_of(("gy",)), lax.axis_size("gy")
    base = place_of(("gx", "gy"))
    before = blocks[jnp.maximum(base - 1, 0)]
    before = unfold_border(jnp.where(y_place > 0, before, 0.0), 1)
    after = blocks[jnp.minimum(base + 1, blocks.shape[0] - 1)]
    after = unfold_border(jnp.where(y_place < y_size - 1, after, 0.0), 0)
    return jnp.where(iota(after.shape, 1) % 2 == 0, after, before)


def border_of(ref, start, stop, border):
    lane = iota(border.shape, 1)
    for k in range(start, stop):
        moved = pltpu.roll(ref[k], (2 * k + 1) % LANES, 1)
        border = jnp.where(lane // 2 == k, moved, border)
    return border


def pack_blocks(rows, blocks, bank):
    width = LANES - MAIN_LANE
    size = LANES // width
    main = rows[:8]
    lane = iota((8, LANES), 1)
    pieces = []
    for i in range(8, rows.shape[0]):
        row = rows[i : i + 1]
        pieces += [row, pltpu.roll(row, LANES - width // 2, 1)]
    if pieces:
        pieces.append(jnp.zeros((8 - len(pieces), LANES), jnp.float32))
        extra = jnp.concatenate(pieces, axis=0)
    for b in range(size):
        block = jnp.where(lane >= MAIN_LANE, pltpu.roll(main, (MAIN_LANE - width * b) % LANES, 1), 0.0)
        if pieces:
            moved = pltpu.roll(extra, (EXTRA_LANE - width * b) % LANES, 1)
            block = jnp.where((lane >= EXTRA_LANE) & (lane < MAIN_LANE), moved, block)
        blocks[bank * size + b] = block


def unpack_blocks(blocks, count, bank):
    width = LANES - MAIN_LANE
    size = LANES // width
    lane = iota((8, LANES), 1)
    main = jnp.zeros((8, LANES), jnp.float32)
    extra = jnp.zeros((8, LANES), jnp.float32)
    for b in range(size):
        block = blocks[bank * size + b]
        moved = pltpu.roll(block, (width * b - MAIN_LANE) % LANES, 1)
        main = jnp.where(lane // width == b, moved, main)
        if count > 8:
            moved = pltpu.roll(block, (width * b - EXTRA_LANE) % LANES, 1)
            extra = jnp.where(lane // width == b, moved, extra)
    rows = [main]
    first = lane[:1] % width < width // 2
    for i in range(count - 8):
        second = pltpu.roll(extra[2 * i + 1 : 2 * i + 2], width // 2, 1)
        rows.append(jnp.where(first, extra[2 * i : 2 * i + 1], second))
    return jnp.concatenate(rows, axis=0) if count > 8 else main


def front_kernel(*refs):
    fields, grid, extra = refs[:4], refs[4], refs[5:7]
    sent, head, head_border, *extra_out = refs[7:12]
    fields_in, small_sems, sems = refs[12:]
    layers, width_x, width_y = head.shape
    small = [pltpu.make_async_copy(fields[i], fields_in[i], small_sems.at[i]) for i in range(4)]
    extras = [pltpu.make_async_copy(extra[i], extra_out[i], small_sems.at[4 + i]) for i in range(2)]
    parts = parts_of(layers, FRONT_CHUNK)
    large = []
    for i, (start, stop) in enumerate(parts):
        rows = pl.ds(start, stop - start)
        large.append(pltpu.make_async_copy(grid.at[rows], head.at[rows], sems.at[i]))
    for copy in (*small, *large, *extras):
        copy.start()
    for copy in small:
        copy.wait()
    for bank in range(fields_in[0].shape[0]):
        rows = [ref[bank : bank + 1, :].astype(jnp.float32) for ref in fields_in]
        rows.append(jnp.zeros((4, LANES), jnp.float32))
        pack_blocks(jnp.concatenate(rows, axis=0), sent, bank)
    heads = jnp.zeros((width_x, width_y), jnp.float32)
    for copy, (start, stop) in zip(large, parts):
        copy.wait()
        heads = border_of(head, start, stop, heads)
    head_border[...] = heads
    add_border(sent, heads)
    for copy in extras:
        copy.wait()


def edge_kernel(axes_x, head, alpha, perm, order, x_first, x_second, conduct, wet_out):
    layers, width_x, width_y = head.shape
    for start, stop in parts_of(layers):
        part = slice(start, stop)
        wet = saturation(head[part], alpha[part])
        conduct[part] = perm[part] * wet * wet * wet
        wet_out[part] = wet
    even = place_of(axes_x) % 2 == 0
    for field, ref in enumerate((head, conduct)):
        rows = slice(field * layers, (field + 1) * layers)
        low, high = ref[:, 0, :], ref[:, width_x - 1, :]
        x_first[rows, :] = jnp.where(even, high, low)
        x_second[rows, :] = jnp.where(even, low, high)


def hot(ids, size):
    return iota((size, LANES), 0) == ids


def pick_kernel(top, got, head, alpha, perm, head_border, back, patch_sat, fields, cond_border):
    layers, width_x, width_y = head.shape
    sat = saturation(head[:top], alpha[:top]).reshape(top * width_x, width_y).astype(jnp.bfloat16)
    zero = jnp.zeros((width_x, width_y), jnp.float32)
    wet = saturation(head_border[...], border_of(alpha, 0, layers, zero))
    border = border_of(perm, 0, layers, zero) * wet * wet * wet
    cond_border[...] = border
    for bank in range(fields.shape[0]):
        rows = unpack_blocks(got, 8, bank)
        fields[bank] = rows
        ids = rows[0:1].astype(jnp.int32)
        lane_hot = hot(lax.rem(ids, width_y), width_y).astype(jnp.float32).astype(jnp.bfloat16)
        row_hot = hot(lax.div(ids, width_y), width_x)
        picked = jnp.dot(sat, lane_hot, preferred_element_type=jnp.float32)
        patch_sat[bank] = jnp.zeros(patch_sat.shape[1:], jnp.float32)
        for k in range(top):
            one = picked[k * width_x : (k + 1) * width_x]
            patch_sat[bank, k : k + 1, :] = jnp.sum(
                jnp.where(row_hot, one, 0.0), axis=0, keepdims=True
            )
        pack_blocks(patch_sat[bank][:top], back, bank)
    add_border(back, border)


def column_sources(top, width_x, width_y, fields, patch_sat, root_decay):
    total = jnp.zeros((top * width_x, width_y), jnp.float32)
    table = root_decay[...]
    for h in range(fields.shape[0]):
        ids, crop, weight, rain = (fields[h, i : i + 1, :] for i in range(4))
        ids = ids.astype(jnp.int32)
        crop = crop.astype(jnp.int32)
        decay = jnp.zeros((1, LANES), jnp.float32)
        for kind in range(table.shape[1]):
            decay = jnp.where(crop == kind, table[:, kind : kind + 1], decay)
        level = iota((top, LANES), 0)
        profile = jnp.exp(-(level.astype(jnp.float32) + 0.5) * decay)
        profile = profile / jnp.sum(profile, axis=0, keepdims=True)
        sat = patch_sat[h][:top]
        inflow = jnp.where(level == 0, rain * (1.0 - sat), 0.0)
        sources = inflow - weight * profile * sat
        lane_hot = hot(lax.rem(ids, width_y), width_y).astype(jnp.float32)
        row_hot = hot(lax.div(ids, width_y), width_x)
        spread = jnp.concatenate(
            [jnp.where(row_hot, sources[k : k + 1], 0.0) for k in range(top)], axis=0
        )
        total = total + lax.dot_general(
            spread,
            lane_hot,
            (((1,), (1,)), ((), ())),
            precision=lax.Precision.HIGHEST,
            preferred_element_type=jnp.float32,
        )
    return total


def interior_kernel(top, *refs):
    head_old, porosity, head, alpha, conduct, wet = refs[:6]
    fields, patch_sat, root_decay, land, order, out = refs[6:]
    layers, width_x, width_y = head.shape
    sources = column_sources(top, width_x, width_y, fields, patch_sat, root_decay)
    sources = sources.reshape(top, width_x, width_y) * land[...].astype(jnp.float32)[None]
    for start, stop in parts_of(layers):
        shape = (stop - start, width_x, width_y)
        part, cond = head[start:stop], conduct[start:stop]
        row, lane = iota(shape, 1), iota(shape, 2)
        wet_old = saturation(head_old[start:stop], alpha[start:stop])
        total = porosity[start:stop] * (wet[start:stop] - wet_old)
        for axis, place, size in ((1, row, width_x), (2, lane, width_y)):
            face = (
                0.5
                * (cond + pltpu.roll(cond, size - 1, axis))
                * (part - pltpu.roll(part, size - 1, axis))
            )
            face = jnp.where(place == size - 1, 0.0, face)
            total = total + (face - pltpu.roll(face, 1, axis))
        below = min(layers, stop + 1)
        part, cond = head[max(0, start - 1) : below], conduct[max(0, start - 1) : below]
        down = 0.5 * (cond[:-1] + cond[1:]) * (part[:-1] - part[1:] + 1.0)
        if start == 0:
            down = jnp.concatenate([jnp.zeros_like(cond[:1]), down], 0)
        if stop == layers:
            down = jnp.concatenate([down, cond[-1:]], 0)
        total = total + (down[1:] - down[:-1])
        if start < top:
            last = min(stop, top)
            own = total[: last - start] - sources[start:last]
            total = jnp.concatenate([own, total[last - start :]], 0) if last < stop else own
        out[start:stop] = total


def last_kernel(axes_x, *refs):
    back, got, y_heads, y_conds, partial, nitrate = refs[:6]
    x_sent, x_got = refs[6:8], refs[8:10]
    residual, nitrate_out, out, value_out, x_faces, sems = refs[10:]
    layers, width_x, width_y = partial.shape
    top = nitrate.shape[0]
    even = place_of(axes_x) % 2 == 0
    faces = []
    for rows in (slice(0, layers), slice(layers, 2 * layers)):
        first, second = (r[rows, :] for r in x_sent)
        low, high = jnp.where(even, second, first), jnp.where(even, first, second)
        first, second = (r[rows, :] for r in x_got)
        before, after = jnp.where(even, second, first), jnp.where(even, first, second)
        faces.append((low, high, before, after))
    heads, conds = faces
    x_faces[0] = 0.5 * (conds[0] + conds[2]) * (heads[0] - heads[2])
    x_faces[1] = 0.5 * (conds[1] + conds[3]) * (heads[1] - heads[3])
    flux = 0.5 * (y_conds[...] + neighbour_borders(back)) * (y_heads[...] - neighbour_borders(got))
    row, lane = iota(flux.shape, 0), iota(flux.shape, 1)
    on_border = (lane == 0) | (lane == width_y - 1)
    parts = parts_of(layers, 2 * CHUNK)
    writes = []
    for i, (start, stop) in enumerate(parts):
        for k in range(start, stop):
            edge = pltpu.roll(flux, width_y - 1 - 2 * k, 1)
            one = partial[k] + jnp.where(on_border, edge, 0.0)
            one = one + jnp.where(row == 0, x_faces[0, k : k + 1, :], 0.0)
            one = one + jnp.where(row == width_x - 1, x_faces[1, k : k + 1, :], 0.0)
            out[k] = one
        rows = pl.ds(start, stop - start)
        copy = pltpu.make_async_copy(out.at[rows], residual.at[rows], sems.at[i])
        copy.start()
        writes.append(copy)
    for bank in range(nitrate.shape[1] // LANES):
        sat = unpack_blocks(back, top, bank)
        lanes = slice(bank * LANES, (bank + 1) * LANES)
        loss = 0.3 * sat * sat
        value = nitrate[:, lanes]
        for _ in range(NSUB):
            upper = jnp.concatenate([value[:1], value[:-1]], 0)
            lower = jnp.concatenate([value[1:], value[-1:]], 0)
            value = value + 0.2 * (upper + lower - 2.0 * value) - loss * value
        value_out[:, lanes] = value
    copy = pltpu.make_async_copy(value_out, nitrate_out, sems.at[len(parts)])
    copy.start()
    writes.append(copy)
    for copy in writes:
        copy.wait()


def swap_pairs(size, first):
    pairs = []
    for i in range(first, size - 1, 2):
        pairs += [(i, i + 1), (i + 1, i)]
    return pairs


def call(body, name, ins, outs, scratch=(), cost=1000):
    space = {"V": pltpu.VMEM, "S": pltpu.SMEM, "H": pltpu.HBM}
    kernel = pl.pallas_call(
        body,
        out_shape=tuple(shape for shape, _ in outs),
        in_specs=[pl.BlockSpec(memory_space=space[i]) for i in ins],
        out_specs=tuple(pl.BlockSpec(memory_space=space[i]) for _, i in outs),
        scratch_shapes=scratch,
        name=name,
        compiler_params=pltpu.CompilerParams(vmem_limit_bytes=VMEM_LIMIT),
        cost_estimate=pl.CostEstimate(flops=cost, bytes_accessed=cost, transcendentals=0),
    )

    def run(*args):
        return kernel(
            *(
                pltpu.with_memory_space_constraint(arg, pltpu.HBM) if i == "H" else arg
                for i, arg in zip(ins, args)
            )
        )

    return run


def per_device(
    pressure,
    pressure_old,
    conductivity,
    vg_alpha,
    porosity,
    land_mask,
    nitrate,
    patch_column,
    crop_type,
    patch_weight,
    rain,
    root_decay,
):
    layers, width_x, width_y = pressure.shape
    top, slots = nitrate.shape
    group, axes_x = ("gx", "gy"), ("sec", "gx")
    owners = lax.axis_size(group)
    per_block = slots // owners
    if LANES % per_block or slots % LANES or per_block != width_x:
        raise ValueError("block size")
    if width_y != LANES or width_x != LANES - MAIN_LANE or 2 * layers > EXTRA_LANE or not 8 <= top <= 11:
        raise ValueError("grid size")
    half = width_x // 2
    banks = slots // LANES
    f32 = jnp.float32
    shape, dma = jax.ShapeDtypeStruct, pltpu.SemaphoreType.DMA
    field = shape((layers, width_x, width_y), f32)
    field_in = pltpu.VMEM((layers, width_x, width_y), f32)
    count, halves = len(parts_of(layers)), len(parts_of(layers, 2 * CHUNK))
    blocks = shape((owners, half, LANES), f32)
    border = shape((width_x, width_y), f32)

    flat = [v.reshape(banks, LANES) for v in (patch_column, crop_type, patch_weight, rain)]
    x_edge = shape((2 * layers, width_y), f32)
    sent, head, head_border, table, land = call(
        front_kernel,
        "front",
        "HHHHHHH",
        (
            (blocks, "V"),
            (field, "V"),
            (border, "V"),
            (shape((1, root_decay.shape[0]), f32), "V"),
            (shape((width_x, width_y), land_mask.dtype), "V"),
        ),
        (
            [pltpu.VMEM((banks, LANES), v.dtype) for v in flat],
            dma((6,)),
            dma((len(parts_of(layers, FRONT_CHUNK)),)),
        ),
        cost=1000000000,
    )(*flat, pressure, root_decay.reshape(1, -1), land_mask)
    got = lax.all_to_all(sent, group, split_axis=0, concat_axis=0, tiled=True)
    back, patch_sat, fields, cond_border = call(
        functools.partial(pick_kernel, top),
        "pick",
        "VVVVV",
        (
            (blocks, "V"),
            (shape((banks, 16, LANES), f32), "V"),
            (shape((banks, 8, LANES), f32), "V"),
            (border, "V"),
        ),
    )(got, head, vg_alpha, conductivity, head_border)
    back = lax.all_to_all(back, group, split_axis=0, concat_axis=0, tiled=True)

    *x_sent, conduct, wet = call(
        functools.partial(edge_kernel, axes_x),
        "edge",
        "VVVV",
        ((x_edge, "V"), (x_edge, "V"), (field, "V"), (field, "V")),
    )(head, vg_alpha, conductivity, patch_sat)
    x_size = lax.axis_size(axes_x)
    x_got = [lax.ppermute(x_sent[i], axes_x, swap_pairs(x_size, i)) for i in (0, 1)]
    (partial,) = call(
        functools.partial(interior_kernel, top), "interior", "VVVVVVVVVVV", ((field, "V"),)
    )(
        pressure_old, porosity, head, vg_alpha, conduct, wet, fields, patch_sat, table, land,
        x_sent[0],
    )

    residual, nitrate_out = call(
        functools.partial(last_kernel, axes_x),
        "last",
        "VVVVVVVVVV",
        ((field, "H"), (shape((top, slots), f32), "H")),
        (
            field_in,
            pltpu.VMEM((top, slots), f32),
            pltpu.VMEM((2, layers, width_y), f32),
            dma((halves + 1,)),
        ),
    )(
        back, got, head_border, cond_border, partial, nitrate, *x_sent, *x_got,
    )
    return (residual, nitrate_out)


def solution(mesh):
    placed = (
        P(None, ("sec", "gx"), "gy"),
        P(None, ("sec", "gx"), "gy"),
        P(None, ("sec", "gx"), "gy"),
        P(None, ("sec", "gx"), "gy"),
        P(None, ("sec", "gx"), "gy"),
        P(("sec", "gx"), "gy"),
        P(None, ("sec", "gx", "gy")),
        P(("sec", "gx", "gy")),
        P(("sec", "gx", "gy")),
        P(("sec", "gx", "gy")),
        P(("sec", "gx", "gy")),
        P(),
    )
    return jax.shard_map(
        per_device,
        mesh=mesh,
        in_specs=placed,
        out_specs=(P(None, ("sec", "gx"), "gy"), P(None, ("sec", "gx", "gy"))),
        check_vma=False,
    )
```

```python
import functools

import jax
import jax.numpy as jnp
from jax import lax
from jax.experimental import pallas as pl
from jax.experimental.pallas import tpu as pltpu
from jax.sharding import PartitionSpec as P

NSUB = 4
LANES = 128
CHUNK = 10
FRONT_CHUNK = 25
EXTRA_LANE, MAIN_LANE = 104, 112
VMEM_LIMIT = 24 * 1024 * 1024


def iota(shape, dim):
    return lax.broadcasted_iota(jnp.int32, shape, dim)


def place_of(axes):
    index = 0
    for axis in axes:
        index = index * lax.axis_size(axis) + lax.axis_index(axis)
    return index


def parts_of(layers, size=CHUNK):
    return [(i, min(layers, i + size)) for i in range(0, layers, size)]


def saturation(head, alpha_field):
    suction = jnp.maximum(-head, 0.0) + jnp.log1p(jnp.exp(-jnp.abs(head)))
    scaled = alpha_field * suction
    return lax.rsqrt(1.0 + scaled * scaled)


def fold_border(border, own_first):
    rows, width = border.shape
    upper, lower = border[: rows // 2], border[rows // 2 :]
    if own_first:
        upper = pltpu.roll(upper, width - 1, 1)
    else:
        lower = pltpu.roll(lower, 1, 1)
    return jnp.where(iota(upper.shape, 1) % 2 == 0, upper, lower)


def unfold_border(block, place):
    width = block.shape[1]
    moved = pltpu.roll(block, 1 if place else width - 1, 1)
    return jnp.concatenate([moved, block] if place else [block, moved], axis=0)


def add_border(blocks, border):
    y_place, y_size = place_of(("gy",)), lax.axis_size("gy")
    base = place_of(("gx", "gy"))

    @pl.when(y_place > 0)
    def _():
        blocks[base - 1] = blocks[base - 1] + fold_border(border, True)

    @pl.when(y_place < y_size - 1)
    def _():
        blocks[base + 1] = blocks[base + 1] + fold_border(border, False)


def neighbour_borders(blocks):
    y_place, y_size = place_of(("gy",)), lax.axis_size("gy")
    base = place_of(("gx", "gy"))
    before = blocks[jnp.maximum(base - 1, 0)]
    before = unfold_border(jnp.where(y_place > 0, before, 0.0), 1)
    after = blocks[jnp.minimum(base + 1, blocks.shape[0] - 1)]
    after = unfold_border(jnp.where(y_place < y_size - 1, after, 0.0), 0)
    return jnp.where(iota(after.shape, 1) % 2 == 0, after, before)


def border_of(ref, start, stop, border):
    lane = iota(border.shape, 1)
    for k in range(start, stop):
        moved = pltpu.roll(ref[k], (2 * k + 1) % LANES, 1)
        border = jnp.where(lane // 2 == k, moved, border)
    return border


def pack_blocks(rows, blocks, bank):
    width = LANES - MAIN_LANE
    size = LANES // width
    main = rows[:8]
    lane = iota((8, LANES), 1)
    pieces = []
    for i in range(8, rows.shape[0]):
        row = rows[i : i + 1]
        pieces += [row, pltpu.roll(row, LANES - width // 2, 1)]
    if pieces:
        pieces.append(jnp.zeros((8 - len(pieces), LANES), jnp.float32))
        extra = jnp.concatenate(pieces, axis=0)
    for b in range(size):
        block = jnp.where(lane >= MAIN_LANE, pltpu.roll(main, (MAIN_LANE - width * b) % LANES, 1), 0.0)
        if pieces:
            moved = pltpu.roll(extra, (EXTRA_LANE - width * b) % LANES, 1)
            block = jnp.where((lane >= EXTRA_LANE) & (lane < MAIN_LANE), moved, block)
        blocks[bank * size + b] = block


def unpack_blocks(blocks, count, bank):
    width = LANES - MAIN_LANE
    size = LANES // width
    lane = iota((8, LANES), 1)
    main = jnp.zeros((8, LANES), jnp.float32)
    extra = jnp.zeros((8, LANES), jnp.float32)
    for b in range(size):
        block = blocks[bank * size + b]
        moved = pltpu.roll(block, (width * b - MAIN_LANE) % LANES, 1)
        main = jnp.where(lane // width == b, moved, main)
        if count > 8:
            moved = pltpu.roll(block, (width * b - EXTRA_LANE) % LANES, 1)
            extra = jnp.where(lane // width == b, moved, extra)
    rows = [main]
    first = lane[:1] % width < width // 2
    for i in range(count - 8):
        second = pltpu.roll(extra[2 * i + 1 : 2 * i + 2], width // 2, 1)
        rows.append(jnp.where(first, extra[2 * i : 2 * i + 1], second))
    return jnp.concatenate(rows, axis=0) if count > 8 else main


def front_kernel(*refs):
    fields, grid, extra = refs[:4], refs[4], refs[5:7]
    sent, head, head_border, *extra_out = refs[7:12]
    fields_in, small_sems, sems = refs[12:]
    layers, width_x, width_y = head.shape
    small = [pltpu.make_async_copy(fields[i], fields_in[i], small_sems.at[i]) for i in range(4)]
    extras = [pltpu.make_async_copy(extra[i], extra_out[i], small_sems.at[4 + i]) for i in range(2)]
    parts = parts_of(layers, FRONT_CHUNK)
    large = []
    for i, (start, stop) in enumerate(parts):
        rows = pl.ds(start, stop - start)
        large.append(pltpu.make_async_copy(grid.at[rows], head.at[rows], sems.at[i]))
    for copy in (*small, *large, *extras):
        copy.start()
    for copy in small:
        copy.wait()
    for bank in range(fields_in[0].shape[0]):
        rows = [ref[bank : bank + 1, :].astype(jnp.float32) for ref in fields_in]
        rows.append(jnp.zeros((4, LANES), jnp.float32))
        pack_blocks(jnp.concatenate(rows, axis=0), sent, bank)
    heads = jnp.zeros((width_x, width_y), jnp.float32)
    for copy, (start, stop) in zip(large, parts):
        copy.wait()
        heads = border_of(head, start, stop, heads)
    head_border[...] = heads
    add_border(sent, heads)
    for copy in extras:
        copy.wait()


def edge_kernel(axes_x, head, alpha, perm, order, x_first, x_second, conduct, wet_out):
    layers, width_x, width_y = head.shape
    for start, stop in parts_of(layers):
        part = slice(start, stop)
        wet = saturation(head[part], alpha[part])
        conduct[part] = perm[part] * wet * wet * wet
        wet_out[part] = wet
    even = place_of(axes_x) % 2 == 0
    for field, ref in enumerate((head, conduct)):
        rows = slice(field * layers, (field + 1) * layers)
        low, high = ref[:, 0, :], ref[:, width_x - 1, :]
        x_first[rows, :] = jnp.where(even, high, low)
        x_second[rows, :] = jnp.where(even, low, high)


def hot(ids, size):
    return iota((size, LANES), 0) == ids


def pick_kernel(top, got, head, alpha, perm, head_border, back, patch_sat, fields, cond_border):
    layers, width_x, width_y = head.shape
    sat = saturation(head[:top], alpha[:top]).reshape(top * width_x, width_y).astype(jnp.bfloat16)
    zero = jnp.zeros((width_x, width_y), jnp.float32)
    wet = saturation(head_border[...], border_of(alpha, 0, layers, zero))
    border = border_of(perm, 0, layers, zero) * wet * wet * wet
    cond_border[...] = border
    for bank in range(fields.shape[0]):
        rows = unpack_blocks(got, 8, bank)
        fields[bank] = rows
        ids = rows[0:1].astype(jnp.int32)
        lane_hot = hot(lax.rem(ids, width_y), width_y).astype(jnp.float32).astype(jnp.bfloat16)
        row_hot = hot(lax.div(ids, width_y), width_x)
        picked = jnp.dot(sat, lane_hot, preferred_element_type=jnp.float32)
        patch_sat[bank] = jnp.zeros(patch_sat.shape[1:], jnp.float32)
        for k in range(top):
            one = picked[k * width_x : (k + 1) * width_x]
            patch_sat[bank, k : k + 1, :] = jnp.sum(
                jnp.where(row_hot, one, 0.0), axis=0, keepdims=True
            )
        pack_blocks(patch_sat[bank][:top], back, bank)
    add_border(back, border)


def column_sources(top, width_x, width_y, fields, patch_sat, root_decay):
    total = jnp.zeros((top * width_x, width_y), jnp.float32)
    table = root_decay[...]
    for h in range(fields.shape[0]):
        ids, crop, weight, rain = (fields[h, i : i + 1, :] for i in range(4))
        ids = ids.astype(jnp.int32)
        crop = crop.astype(jnp.int32)
        decay = jnp.zeros((1, LANES), jnp.float32)
        for kind in range(table.shape[1]):
            decay = jnp.where(crop == kind, table[:, kind : kind + 1], decay)
        level = iota((top, LANES), 0)
        profile = jnp.exp(-(level.astype(jnp.float32) + 0.5) * decay)
        profile = profile / jnp.sum(profile, axis=0, keepdims=True)
        sat = patch_sat[h][:top]
        inflow = jnp.where(level == 0, rain * (1.0 - sat), 0.0)
        sources = inflow - weight * profile * sat
        lane_hot = hot(lax.rem(ids, width_y), width_y).astype(jnp.float32)
        row_hot = hot(lax.div(ids, width_y), width_x)
        spread = jnp.concatenate(
            [jnp.where(row_hot, sources[k : k + 1], 0.0) for k in range(top)], axis=0
        )
        total = total + lax.dot_general(
            spread,
            lane_hot,
            (((1,), (1,)), ((), ())),
            precision=lax.Precision.HIGHEST,
            preferred_element_type=jnp.float32,
        )
    return total


def interior_kernel(top, *refs):
    head_old, porosity, head, alpha, conduct, wet = refs[:6]
    fields, patch_sat, root_decay, land, order, out = refs[6:]
    layers, width_x, width_y = head.shape
    sources = column_sources(top, width_x, width_y, fields, patch_sat, root_decay)
    sources = sources.reshape(top, width_x, width_y) * land[...].astype(jnp.float32)[None]
    for start, stop in parts_of(layers):
        shape = (stop - start, width_x, width_y)
        part, cond = head[start:stop], conduct[start:stop]
        row, lane = iota(shape, 1), iota(shape, 2)
        wet_old = saturation(head_old[start:stop], alpha[start:stop])
        total = porosity[start:stop] * (wet[start:stop] - wet_old)
        for axis, place, size in ((1, row, width_x), (2, lane, width_y)):
            face = (
                0.5
                * (cond + pltpu.roll(cond, size - 1, axis))
                * (part - pltpu.roll(part, size - 1, axis))
            )
            face = jnp.where(place == size - 1, 0.0, face)
            total = total + (face - pltpu.roll(face, 1, axis))
        below = min(layers, stop + 1)
        part, cond = head[max(0, start - 1) : below], conduct[max(0, start - 1) : below]
        down = 0.5 * (cond[:-1] + cond[1:]) * (part[:-1] - part[1:] + 1.0)
        if start == 0:
            down = jnp.concatenate([jnp.zeros_like(cond[:1]), down], 0)
        if stop == layers:
            down = jnp.concatenate([down, cond[-1:]], 0)
        total = total + (down[1:] - down[:-1])
        if start < top:
            last = min(stop, top)
            own = total[: last - start] - sources[start:last]
            total = jnp.concatenate([own, total[last - start :]], 0) if last < stop else own
        out[start:stop] = total


def faces_kernel(axes_x, partial, *refs):
    x_sent, x_got, out, x_faces = refs[:2], refs[2:4], refs[4], refs[5]
    layers, width_x, width_y = partial.shape
    even = place_of(axes_x) % 2 == 0
    faces = []
    for rows in (slice(0, layers), slice(layers, 2 * layers)):
        first, second = (r[rows, :] for r in x_sent)
        low, high = jnp.where(even, second, first), jnp.where(even, first, second)
        first, second = (r[rows, :] for r in x_got)
        before, after = jnp.where(even, second, first), jnp.where(even, first, second)
        faces.append((low, high, before, after))
    heads, conds = faces
    x_faces[0] = 0.5 * (conds[0] + conds[2]) * (heads[0] - heads[2])
    x_faces[1] = 0.5 * (conds[1] + conds[3]) * (heads[1] - heads[3])
    half = width_x // 2
    row = iota((half, width_y), 0)
    for k in range(layers):
        upper = jnp.where(row == 0, x_faces[0, k : k + 1, :], 0.0)
        lower = jnp.where(row == half - 1, x_faces[1, k : k + 1, :], 0.0)
        out[k, :half] = partial[k, :half] + upper
        out[k, half:] = partial[k, half:] + lower


def last_kernel(*refs):
    back, got, y_heads, y_conds, partial, nitrate = refs[:6]
    residual, nitrate_out, out, value_out, sems = refs[6:]
    layers, width_x, width_y = partial.shape
    top = nitrate.shape[0]
    flux = 0.5 * (y_conds[...] + neighbour_borders(back)) * (y_heads[...] - neighbour_borders(got))
    lane = iota(flux.shape, 1)
    on_border = (lane == 0) | (lane == width_y - 1)
    parts = parts_of(layers, 2 * CHUNK)
    writes = []
    for i, (start, stop) in enumerate(parts):
        for k in range(start, stop):
            edge = pltpu.roll(flux, width_y - 1 - 2 * k, 1)
            out[k] = partial[k] + jnp.where(on_border, edge, 0.0)
        rows = pl.ds(start, stop - start)
        copy = pltpu.make_async_copy(out.at[rows], residual.at[rows], sems.at[i])
        copy.start()
        writes.append(copy)
    for bank in range(nitrate.shape[1] // LANES):
        sat = unpack_blocks(back, top, bank)
        lanes = slice(bank * LANES, (bank + 1) * LANES)
        loss = 0.3 * sat * sat
        value = nitrate[:, lanes]
        for _ in range(NSUB):
            upper = jnp.concatenate([value[:1], value[:-1]], 0)
            lower = jnp.concatenate([value[1:], value[-1:]], 0)
            value = value + 0.2 * (upper + lower - 2.0 * value) - loss * value
        value_out[:, lanes] = value
    copy = pltpu.make_async_copy(value_out, nitrate_out, sems.at[len(parts)])
    copy.start()
    writes.append(copy)
    for copy in writes:
        copy.wait()


def swap_pairs(size, first):
    pairs = []
    for i in range(first, size - 1, 2):
        pairs += [(i, i + 1), (i + 1, i)]
    return pairs


def call(body, name, ins, outs, scratch=(), cost=1000):
    space = {"V": pltpu.VMEM, "S": pltpu.SMEM, "H": pltpu.HBM}
    kernel = pl.pallas_call(
        body,
        out_shape=tuple(shape for shape, _ in outs),
        in_specs=[pl.BlockSpec(memory_space=space[i]) for i in ins],
        out_specs=tuple(pl.BlockSpec(memory_space=space[i]) for _, i in outs),
        scratch_shapes=scratch,
        name=name,
        compiler_params=pltpu.CompilerParams(vmem_limit_bytes=VMEM_LIMIT),
        cost_estimate=pl.CostEstimate(flops=cost, bytes_accessed=cost, transcendentals=0),
    )

    def run(*args):
        return kernel(
            *(
                pltpu.with_memory_space_constraint(arg, pltpu.HBM) if i == "H" else arg
                for i, arg in zip(ins, args)
            )
        )

    return run


def per_device(
    pressure,
    pressure_old,
    conductivity,
    vg_alpha,
    porosity,
    land_mask,
    nitrate,
    patch_column,
    crop_type,
    patch_weight,
    rain,
    root_decay,
):
    layers, width_x, width_y = pressure.shape
    top, slots = nitrate.shape
    group, axes_x = ("gx", "gy"), ("sec", "gx")
    owners = lax.axis_size(group)
    per_block = slots // owners
    if LANES % per_block or slots % LANES or per_block != width_x:
        raise ValueError("block size")
    if width_y != LANES or width_x != LANES - MAIN_LANE or 2 * layers > EXTRA_LANE or not 8 <= top <= 11:
        raise ValueError("grid size")
    half = width_x // 2
    banks = slots // LANES
    f32 = jnp.float32
    shape, dma = jax.ShapeDtypeStruct, pltpu.SemaphoreType.DMA
    field = shape((layers, width_x, width_y), f32)
    field_in = pltpu.VMEM((layers, width_x, width_y), f32)
    count, halves = len(parts_of(layers)), len(parts_of(layers, 2 * CHUNK))
    blocks = shape((owners, half, LANES), f32)
    border = shape((width_x, width_y), f32)

    flat = [v.reshape(banks, LANES) for v in (patch_column, crop_type, patch_weight, rain)]
    x_edge = shape((2 * layers, width_y), f32)
    sent, head, head_border, table, land = call(
        front_kernel,
        "front",
        "HHHHHHH",
        (
            (blocks, "V"),
            (field, "V"),
            (border, "V"),
            (shape((1, root_decay.shape[0]), f32), "V"),
            (shape((width_x, width_y), land_mask.dtype), "V"),
        ),
        (
            [pltpu.VMEM((banks, LANES), v.dtype) for v in flat],
            dma((6,)),
            dma((len(parts_of(layers, FRONT_CHUNK)),)),
        ),
        cost=1000000000,
    )(*flat, pressure, root_decay.reshape(1, -1), land_mask)
    got = lax.all_to_all(sent, group, split_axis=0, concat_axis=0, tiled=True)
    back, patch_sat, fields, cond_border = call(
        functools.partial(pick_kernel, top),
        "pick",
        "VVVVV",
        (
            (blocks, "V"),
            (shape((banks, 16, LANES), f32), "V"),
            (shape((banks, 8, LANES), f32), "V"),
            (border, "V"),
        ),
    )(got, head, vg_alpha, conductivity, head_border)
    back = lax.all_to_all(back, group, split_axis=0, concat_axis=0, tiled=True)

    *x_sent, conduct, wet = call(
        functools.partial(edge_kernel, axes_x),
        "edge",
        "VVVV",
        ((x_edge, "V"), (x_edge, "V"), (field, "V"), (field, "V")),
    )(head, vg_alpha, conductivity, patch_sat)
    x_size = lax.axis_size(axes_x)
    x_got = [lax.ppermute(x_sent[i], axes_x, swap_pairs(x_size, i)) for i in (0, 1)]
    (partial,) = call(
        functools.partial(interior_kernel, top), "interior", "VVVVVVVVVVV", ((field, "V"),)
    )(
        pressure_old, porosity, head, vg_alpha, conduct, wet, fields, patch_sat, table, land,
        x_sent[0],
    )

    (partial,) = call(
        functools.partial(faces_kernel, axes_x),
        "faces",
        "VVVVV",
        ((field, "V"),),
        (pltpu.VMEM((2, layers, width_y), f32),),
    )(partial, *x_sent, *x_got)
    residual, nitrate_out = call(
        last_kernel,
        "last",
        "VVVVVV",
        ((field, "H"), (shape((top, slots), f32), "H")),
        (
            field_in,
            pltpu.VMEM((top, slots), f32),
            dma((halves + 1,)),
        ),
    )(
        back, got, head_border, cond_border, partial, nitrate,
    )
    return (residual, nitrate_out)


def solution(mesh):
    placed = (
        P(None, ("sec", "gx"), "gy"),
        P(None, ("sec", "gx"), "gy"),
        P(None, ("sec", "gx"), "gy"),
        P(None, ("sec", "gx"), "gy"),
        P(None, ("sec", "gx"), "gy"),
        P(("sec", "gx"), "gy"),
        P(None, ("sec", "gx", "gy")),
        P(("sec", "gx", "gy")),
        P(("sec", "gx", "gy")),
        P(("sec", "gx", "gy")),
        P(("sec", "gx", "gy")),
        P(),
    )
    return jax.shard_map(
        per_device,
        mesh=mesh,
        in_specs=placed,
        out_specs=(P(None, ("sec", "gx"), "gy"), P(None, ("sec", "gx", "gy"))),
        check_vma=False,
    )
```

```python
import functools

import jax
import jax.numpy as jnp
from jax import lax
from jax.experimental import pallas as pl
from jax.experimental.pallas import tpu as pltpu
from jax.sharding import PartitionSpec as P

NSUB = 4
LANES = 128
CHUNK = 10
FRONT_CHUNK = 25
EXTRA_LANE, MAIN_LANE = 104, 112
VMEM_LIMIT = 24 * 1024 * 1024


def iota(shape, dim):
    return lax.broadcasted_iota(jnp.int32, shape, dim)


def place_of(axes):
    index = 0
    for axis in axes:
        index = index * lax.axis_size(axis) + lax.axis_index(axis)
    return index


def parts_of(layers, size=CHUNK):
    return [(i, min(layers, i + size)) for i in range(0, layers, size)]


def saturation(head, alpha_field):
    suction = jnp.maximum(-head, 0.0) + jnp.log1p(jnp.exp(-jnp.abs(head)))
    scaled = alpha_field * suction
    return lax.rsqrt(1.0 + scaled * scaled)


def fold_border(border, own_first):
    rows, width = border.shape
    upper, lower = border[: rows // 2], border[rows // 2 :]
    if own_first:
        upper = pltpu.roll(upper, width - 1, 1)
    else:
        lower = pltpu.roll(lower, 1, 1)
    return jnp.where(iota(upper.shape, 1) % 2 == 0, upper, lower)


def unfold_border(block, place):
    width = block.shape[1]
    moved = pltpu.roll(block, 1 if place else width - 1, 1)
    return jnp.concatenate([moved, block] if place else [block, moved], axis=0)


def add_border(blocks, border):
    y_place, y_size = place_of(("gy",)), lax.axis_size("gy")
    base = place_of(("gx", "gy"))

    @pl.when(y_place > 0)
    def _():
        blocks[base - 1] = blocks[base - 1] + fold_border(border, True)

    @pl.when(y_place < y_size - 1)
    def _():
        blocks[base + 1] = blocks[base + 1] + fold_border(border, False)


def neighbour_borders(blocks):
    y_place, y_size = place_of(("gy",)), lax.axis_size("gy")
    base = place_of(("gx", "gy"))
    before = blocks[jnp.maximum(base - 1, 0)]
    before = unfold_border(jnp.where(y_place > 0, before, 0.0), 1)
    after = blocks[jnp.minimum(base + 1, blocks.shape[0] - 1)]
    after = unfold_border(jnp.where(y_place < y_size - 1, after, 0.0), 0)
    return jnp.where(iota(after.shape, 1) % 2 == 0, after, before)


def border_of(ref, start, stop, border):
    lane = iota(border.shape, 1)
    for k in range(start, stop):
        moved = pltpu.roll(ref[k], (2 * k + 1) % LANES, 1)
        border = jnp.where(lane // 2 == k, moved, border)
    return border


def pack_blocks(rows, blocks, bank):
    width = LANES - MAIN_LANE
    size = LANES // width
    main = rows[:8]
    lane = iota((8, LANES), 1)
    pieces = []
    for i in range(8, rows.shape[0]):
        row = rows[i : i + 1]
        pieces += [row, pltpu.roll(row, LANES - width // 2, 1)]
    if pieces:
        pieces.append(jnp.zeros((8 - len(pieces), LANES), jnp.float32))
        extra = jnp.concatenate(pieces, axis=0)
    for b in range(size):
        block = jnp.where(lane >= MAIN_LANE, pltpu.roll(main, (MAIN_LANE - width * b) % LANES, 1), 0.0)
        if pieces:
            moved = pltpu.roll(extra, (EXTRA_LANE - width * b) % LANES, 1)
            block = jnp.where((lane >= EXTRA_LANE) & (lane < MAIN_LANE), moved, block)
        blocks[bank * size + b] = block


def unpack_blocks(blocks, count, bank):
    width = LANES - MAIN_LANE
    size = LANES // width
    lane = iota((8, LANES), 1)
    main = jnp.zeros((8, LANES), jnp.float32)
    extra = jnp.zeros((8, LANES), jnp.float32)
    for b in range(size):
        block = blocks[bank * size + b]
        moved = pltpu.roll(block, (width * b - MAIN_LANE) % LANES, 1)
        main = jnp.where(lane // width == b, moved, main)
        if count > 8:
            moved = pltpu.roll(block, (width * b - EXTRA_LANE) % LANES, 1)
            extra = jnp.where(lane // width == b, moved, extra)
    rows = [main]
    first = lane[:1] % width < width // 2
    for i in range(count - 8):
        second = pltpu.roll(extra[2 * i + 1 : 2 * i + 2], width // 2, 1)
        rows.append(jnp.where(first, extra[2 * i : 2 * i + 1], second))
    return jnp.concatenate(rows, axis=0) if count > 8 else main


def front_kernel(*refs):
    fields, grid, extra = refs[:4], refs[4], refs[5:7]
    sent, head, head_border, *extra_out = refs[7:12]
    fields_in, small_sems, sems = refs[12:]
    layers, width_x, width_y = head.shape
    small = [pltpu.make_async_copy(fields[i], fields_in[i], small_sems.at[i]) for i in range(4)]
    extras = [pltpu.make_async_copy(extra[i], extra_out[i], small_sems.at[4 + i]) for i in range(2)]
    parts = parts_of(layers, FRONT_CHUNK)
    large = []
    for i, (start, stop) in enumerate(parts):
        rows = pl.ds(start, stop - start)
        large.append(pltpu.make_async_copy(grid.at[rows], head.at[rows], sems.at[i]))
    for copy in (*small, *large, *extras):
        copy.start()
    for copy in small:
        copy.wait()
    for bank in range(fields_in[0].shape[0]):
        rows = [ref[bank : bank + 1, :].astype(jnp.float32) for ref in fields_in]
        rows.append(jnp.zeros((4, LANES), jnp.float32))
        pack_blocks(jnp.concatenate(rows, axis=0), sent, bank)
    heads = jnp.zeros((width_x, width_y), jnp.float32)
    for copy, (start, stop) in zip(large, parts):
        copy.wait()
        heads = border_of(head, start, stop, heads)
    head_border[...] = heads
    add_border(sent, heads)
    for copy in extras:
        copy.wait()


def edge_kernel(axes_x, head, alpha, perm, order, x_first, x_second, conduct, wet_out):
    layers, width_x, width_y = head.shape
    for start, stop in parts_of(layers):
        part = slice(start, stop)
        wet = saturation(head[part], alpha[part])
        conduct[part] = perm[part] * wet * wet * wet
        wet_out[part] = wet
    even = place_of(axes_x) % 2 == 0
    for field, ref in enumerate((head, conduct)):
        rows = slice(field * layers, (field + 1) * layers)
        low, high = ref[:, 0, :], ref[:, width_x - 1, :]
        x_first[rows, :] = jnp.where(even, high, low)
        x_second[rows, :] = jnp.where(even, low, high)


def hot(ids, size):
    return iota((size, LANES), 0) == ids


def pick_kernel(top, got, head, alpha, perm, head_border, back, patch_sat, fields, cond_border):
    layers, width_x, width_y = head.shape
    sat = saturation(head[:top], alpha[:top]).reshape(top * width_x, width_y).astype(jnp.bfloat16)
    zero = jnp.zeros((width_x, width_y), jnp.float32)
    wet = saturation(head_border[...], border_of(alpha, 0, layers, zero))
    border = border_of(perm, 0, layers, zero) * wet * wet * wet
    cond_border[...] = border
    for bank in range(fields.shape[0]):
        rows = unpack_blocks(got, 8, bank)
        fields[bank] = rows
        ids = rows[0:1].astype(jnp.int32)
        lane_hot = hot(lax.rem(ids, width_y), width_y).astype(jnp.float32).astype(jnp.bfloat16)
        row_hot = hot(lax.div(ids, width_y), width_x)
        picked = jnp.dot(sat, lane_hot, preferred_element_type=jnp.float32)
        patch_sat[bank] = jnp.zeros(patch_sat.shape[1:], jnp.float32)
        chosen = jnp.where(row_hot[None], picked.reshape(top, width_x, LANES), 0.0)
        patch_sat[bank, :top, :] = jnp.sum(chosen, axis=1)
        pack_blocks(patch_sat[bank][:top], back, bank)
    add_border(back, border)


def column_sources(top, width_x, width_y, fields, patch_sat, root_decay):
    total = jnp.zeros((top * width_x, width_y), jnp.float32)
    table = root_decay[...]
    for h in range(fields.shape[0]):
        ids, crop, weight, rain = (fields[h, i : i + 1, :] for i in range(4))
        ids = ids.astype(jnp.int32)
        crop = crop.astype(jnp.int32)
        decay = jnp.zeros((1, LANES), jnp.float32)
        for kind in range(table.shape[1]):
            decay = jnp.where(crop == kind, table[:, kind : kind + 1], decay)
        level = iota((top, LANES), 0)
        profile = jnp.exp(-(level.astype(jnp.float32) + 0.5) * decay)
        profile = profile / jnp.sum(profile, axis=0, keepdims=True)
        sat = patch_sat[h][:top]
        inflow = jnp.where(level == 0, rain * (1.0 - sat), 0.0)
        sources = inflow - weight * profile * sat
        lane_hot = hot(lax.rem(ids, width_y), width_y).astype(jnp.float32)
        row_hot = hot(lax.div(ids, width_y), width_x)
        spread = jnp.concatenate(
            [jnp.where(row_hot, sources[k : k + 1], 0.0) for k in range(top)], axis=0
        )
        total = total + lax.dot_general(
            spread,
            lane_hot,
            (((1,), (1,)), ((), ())),
            precision=lax.Precision.HIGHEST,
            preferred_element_type=jnp.float32,
        )
    return total


def interior_kernel(top, *refs):
    head_old, porosity, head, alpha, conduct, wet = refs[:6]
    fields, patch_sat, root_decay, land, order, out = refs[6:]
    layers, width_x, width_y = head.shape
    sources = column_sources(top, width_x, width_y, fields, patch_sat, root_decay)
    sources = sources.reshape(top, width_x, width_y) * land[...].astype(jnp.float32)[None]
    for start, stop in parts_of(layers):
        shape = (stop - start, width_x, width_y)
        part, cond = head[start:stop], conduct[start:stop]
        row, lane = iota(shape, 1), iota(shape, 2)
        wet_old = saturation(head_old[start:stop], alpha[start:stop])
        total = porosity[start:stop] * (wet[start:stop] - wet_old)
        for axis, place, size in ((1, row, width_x), (2, lane, width_y)):
            face = (
                0.5
                * (cond + pltpu.roll(cond, size - 1, axis))
                * (part - pltpu.roll(part, size - 1, axis))
            )
            face = jnp.where(place == size - 1, 0.0, face)
            total = total + (face - pltpu.roll(face, 1, axis))
        below = min(layers, stop + 1)
        part, cond = head[max(0, start - 1) : below], conduct[max(0, start - 1) : below]
        down = 0.5 * (cond[:-1] + cond[1:]) * (part[:-1] - part[1:] + 1.0)
        if start == 0:
            down = jnp.concatenate([jnp.zeros_like(cond[:1]), down], 0)
        if stop == layers:
            down = jnp.concatenate([down, cond[-1:]], 0)
        total = total + (down[1:] - down[:-1])
        if start < top:
            last = min(stop, top)
            own = total[: last - start] - sources[start:last]
            total = jnp.concatenate([own, total[last - start :]], 0) if last < stop else own
        out[start:stop] = total


def last_kernel(axes_x, *refs):
    back, got, y_heads, y_conds, partial, nitrate = refs[:6]
    x_sent, x_got = refs[6:8], refs[8:10]
    residual, nitrate_out, out, value_out, x_faces, sems = refs[10:]
    layers, width_x, width_y = partial.shape
    top = nitrate.shape[0]
    even = place_of(axes_x) % 2 == 0
    faces = []
    for rows in (slice(0, layers), slice(layers, 2 * layers)):
        first, second = (r[rows, :] for r in x_sent)
        low, high = jnp.where(even, second, first), jnp.where(even, first, second)
        first, second = (r[rows, :] for r in x_got)
        before, after = jnp.where(even, second, first), jnp.where(even, first, second)
        faces.append((low, high, before, after))
    heads, conds = faces
    x_faces[0] = 0.5 * (conds[0] + conds[2]) * (heads[0] - heads[2])
    x_faces[1] = 0.5 * (conds[1] + conds[3]) * (heads[1] - heads[3])
    flux = 0.5 * (y_conds[...] + neighbour_borders(back)) * (y_heads[...] - neighbour_borders(got))
    row, lane = iota(flux.shape, 0), iota(flux.shape, 1)
    on_border = (lane == 0) | (lane == width_y - 1)
    parts = parts_of(layers)
    writes = []
    for i, (start, stop) in enumerate(parts):
        for k in range(start, stop):
            edge = pltpu.roll(flux, width_y - 1 - 2 * k, 1)
            one = partial[k] + jnp.where(on_border, edge, 0.0)
            one = one + jnp.where(row == 0, x_faces[0, k : k + 1, :], 0.0)
            one = one + jnp.where(row == width_x - 1, x_faces[1, k : k + 1, :], 0.0)
            out[k] = one
        rows = pl.ds(start, stop - start)
        copy = pltpu.make_async_copy(out.at[rows], residual.at[rows], sems.at[i])
        copy.start()
        writes.append(copy)
    for bank in range(nitrate.shape[1] // LANES):
        sat = unpack_blocks(back, top, bank)
        lanes = slice(bank * LANES, (bank + 1) * LANES)
        loss = 0.3 * sat * sat
        value = nitrate[:, lanes]
        for _ in range(NSUB):
            upper = jnp.concatenate([value[:1], value[:-1]], 0)
            lower = jnp.concatenate([value[1:], value[-1:]], 0)
            value = value + 0.2 * (upper + lower - 2.0 * value) - loss * value
        value_out[:, lanes] = value
    copy = pltpu.make_async_copy(value_out, nitrate_out, sems.at[len(parts)])
    copy.start()
    writes.append(copy)
    for copy in writes:
        copy.wait()


def swap_pairs(size, first):
    pairs = []
    for i in range(first, size - 1, 2):
        pairs += [(i, i + 1), (i + 1, i)]
    return pairs


def call(body, name, ins, outs, scratch=(), cost=1000):
    space = {"V": pltpu.VMEM, "S": pltpu.SMEM, "H": pltpu.HBM}
    kernel = pl.pallas_call(
        body,
        out_shape=tuple(shape for shape, _ in outs),
        in_specs=[pl.BlockSpec(memory_space=space[i]) for i in ins],
        out_specs=tuple(pl.BlockSpec(memory_space=space[i]) for _, i in outs),
        scratch_shapes=scratch,
        name=name,
        compiler_params=pltpu.CompilerParams(vmem_limit_bytes=VMEM_LIMIT),
        cost_estimate=pl.CostEstimate(flops=cost, bytes_accessed=cost, transcendentals=0),
    )

    def run(*args):
        return kernel(
            *(
                pltpu.with_memory_space_constraint(arg, pltpu.HBM) if i == "H" else arg
                for i, arg in zip(ins, args)
            )
        )

    return run


def per_device(
    pressure,
    pressure_old,
    conductivity,
    vg_alpha,
    porosity,
    land_mask,
    nitrate,
    patch_column,
    crop_type,
    patch_weight,
    rain,
    root_decay,
):
    layers, width_x, width_y = pressure.shape
    top, slots = nitrate.shape
    group, axes_x = ("gx", "gy"), ("sec", "gx")
    owners = lax.axis_size(group)
    per_block = slots // owners
    if LANES % per_block or slots % LANES or per_block != width_x:
        raise ValueError("block size")
    if width_y != LANES or width_x != LANES - MAIN_LANE or 2 * layers > EXTRA_LANE or not 8 <= top <= 11:
        raise ValueError("grid size")
    half = width_x // 2
    banks = slots // LANES
    f32 = jnp.float32
    shape, dma = jax.ShapeDtypeStruct, pltpu.SemaphoreType.DMA
    field = shape((layers, width_x, width_y), f32)
    field_in = pltpu.VMEM((layers, width_x, width_y), f32)
    count, halves = len(parts_of(layers)), len(parts_of(layers))
    blocks = shape((owners, half, LANES), f32)
    border = shape((width_x, width_y), f32)

    flat = [v.reshape(banks, LANES) for v in (patch_column, crop_type, patch_weight, rain)]
    x_edge = shape((2 * layers, width_y), f32)
    sent, head, head_border, table, land = call(
        front_kernel,
        "front",
        "HHHHHHH",
        (
            (blocks, "V"),
            (field, "V"),
            (border, "V"),
            (shape((1, root_decay.shape[0]), f32), "V"),
            (shape((width_x, width_y), land_mask.dtype), "V"),
        ),
        (
            [pltpu.VMEM((banks, LANES), v.dtype) for v in flat],
            dma((6,)),
            dma((len(parts_of(layers, FRONT_CHUNK)),)),
        ),
        cost=1000000000,
    )(*flat, pressure, root_decay.reshape(1, -1), land_mask)
    got = lax.all_to_all(sent, group, split_axis=0, concat_axis=0, tiled=True)
    back, patch_sat, fields, cond_border = call(
        functools.partial(pick_kernel, top),
        "pick",
        "VVVVV",
        (
            (blocks, "V"),
            (shape((banks, 16, LANES), f32), "V"),
            (shape((banks, 8, LANES), f32), "V"),
            (border, "V"),
        ),
    )(got, head, vg_alpha, conductivity, head_border)
    back = lax.all_to_all(back, group, split_axis=0, concat_axis=0, tiled=True)

    *x_sent, conduct, wet = call(
        functools.partial(edge_kernel, axes_x),
        "edge",
        "VVVV",
        ((x_edge, "V"), (x_edge, "V"), (field, "V"), (field, "V")),
    )(head, vg_alpha, conductivity, patch_sat)
    x_size = lax.axis_size(axes_x)
    x_got = [lax.ppermute(x_sent[i], axes_x, swap_pairs(x_size, i)) for i in (0, 1)]
    (partial,) = call(
        functools.partial(interior_kernel, top), "interior", "VVVVVVVVVVV", ((field, "V"),)
    )(
        pressure_old, porosity, head, vg_alpha, conduct, wet, fields, patch_sat, table, land,
        x_sent[0],
    )

    residual, nitrate_out = call(
        functools.partial(last_kernel, axes_x),
        "last",
        "VVVVVVVVVV",
        ((field, "H"), (shape((top, slots), f32), "H")),
        (
            field_in,
            pltpu.VMEM((top, slots), f32),
            pltpu.VMEM((2, layers, width_y), f32),
            dma((halves + 1,)),
        ),
    )(
        back, got, head_border, cond_border, partial, nitrate, *x_sent, *x_got,
    )
    return (residual, nitrate_out)


def solution(mesh):
    placed = (
        P(None, ("sec", "gx"), "gy"),
        P(None, ("sec", "gx"), "gy"),
        P(None, ("sec", "gx"), "gy"),
        P(None, ("sec", "gx"), "gy"),
        P(None, ("sec", "gx"), "gy"),
        P(("sec", "gx"), "gy"),
        P(None, ("sec", "gx", "gy")),
        P(("sec", "gx", "gy")),
        P(("sec", "gx", "gy")),
        P(("sec", "gx", "gy")),
        P(("sec", "gx", "gy")),
        P(),
    )
    return jax.shard_map(
        per_device,
        mesh=mesh,
        in_specs=placed,
        out_specs=(P(None, ("sec", "gx"), "gy"), P(None, ("sec", "gx", "gy"))),
        check_vma=False,
    )
```

```python
import functools

import jax
import jax.numpy as jnp
from jax import lax
from jax.experimental import pallas as pl
from jax.experimental.pallas import tpu as pltpu
from jax.sharding import PartitionSpec as P

NSUB = 4
LANES = 128
CHUNK = 10
FRONT_CHUNK = 25
EXTRA_LANE, MAIN_LANE = 104, 112
VMEM_LIMIT = 24 * 1024 * 1024


def iota(shape, dim):
    return lax.broadcasted_iota(jnp.int32, shape, dim)


def place_of(axes):
    index = 0
    for axis in axes:
        index = index * lax.axis_size(axis) + lax.axis_index(axis)
    return index


def parts_of(layers, size=CHUNK):
    return [(i, min(layers, i + size)) for i in range(0, layers, size)]


def saturation(head, alpha_field):
    suction = jnp.maximum(-head, 0.0) + jnp.log1p(jnp.exp(-jnp.abs(head)))
    scaled = alpha_field * suction
    return lax.rsqrt(1.0 + scaled * scaled)


def fold_border(border, own_first):
    rows, width = border.shape
    upper, lower = border[: rows // 2], border[rows // 2 :]
    if own_first:
        upper = pltpu.roll(upper, width - 1, 1)
    else:
        lower = pltpu.roll(lower, 1, 1)
    return jnp.where(iota(upper.shape, 1) % 2 == 0, upper, lower)


def unfold_border(block, place):
    width = block.shape[1]
    moved = pltpu.roll(block, 1 if place else width - 1, 1)
    return jnp.concatenate([moved, block] if place else [block, moved], axis=0)


def add_border(blocks, border):
    y_place, y_size = place_of(("gy",)), lax.axis_size("gy")
    base = place_of(("gx", "gy"))

    @pl.when(y_place > 0)
    def _():
        blocks[base - 1] = blocks[base - 1] + fold_border(border, True)

    @pl.when(y_place < y_size - 1)
    def _():
        blocks[base + 1] = blocks[base + 1] + fold_border(border, False)


def neighbour_borders(blocks):
    y_place, y_size = place_of(("gy",)), lax.axis_size("gy")
    base = place_of(("gx", "gy"))
    before = blocks[jnp.maximum(base - 1, 0)]
    before = unfold_border(jnp.where(y_place > 0, before, 0.0), 1)
    after = blocks[jnp.minimum(base + 1, blocks.shape[0] - 1)]
    after = unfold_border(jnp.where(y_place < y_size - 1, after, 0.0), 0)
    return jnp.where(iota(after.shape, 1) % 2 == 0, after, before)


def border_of(ref, start, stop, border):
    lane = iota(border.shape, 1)
    for k in range(start, stop):
        moved = pltpu.roll(ref[k], (2 * k + 1) % LANES, 1)
        border = jnp.where(lane // 2 == k, moved, border)
    return border


def pack_blocks(rows, blocks, bank):
    width = LANES - MAIN_LANE
    size = LANES // width
    main = rows[:8]
    lane = iota((8, LANES), 1)
    pieces = []
    for i in range(8, rows.shape[0]):
        row = rows[i : i + 1]
        pieces += [row, pltpu.roll(row, LANES - width // 2, 1)]
    if pieces:
        pieces.append(jnp.zeros((8 - len(pieces), LANES), jnp.float32))
        extra = jnp.concatenate(pieces, axis=0)
    for b in range(size):
        block = jnp.where(lane >= MAIN_LANE, pltpu.roll(main, (MAIN_LANE - width * b) % LANES, 1), 0.0)
        if pieces:
            moved = pltpu.roll(extra, (EXTRA_LANE - width * b) % LANES, 1)
            block = jnp.where((lane >= EXTRA_LANE) & (lane < MAIN_LANE), moved, block)
        blocks[bank * size + b] = block


def unpack_blocks(blocks, count, bank):
    width = LANES - MAIN_LANE
    size = LANES // width
    lane = iota((8, LANES), 1)
    main = jnp.zeros((8, LANES), jnp.float32)
    extra = jnp.zeros((8, LANES), jnp.float32)
    for b in range(size):
        block = blocks[bank * size + b]
        moved = pltpu.roll(block, (width * b - MAIN_LANE) % LANES, 1)
        main = jnp.where(lane // width == b, moved, main)
        if count > 8:
            moved = pltpu.roll(block, (width * b - EXTRA_LANE) % LANES, 1)
            extra = jnp.where(lane // width == b, moved, extra)
    rows = [main]
    first = lane[:1] % width < width // 2
    for i in range(count - 8):
        second = pltpu.roll(extra[2 * i + 1 : 2 * i + 2], width // 2, 1)
        rows.append(jnp.where(first, extra[2 * i : 2 * i + 1], second))
    return jnp.concatenate(rows, axis=0) if count > 8 else main


def front_kernel(*refs):
    fields, grid, extra = refs[:4], refs[4], refs[5:7]
    sent, head, head_border, *extra_out = refs[7:12]
    fields_in, small_sems, sems = refs[12:]
    layers, width_x, width_y = head.shape
    small = [pltpu.make_async_copy(fields[i], fields_in[i], small_sems.at[i]) for i in range(4)]
    extras = [pltpu.make_async_copy(extra[i], extra_out[i], small_sems.at[4 + i]) for i in range(2)]
    parts = parts_of(layers, FRONT_CHUNK)
    large = []
    for i, (start, stop) in enumerate(parts):
        rows = pl.ds(start, stop - start)
        large.append(pltpu.make_async_copy(grid.at[rows], head.at[rows], sems.at[i]))
    for copy in (*large, *small, *extras):
        copy.start()
    for copy in small:
        copy.wait()
    for bank in range(fields_in[0].shape[0]):
        rows = [ref[bank : bank + 1, :].astype(jnp.float32) for ref in fields_in]
        rows.append(jnp.zeros((4, LANES), jnp.float32))
        pack_blocks(jnp.concatenate(rows, axis=0), sent, bank)
    heads = jnp.zeros((width_x, width_y), jnp.float32)
    for copy, (start, stop) in zip(large, parts):
        copy.wait()
        heads = border_of(head, start, stop, heads)
    head_border[...] = heads
    add_border(sent, heads)
    for copy in extras:
        copy.wait()


def edge_kernel(axes_x, head, alpha, perm, order, x_first, x_second, conduct, wet_out):
    layers, width_x, width_y = head.shape
    for start, stop in parts_of(layers):
        part = slice(start, stop)
        wet = saturation(head[part], alpha[part])
        conduct[part] = perm[part] * wet * wet * wet
        wet_out[part] = wet
    even = place_of(axes_x) % 2 == 0
    for field, ref in enumerate((head, conduct)):
        rows = slice(field * layers, (field + 1) * layers)
        low, high = ref[:, 0, :], ref[:, width_x - 1, :]
        x_first[rows, :] = jnp.where(even, high, low)
        x_second[rows, :] = jnp.where(even, low, high)


def hot(ids, size):
    return iota((size, LANES), 0) == ids


def pick_kernel(top, got, head, alpha, perm, head_border, back, patch_sat, fields, cond_border):
    layers, width_x, width_y = head.shape
    sat = saturation(head[:top], alpha[:top]).reshape(top * width_x, width_y).astype(jnp.bfloat16)
    zero = jnp.zeros((width_x, width_y), jnp.float32)
    wet = saturation(head_border[...], border_of(alpha, 0, layers, zero))
    border = border_of(perm, 0, layers, zero) * wet * wet * wet
    cond_border[...] = border
    for bank in range(fields.shape[0]):
        rows = unpack_blocks(got, 8, bank)
        fields[bank] = rows
        ids = rows[0:1].astype(jnp.int32)
        lane_hot = hot(lax.rem(ids, width_y), width_y).astype(jnp.float32).astype(jnp.bfloat16)
        row_hot = hot(lax.div(ids, width_y), width_x)
        picked = jnp.dot(sat, lane_hot, preferred_element_type=jnp.float32)
        patch_sat[bank] = jnp.zeros(patch_sat.shape[1:], jnp.float32)
        chosen = jnp.where(row_hot[None], picked.reshape(top, width_x, LANES), 0.0)
        patch_sat[bank, :top, :] = jnp.sum(chosen, axis=1)
        pack_blocks(patch_sat[bank][:top], back, bank)
    add_border(back, border)


def column_sources(top, width_x, width_y, fields, patch_sat, root_decay):
    total = jnp.zeros((top * width_x, width_y), jnp.float32)
    table = root_decay[...]
    for h in range(fields.shape[0]):
        ids, crop, weight, rain = (fields[h, i : i + 1, :] for i in range(4))
        ids = ids.astype(jnp.int32)
        crop = crop.astype(jnp.int32)
        decay = jnp.zeros((1, LANES), jnp.float32)
        for kind in range(table.shape[1]):
            decay = jnp.where(crop == kind, table[:, kind : kind + 1], decay)
        level = iota((top, LANES), 0)
        profile = jnp.exp(-(level.astype(jnp.float32) + 0.5) * decay)
        profile = profile / jnp.sum(profile, axis=0, keepdims=True)
        sat = patch_sat[h][:top]
        inflow = jnp.where(level == 0, rain * (1.0 - sat), 0.0)
        sources = inflow - weight * profile * sat
        lane_hot = hot(lax.rem(ids, width_y), width_y).astype(jnp.float32)
        row_hot = hot(lax.div(ids, width_y), width_x)
        spread = jnp.concatenate(
            [jnp.where(row_hot, sources[k : k + 1], 0.0) for k in range(top)], axis=0
        )
        total = total + lax.dot_general(
            spread,
            lane_hot,
            (((1,), (1,)), ((), ())),
            precision=lax.Precision.HIGHEST,
            preferred_element_type=jnp.float32,
        )
    return total


def interior_kernel(top, *refs):
    head_old, porosity, head, alpha, conduct, wet = refs[:6]
    fields, patch_sat, root_decay, land, order, out = refs[6:]
    layers, width_x, width_y = head.shape
    sources = column_sources(top, width_x, width_y, fields, patch_sat, root_decay)
    sources = sources.reshape(top, width_x, width_y) * land[...].astype(jnp.float32)[None]
    for start, stop in parts_of(layers):
        shape = (stop - start, width_x, width_y)
        part, cond = head[start:stop], conduct[start:stop]
        row, lane = iota(shape, 1), iota(shape, 2)
        wet_old = saturation(head_old[start:stop], alpha[start:stop])
        total = porosity[start:stop] * (wet[start:stop] - wet_old)
        for axis, place, size in ((1, row, width_x), (2, lane, width_y)):
            face = (
                0.5
                * (cond + pltpu.roll(cond, size - 1, axis))
                * (part - pltpu.roll(part, size - 1, axis))
            )
            face = jnp.where(place == size - 1, 0.0, face)
            total = total + (face - pltpu.roll(face, 1, axis))
        below = min(layers, stop + 1)
        part, cond = head[max(0, start - 1) : below], conduct[max(0, start - 1) : below]
        down = 0.5 * (cond[:-1] + cond[1:]) * (part[:-1] - part[1:] + 1.0)
        if start == 0:
            down = jnp.concatenate([jnp.zeros_like(cond[:1]), down], 0)
        if stop == layers:
            down = jnp.concatenate([down, cond[-1:]], 0)
        total = total + (down[1:] - down[:-1])
        if start < top:
            last = min(stop, top)
            own = total[: last - start] - sources[start:last]
            total = jnp.concatenate([own, total[last - start :]], 0) if last < stop else own
        out[start:stop] = total


def last_kernel(axes_x, *refs):
    back, got, y_heads, y_conds, partial, nitrate = refs[:6]
    x_sent, x_got = refs[6:8], refs[8:10]
    residual, nitrate_out, out, value_out, x_faces, sems = refs[10:]
    layers, width_x, width_y = partial.shape
    top = nitrate.shape[0]
    even = place_of(axes_x) % 2 == 0
    faces = []
    for rows in (slice(0, layers), slice(layers, 2 * layers)):
        first, second = (r[rows, :] for r in x_sent)
        low, high = jnp.where(even, second, first), jnp.where(even, first, second)
        first, second = (r[rows, :] for r in x_got)
        before, after = jnp.where(even, second, first), jnp.where(even, first, second)
        faces.append((low, high, before, after))
    heads, conds = faces
    x_faces[0] = 0.5 * (conds[0] + conds[2]) * (heads[0] - heads[2])
    x_faces[1] = 0.5 * (conds[1] + conds[3]) * (heads[1] - heads[3])
    flux = 0.5 * (y_conds[...] + neighbour_borders(back)) * (y_heads[...] - neighbour_borders(got))
    row, lane = iota(flux.shape, 0), iota(flux.shape, 1)
    on_border = (lane == 0) | (lane == width_y - 1)
    parts = parts_of(layers)
    writes = []
    for i, (start, stop) in enumerate(parts):
        for k in range(start, stop):
            edge = pltpu.roll(flux, width_y - 1 - 2 * k, 1)
            one = partial[k] + jnp.where(on_border, edge, 0.0)
            one = one + jnp.where(row == 0, x_faces[0, k : k + 1, :], 0.0)
            one = one + jnp.where(row == width_x - 1, x_faces[1, k : k + 1, :], 0.0)
            out[k] = one
        rows = pl.ds(start, stop - start)
        copy = pltpu.make_async_copy(out.at[rows], residual.at[rows], sems.at[i])
        copy.start()
        writes.append(copy)
    for bank in range(nitrate.shape[1] // LANES):
        sat = unpack_blocks(back, top, bank)
        lanes = slice(bank * LANES, (bank + 1) * LANES)
        loss = 0.3 * sat * sat
        value = nitrate[:, lanes]
        for _ in range(NSUB):
            upper = jnp.concatenate([value[:1], value[:-1]], 0)
            lower = jnp.concatenate([value[1:], value[-1:]], 0)
            value = value + 0.2 * (upper + lower - 2.0 * value) - loss * value
        value_out[:, lanes] = value
    copy = pltpu.make_async_copy(value_out, nitrate_out, sems.at[len(parts)])
    copy.start()
    writes.append(copy)
    for copy in writes:
        copy.wait()


def swap_pairs(size, first):
    pairs = []
    for i in range(first, size - 1, 2):
        pairs += [(i, i + 1), (i + 1, i)]
    return pairs


def call(body, name, ins, outs, scratch=(), cost=1000):
    space = {"V": pltpu.VMEM, "S": pltpu.SMEM, "H": pltpu.HBM}
    kernel = pl.pallas_call(
        body,
        out_shape=tuple(shape for shape, _ in outs),
        in_specs=[pl.BlockSpec(memory_space=space[i]) for i in ins],
        out_specs=tuple(pl.BlockSpec(memory_space=space[i]) for _, i in outs),
        scratch_shapes=scratch,
        name=name,
        compiler_params=pltpu.CompilerParams(vmem_limit_bytes=VMEM_LIMIT),
        cost_estimate=pl.CostEstimate(flops=cost, bytes_accessed=cost, transcendentals=0),
    )

    def run(*args):
        return kernel(
            *(
                pltpu.with_memory_space_constraint(arg, pltpu.HBM) if i == "H" else arg
                for i, arg in zip(ins, args)
            )
        )

    return run


def per_device(
    pressure,
    pressure_old,
    conductivity,
    vg_alpha,
    porosity,
    land_mask,
    nitrate,
    patch_column,
    crop_type,
    patch_weight,
    rain,
    root_decay,
):
    layers, width_x, width_y = pressure.shape
    top, slots = nitrate.shape
    group, axes_x = ("gx", "gy"), ("sec", "gx")
    owners = lax.axis_size(group)
    per_block = slots // owners
    if LANES % per_block or slots % LANES or per_block != width_x:
        raise ValueError("block size")
    if width_y != LANES or width_x != LANES - MAIN_LANE or 2 * layers > EXTRA_LANE or not 8 <= top <= 11:
        raise ValueError("grid size")
    half = width_x // 2
    banks = slots // LANES
    f32 = jnp.float32
    shape, dma = jax.ShapeDtypeStruct, pltpu.SemaphoreType.DMA
    field = shape((layers, width_x, width_y), f32)
    field_in = pltpu.VMEM((layers, width_x, width_y), f32)
    count, halves = len(parts_of(layers)), len(parts_of(layers))
    blocks = shape((owners, half, LANES), f32)
    border = shape((width_x, width_y), f32)

    flat = [v.reshape(banks, LANES) for v in (patch_column, crop_type, patch_weight, rain)]
    x_edge = shape((2 * layers, width_y), f32)
    sent, head, head_border, table, land = call(
        front_kernel,
        "front",
        "HHHHHHH",
        (
            (blocks, "V"),
            (field, "V"),
            (border, "V"),
            (shape((1, root_decay.shape[0]), f32), "V"),
            (shape((width_x, width_y), land_mask.dtype), "V"),
        ),
        (
            [pltpu.VMEM((banks, LANES), v.dtype) for v in flat],
            dma((6,)),
            dma((len(parts_of(layers, FRONT_CHUNK)),)),
        ),
        cost=1000000000,
    )(*flat, pressure, root_decay.reshape(1, -1), land_mask)
    got = lax.all_to_all(sent, group, split_axis=0, concat_axis=0, tiled=True)
    back, patch_sat, fields, cond_border = call(
        functools.partial(pick_kernel, top),
        "pick",
        "VVVVV",
        (
            (blocks, "V"),
            (shape((banks, 16, LANES), f32), "V"),
            (shape((banks, 8, LANES), f32), "V"),
            (border, "V"),
        ),
    )(got, head, vg_alpha, conductivity, head_border)
    back = lax.all_to_all(back, group, split_axis=0, concat_axis=0, tiled=True)

    *x_sent, conduct, wet = call(
        functools.partial(edge_kernel, axes_x),
        "edge",
        "VVVV",
        ((x_edge, "V"), (x_edge, "V"), (field, "V"), (field, "V")),
    )(head, vg_alpha, conductivity, patch_sat)
    x_size = lax.axis_size(axes_x)
    x_got = [lax.ppermute(x_sent[i], axes_x, swap_pairs(x_size, i)) for i in (0, 1)]
    (partial,) = call(
        functools.partial(interior_kernel, top), "interior", "VVVVVVVVVVV", ((field, "V"),)
    )(
        pressure_old, porosity, head, vg_alpha, conduct, wet, fields, patch_sat, table, land,
        x_sent[0],
    )

    residual, nitrate_out = call(
        functools.partial(last_kernel, axes_x),
        "last",
        "VVVVVVVVVV",
        ((field, "H"), (shape((top, slots), f32), "H")),
        (
            field_in,
            pltpu.VMEM((top, slots), f32),
            pltpu.VMEM((2, layers, width_y), f32),
            dma((halves + 1,)),
        ),
    )(
        back, got, head_border, cond_border, partial, nitrate, *x_sent, *x_got,
    )
    return (residual, nitrate_out)


def solution(mesh):
    placed = (
        P(None, ("sec", "gx"), "gy"),
        P(None, ("sec", "gx"), "gy"),
        P(None, ("sec", "gx"), "gy"),
        P(None, ("sec", "gx"), "gy"),
        P(None, ("sec", "gx"), "gy"),
        P(("sec", "gx"), "gy"),
        P(None, ("sec", "gx", "gy")),
        P(("sec", "gx", "gy")),
        P(("sec", "gx", "gy")),
        P(("sec", "gx", "gy")),
        P(("sec", "gx", "gy")),
        P(),
    )
    return jax.shard_map(
        per_device,
        mesh=mesh,
        in_specs=placed,
        out_specs=(P(None, ("sec", "gx"), "gy"), P(None, ("sec", "gx", "gy"))),
        check_vma=False,
    )
```
